256 devices in a mesh: noise: 16 (over y_lo, z), tile: 16 (over y_hi, x, core).
Axes of the slice: x: 4, y: 4 (y_hi: 2, y_lo: 2; y = y_hi * 2 + y_lo), z: 8, core: 2. Of those that a mesh axis runs over, the one named last changes fastest.
Arguments:
- queue_state: float32 [64, 69, 16, 256], P('noise', None, 'tile'), may hold values from -6 to 6
- fresh_noise: float32 [2, 69, 16, 256], P(None, None, 'tile'), may hold values from -6 to 6
- plan: float32 [17], replicated, may hold values from 0.5 to 2
- levels: int32 [64], P('noise'), may hold values from 0 to 15
- neighbours: int32 [16, 4], replicated, may hold values from -1 to 15, as said below
- in_weight: bfloat16 [256, 69], replicated, may hold values from -0.75 to 0.75
- level_embed: float32 [256], replicated, may hold values from -3 to 3
- conv_weight: bfloat16 [9, 256, 256], replicated, may hold values from -0.125 to 0.125
- norm_gain: float32 [256], replicated, may hold values from 0.5 to 1.5
- query_weight: bfloat16 [256, 256], replicated, may hold values from -0.375 to 0.375
- memory_weight: bfloat16 [512, 256], replicated, may hold values from -0.375 to 0.375
- attend_out: bfloat16 [256, 256], replicated, may hold values from -0.375 to 0.375
- decode_weight: bfloat16 [69, 256], replicated, may hold values from -0.375 to 0.375
Outputs:
- queue_after: float32 [64, 69, 16, 256], P('noise', None, 'tile')
The draws below stay inside these ranges and needn't reach their ends.
Inputs may be any that keep to these rules, and one draw needn't show every extreme that they name: The tiles fill a grid of 2 rows and 8 columns, each tile once, in an arrangement drawn per run; west and east neighbours run along a row, which closes into a loop; -1 stands for the missing north neighbour of the first row and south neighbour of the last row.
All inputs are finite; a program needn't handle non-finite values.
Results may differ from the reference program's by a relative error of at most 0.012.
Values may be sent and summed in bfloat16 or wider, within the bound.
No kernel may reach another device: no remote copies, remote signals or barrier semaphores. Data moves between devices by JAX's collectives and lax.ppermute only.
A program may use at most 64 MiB of HBM per device.

```python
import math
import jax
import jax.numpy as jnp
from jax import lax

FIELDS = 69
WIDTH = 256
HEADS = 8
TILE = 16
FR_DEV = 4
LEVELS = 16
STEPS = 2
TILE_ROWS = 2
NTILES = 16
QUEUE = 64


def place_tile(placed, slot_index, tile_id):
    where_now = jnp.argmax((placed == tile_id).astype(jnp.int32)).astype(jnp.int32)
    held = placed[slot_index]
    placed = placed.at[where_now].set(held)
    return placed.at[slot_index].set(tile_id)


def draw_neighbours(key, part):
    column_count = NTILES // TILE_ROWS
    half_away = NTILES // 2
    order_key = jax.random.fold_in(key, 11)
    anchor_key = jax.random.fold_in(key, 12)
    column_key = jax.random.fold_in(key, 13)
    row_key = jax.random.fold_in(key, 14)
    placed = jax.random.permutation(order_key, NTILES).astype(jnp.int32)
    anchor = jax.random.randint(anchor_key, (), 0, NTILES).astype(jnp.int32)
    anchor_col = jax.random.randint(column_key, (), 0, column_count).astype(jnp.int32)
    anchor_row = jax.random.randint(row_key, (), 0, 2).astype(jnp.int32)
    other_row = (1 - anchor_row).astype(jnp.int32)
    first_slot = (anchor_row * column_count + anchor_col).astype(jnp.int32)
    east_slot = (anchor_row * column_count + (anchor_col + 1) % column_count).astype(jnp.int32)
    below_slot = (other_row * column_count + anchor_col).astype(jnp.int32)
    placed = place_tile(placed, first_slot, anchor)
    placed = place_tile(placed, east_slot, ((anchor + half_away) % NTILES).astype(jnp.int32))
    placed = place_tile(placed, below_slot, ((anchor + 1) % NTILES).astype(jnp.int32))
    where_is = jnp.argsort(placed, stable=True).astype(jnp.int32)
    row_of = where_is // column_count
    column_of = where_is % column_count
    west_tile = placed[row_of * column_count + (column_of + column_count - 1) % column_count]
    east_tile = placed[row_of * column_count + (column_of + 1) % column_count]
    north_tile = jnp.where(row_of > 0, placed[jnp.maximum(row_of - 1, 0) * column_count + column_of], -1)
    south_tile = jnp.where(row_of < TILE_ROWS - 1, placed[jnp.minimum(row_of + 1, TILE_ROWS - 1) * column_count + column_of], -1)
    return jnp.stack([west_tile, east_tile, north_tile, south_tile], axis=1).astype(jnp.int32)


def set_ends(entries, rng, smallest, high):
    longest = entries.shape.index(max(entries.shape))
    spots = []
    for shift in (0, 1):
        where = [jax.random.randint(jax.random.fold_in(rng, axis), (), 0, length) for axis, length in enumerate(entries.shape)]
        where[longest] = (where[longest] + shift) % entries.shape[longest]
        spots.append(tuple(where))
    return entries.at[spots[0]].set(smallest).at[spots[1]].set(high)


def block_scale(own_key, shape, cuts, smallest, top_value):
    loudness = 1.0
    for axis_at, shards_of in cuts:
        draws = jax.random.uniform(jax.random.fold_in(jax.random.fold_in(own_key, 6), axis_at), (shards_of,), jnp.float32, smallest / len(cuts), top_value / len(cuts))
        loudness = loudness * jnp.repeat(jnp.exp(draws), shape[axis_at] // shards_of).reshape((-1,) + (1,) * (len(shape) - 1 - axis_at))
    return loudness


def centred(stream_key, shape, deviation, most, pieces=(), kind=jnp.bfloat16):
    result = jax.random.normal(stream_key, shape, jnp.float32) * deviation
    if len(pieces) > 0:
        result = block_scale(stream_key, shape, pieces, -0.22, 0.18) * result
    return jnp.clip(result, min=-most, max=most).astype(kind)


def setup_inputs(seed: int = 0) -> dict:
    keys = jax.random.split(jax.random.key(seed), 14)
    queue_state = centred(keys[0], (QUEUE, FIELDS, NTILES, TILE * TILE), 1.0, 6.0, ((0, 16), (2, 16)), jnp.float32)
    fresh_noise = centred(keys[1], (STEPS, FIELDS, NTILES, TILE * TILE), 1.0, 6.0, ((2, 16),), jnp.float32)
    plan = jnp.clip(jnp.exp(jax.random.uniform(keys[2], (LEVELS + 1,), jnp.float32, math.log(0.5), math.log(2.0))), 0.5, 2.0)
    levels = set_ends(jax.random.randint(keys[3], (QUEUE,), 0, LEVELS), jax.random.fold_in(keys[3], 1), 0, LEVELS - 1).astype(jnp.int32)
    neighbours = draw_neighbours(jax.random.fold_in(keys[13], 71), 0)
    in_weight = centred(keys[5], (WIDTH, FIELDS), FIELDS ** -0.5, 0.75)
    level_embed = centred(keys[6], (WIDTH,), 0.5, 3.0, (), jnp.float32)
    conv_weight = centred(keys[7], (9, WIDTH, WIDTH), (9 * WIDTH) ** -0.5, 0.125)
    norm_gain = jnp.clip(1.0 + 0.1 * jax.random.normal(keys[8], (WIDTH,), jnp.float32), 0.5, 1.5)
    query_weight = centred(keys[9], (WIDTH, WIDTH), WIDTH ** -0.5, 0.375)
    memory_weight = centred(keys[10], (2 * WIDTH, WIDTH), WIDTH ** -0.5, 0.375)
    attend_out = centred(keys[11], (WIDTH, WIDTH), WIDTH ** -0.5, 0.375)
    decode_weight = centred(keys[12], (FIELDS, WIDTH), WIDTH ** -0.5, 0.375)
    return {"queue_state": queue_state, "fresh_noise": fresh_noise, "plan": plan, "levels": levels, "neighbours": neighbours, "in_weight": in_weight, "level_embed": level_embed, "conv_weight": conv_weight, "norm_gain": norm_gain, "query_weight": query_weight, "memory_weight": memory_weight, "attend_out": attend_out, "decode_weight": decode_weight}


def pick_tiles(source, tile_index):
    chosen = jnp.take(source, jnp.maximum(tile_index, 0), axis=1)
    return jnp.where((tile_index >= 0)[None, :, None], chosen, jnp.zeros_like(chosen))

def pad_tiles(frame_low, neighbours):
    west_col = pick_tiles(frame_low[:, :, :, TILE - 1], neighbours[:, 0])
    east_col = pick_tiles(frame_low[:, :, :, 0], neighbours[:, 1])
    middle = jnp.concatenate([west_col[..., None], frame_low, east_col[..., None]], axis=3)
    north_row = pick_tiles(middle[:, :, TILE - 1, :], neighbours[:, 2])
    south_row = pick_tiles(middle[:, :, 0, :], neighbours[:, 3])
    return jnp.concatenate([north_row[:, :, None, :], middle, south_row[:, :, None, :]], axis=2)

def frame_features(frame_state, sigma_one, in_weight, level_embed, conv_weight, norm_gain, neighbours):
    cell_count = NTILES * TILE * TILE
    in_scale = 1.0 / jnp.sqrt(sigma_one * sigma_one + 1.0)
    scaled = (in_scale * frame_state).reshape(FIELDS, cell_count).astype(jnp.bfloat16)
    lifted = jnp.dot(in_weight, scaled, preferred_element_type=jnp.float32) + jnp.log(sigma_one) * level_embed[:, None]
    lifted_low = lax.optimization_barrier(lifted.astype(jnp.bfloat16))
    padded = pad_tiles(lifted_low.reshape(WIDTH, NTILES, TILE, TILE), neighbours)
    convolved = jnp.zeros((WIDTH, cell_count), jnp.float32)
    for offset in range(9):
        down_by = offset // 3
        right_by = offset % 3
        window = padded[:, :, down_by:down_by + TILE, right_by:right_by + TILE].reshape(WIDTH, cell_count)
        convolved = convolved + jnp.dot(conv_weight[offset], window, preferred_element_type=jnp.float32)
    hidden = lax.optimization_barrier((lifted_low.astype(jnp.float32) + jax.nn.silu(convolved)).astype(jnp.bfloat16))
    widened = hidden.astype(jnp.float32)
    normed = (widened * lax.rsqrt(lax.optimization_barrier(jnp.mean(widened * widened, axis=0, keepdims=True)) + 1e-06) * norm_gain[:, None]).astype(jnp.bfloat16)
    return (hidden, normed)

def denoise(queue_now, sigmas, sigmas_next, neighbours, in_weight, level_embed, conv_weight, norm_gain, query_weight, memory_weight, attend_out, decode_weight):
    cell_count = NTILES * TILE * TILE
    head_size = WIDTH // HEADS

    def per_frame(frame_pair):
        frame_state, sigma_one = frame_pair
        hidden, normed = frame_features(frame_state, sigma_one, in_weight, level_embed, conv_weight, norm_gain, neighbours)
        queries = jnp.dot(query_weight, normed, preferred_element_type=jnp.float32).astype(jnp.bfloat16)
        memory = jnp.dot(memory_weight, normed, preferred_element_type=jnp.float32).astype(jnp.bfloat16)
        return (hidden, queries, memory)
    hidden_all, queries_all, memory_all = lax.map(per_frame, (queue_now, sigmas))
    memory_all = jnp.concatenate([memory_all, jnp.zeros((FR_DEV,) + memory_all.shape[1:], memory_all.dtype)], axis=0)

    def per_block(block_id):
        begin_at = (block_id * FR_DEV).astype(jnp.int32)
        block_query = lax.dynamic_slice_in_dim(queries_all, begin_at, FR_DEV, 0).astype(jnp.float32)
        block_query = block_query.reshape(FR_DEV, HEADS, head_size, cell_count)
        block_memory = lax.dynamic_slice_in_dim(memory_all, begin_at, 2 * FR_DEV, 0).astype(jnp.float32)
        key_heads = block_memory[:, :WIDTH].reshape(2 * FR_DEV, HEADS, head_size, cell_count)
        value_heads = block_memory[:, WIDTH:].reshape(2 * FR_DEV, HEADS, head_size, cell_count)
        scores = jnp.einsum('ihdm,jhdm->ijhm', block_query, key_heads, precision=lax.Precision.HIGHEST) * head_size ** (-0.5)
        usable = begin_at + jnp.arange(2 * FR_DEV, dtype=jnp.int32) < QUEUE
        scores = jnp.where(usable[None, :, None, None], scores, -jnp.inf)
        weights = lax.optimization_barrier(jax.nn.softmax(scores, axis=1).astype(jnp.bfloat16)).astype(jnp.float32)
        context = jnp.einsum('ijhm,jhdm->ihdm', weights, value_heads, precision=lax.Precision.HIGHEST)
        context = lax.optimization_barrier(context.astype(jnp.bfloat16)).astype(jnp.float32).reshape(FR_DEV, WIDTH, cell_count)
        attended = jnp.einsum('oc,icm->iom', attend_out.astype(jnp.float32), context, precision=lax.Precision.HIGHEST)
        block_hidden = lax.dynamic_slice_in_dim(hidden_all, begin_at, FR_DEV, 0).astype(jnp.float32)
        refined = lax.optimization_barrier((block_hidden + attended).astype(jnp.bfloat16)).astype(jnp.float32)
        projected = jnp.einsum('fc,icm->ifm', decode_weight.astype(jnp.float32), refined, precision=lax.Precision.HIGHEST)
        block_state = lax.dynamic_slice_in_dim(queue_now, begin_at, FR_DEV, 0).reshape(FR_DEV, FIELDS, cell_count)
        block_sigma = lax.dynamic_slice_in_dim(sigmas, begin_at, FR_DEV, 0)
        block_next = lax.dynamic_slice_in_dim(sigmas_next, begin_at, FR_DEV, 0)
        spread = block_sigma * block_sigma + 1.0
        denoised = (1.0 / spread)[:, None, None] * block_state + (block_sigma / jnp.sqrt(spread))[:, None, None] * projected
        return block_state + ((block_next - block_sigma) / block_sigma)[:, None, None] * (block_state - denoised)
    blocks = lax.map(per_block, jnp.arange(QUEUE // FR_DEV, dtype=jnp.int32))
    return blocks.reshape(queue_now.shape)

def reference(queue_state, fresh_noise, plan, levels, neighbours, in_weight, level_embed, conv_weight, norm_gain, query_weight, memory_weight, attend_out, decode_weight):
    sigmas = plan[levels]
    sigmas_next = plan[levels + 1]
    queue_now = queue_state
    for step_index in range(STEPS):
        entering = sigmas[QUEUE - 1] * fresh_noise[step_index]
        queue_now = jnp.concatenate([queue_now[1:], entering[None]], axis=0)
        queue_now = denoise(queue_now, sigmas, sigmas_next, neighbours, in_weight, level_embed, conv_weight, norm_gain, query_weight, memory_weight, attend_out, decode_weight)
    return queue_now
```

```python
import jax
import jax.numpy as jnp
from jax import lax
from jax.experimental import pallas as pl
from jax.experimental.pallas import tpu as pltpu
from jax.sharding import Mesh
from jax.sharding import PartitionSpec as P

FIELDS = 69
ROWS = 72
WIDTH = 256
HEADS = 8
HEAD = WIDTH // HEADS
TILE = 16
CELLS = TILE * TILE
TAPS = 9
FR_DEV = 4
STEPS = 2
NTILES = 16
TILE_AXES = ("tile_0", "tile_1", "tile_2")
BF = jnp.bfloat16
F32 = jnp.float32

VMEM = pl.BlockSpec(memory_space=pltpu.VMEM)
SMEM = pl.BlockSpec(memory_space=pltpu.SMEM)


def iota(shape, dim):
    return lax.broadcasted_iota(jnp.int32, shape, dim)


def mm(a, b):
    return jnp.dot(a, b, preferred_element_type=F32)


def mm_nt(a, b):
    return lax.dot_general(a, b, (((1,), (1,)), ((), ())), preferred_element_type=F32)


def split_hi_lo(v):
    hi = v.astype(BF).astype(F32)
    return hi, v - hi


def weights_kernel(
    in_ref, embed_ref, conv_ref, gain_ref, query_ref, memory_ref, out_ref, decode_ref,
    taps_out, lift_out, qkv_out, attend_out, decode_out, folded,
):
    rows = iota((ROWS, WIDTH), 0)
    weight = in_ref[...].astype(F32)
    unit = (iota((ROWS, FIELDS), 0) == iota((ROWS, FIELDS), 1)).astype(BF)
    lift_t = mm_nt(unit, weight.astype(BF))
    embed = jnp.broadcast_to(embed_ref[...], (ROWS, WIDTH))
    embed_hi, embed_lo = split_hi_lo(embed)
    stacked = jnp.where(
        rows == FIELDS, embed_hi, jnp.where(rows == FIELDS + 1, embed_lo, lift_t)
    ).astype(BF)
    lift_rows = jnp.where(
        rows >= FIELDS, jnp.where(rows == FIELDS + 2, embed_lo, embed_hi), lift_t
    )
    lift_out[...] = jnp.transpose(lift_rows).astype(BF)
    for tap in range(TAPS):
        both = mm_nt(stacked, conv_ref[tap])
        whole = jnp.broadcast_to(
            both[FIELDS : FIELDS + 1] + both[FIELDS + 1 : FIELDS + 2], (ROWS, WIDTH)
        )
        hi, lo = split_hi_lo(whole)
        folded[pl.ds(tap * ROWS, ROWS), :] = jnp.where(
            rows >= FIELDS, jnp.where(rows == FIELDS + 2, lo, hi), both
        )
    taps_out[...] = jnp.transpose(folded[...]).astype(BF)
    place = iota((WIDTH, WIDTH), 0)
    order = ((place % HEADS) * HEAD + place // HEADS == iota((WIDTH, WIDTH), 1)).astype(BF)
    gain = gain_ref[...]
    qkv_out[0:WIDTH, :] = (mm(order, query_ref[...]) * gain).astype(BF)
    for part in range(2):
        qkv_out[pl.ds((part + 1) * WIDTH, WIDTH), :] = (
            mm(order, memory_ref[pl.ds(part * WIDTH, WIDTH), :]) * gain
        ).astype(BF)
    attend_out[...] = mm_nt(out_ref[...], order).astype(BF)
    unit = (iota((ROWS, FIELDS), 0) == iota((ROWS, FIELDS), 1)).astype(BF)
    decode_out[...] = mm(unit, decode_ref[...]).astype(BF)


def prepare_weights(in_weight, embed, conv, gain, query, memory, attend, decode):
    return pl.pallas_call(
        weights_kernel,
        out_shape=(
            jax.ShapeDtypeStruct((WIDTH, TAPS * ROWS), BF),
            jax.ShapeDtypeStruct((WIDTH, ROWS), BF),
            jax.ShapeDtypeStruct((3 * WIDTH, WIDTH), BF),
            jax.ShapeDtypeStruct((WIDTH, WIDTH), BF),
            jax.ShapeDtypeStruct((ROWS, WIDTH), BF),
        ),
        in_specs=[VMEM] * 8,
        out_specs=(VMEM,) * 5,
        scratch_shapes=[pltpu.VMEM((TAPS * ROWS, WIDTH), F32)],
        name="weights",
    )(in_weight, embed.reshape(1, WIDTH), conv, gain.reshape(1, WIDTH), query, memory, attend, decode)


def border_kernel(place_ref, near_ref, queue_ref, fresh_ref, frames_out, slots_out, full, lines):
    me = place_ref[0]
    full[...] = jnp.zeros_like(full)
    for f in range(FR_DEV):
        full[pl.ds(f * ROWS, FIELDS), :] = queue_ref[f]
    full[pl.ds(FR_DEV * ROWS, FIELDS), :] = fresh_ref[0]
    frames = full[...].astype(BF)
    for f in range(FR_DEV):
        frames_out[f] = full[pl.ds(f * ROWS, ROWS), :].astype(BF)
    cell = iota((CELLS, 128), 0)
    want = iota((CELLS, 128), 1)
    line = want // TILE
    along = want % TILE
    source = jnp.where(
        line == 0,
        along * TILE + TILE - 1,
        jnp.where(
            line == 1,
            along * TILE,
            jnp.where(line == 2, (TILE - 1) * TILE + along, along),
        ),
    )
    pick = jnp.logical_and(cell == source, line < 4).astype(BF)
    found = mm(frames, pick)
    lane_block = iota((ROWS, 128), 1) // TILE
    for r in range(4):
        packed = jnp.zeros((ROWS, 128), F32)
        for f in range(FR_DEV + 1):
            one = found[f * ROWS : (f + 1) * ROWS]
            turn = (TILE * (f - r)) % 128
            if turn:
                one = pltpu.roll(one, turn, 1)
            packed = jnp.where(lane_block == f, one, packed)
        lines[r] = packed.astype(BF)
    for j in range(NTILES):
        north = near_ref[j, 2]
        beside = jnp.maximum(north, near_ref[j, 3])
        from_west = jnp.logical_or(near_ref[j, 0] == me, near_ref[beside, 0] == me)
        from_east = jnp.logical_or(near_ref[j, 1] == me, near_ref[beside, 1] == me)
        vertical = jnp.where(north >= 0, 2, 3)
        code = jnp.where(from_west, 0, jnp.where(from_east, 1, vertical))
        slots_out[j] = lines[code]


def border_lines(place, near, queue, fresh):
    return pl.pallas_call(
        border_kernel,
        out_shape=(
            jax.ShapeDtypeStruct((FR_DEV, ROWS, CELLS), BF),
            jax.ShapeDtypeStruct((NTILES, ROWS, 128), BF),
        ),
        in_specs=[SMEM, SMEM, VMEM, VMEM],
        out_specs=(VMEM, VMEM),
        scratch_shapes=[
            pltpu.VMEM(((FR_DEV + 1) * ROWS, CELLS), F32),
            pltpu.VMEM((4, ROWS, 128), BF),
        ],
        name="border",
    )(place, near, queue, fresh)


def ring_kernel(place_ref, near_ref, slots_ref, frames_ref, ring_out, near_out, far_out):
    me = place_ref[0]
    north = near_ref[me, 2]
    beside = jnp.maximum(north, near_ref[me, 3])
    west = slots_ref[near_ref[me, 0]].astype(F32)
    east = slots_ref[near_ref[me, 1]].astype(F32)
    line = slots_ref[beside].astype(F32)
    corner_west = slots_ref[near_ref[beside, 0]].astype(F32)
    corner_east = slots_ref[near_ref[beside, 1]].astype(F32)
    lane = iota((ROWS, 128), 1)
    below = north >= 0
    west_end = jnp.where(below, pltpu.roll(corner_west, 128 - (TILE - 1), 1), corner_west)
    east_end = jnp.where(below, pltpu.roll(corner_east, 128 - (TILE - 1), 1), corner_east)
    ends = jnp.where(lane % TILE == 0, west_end, pltpu.roll(east_end, 1, 1))
    sides = (west, east, line, ends)
    rings = []
    for f in range(FR_DEV + 1):
        ring = jnp.zeros((ROWS, 128), F32)
        for r in range(4):
            turn = (TILE * (r - f)) % 128
            one = pltpu.roll(sides[r], turn, 1) if turn else sides[r]
            keep = lane // TILE == r if r < 3 else jnp.logical_and(lane >= 48, lane < 50)
            ring = jnp.where(keep, one, ring)
        rings.append(ring)
        ring_out[f] = ring.astype(BF)
    for pair in range(2):
        near_out[pair] = jnp.where(
            lane < 64, rings[2 * pair], pltpu.roll(rings[2 * pair + 1], 64, 1)
        ).astype(BF)
    far_out[:, 0:CELLS] = frames_ref[0]
    far_out[:, CELLS : CELLS + 128] = rings[0].astype(BF)


def ring_cells(place, near, slots, frames):
    return pl.pallas_call(
        ring_kernel,
        out_shape=(
            jax.ShapeDtypeStruct((FR_DEV + 1, ROWS, 128), BF),
            jax.ShapeDtypeStruct((2, ROWS, 128), BF),
            jax.ShapeDtypeStruct((ROWS, CELLS + 128), BF),
        ),
        in_specs=[SMEM, SMEM, VMEM, VMEM],
        out_specs=(VMEM,) * 3,
        name="ring",
    )(place, near, slots, frames)


def with_log_rows(scaled, log_hi, log_lo, lanes):
    rows = iota((ROWS, lanes), 0)
    return jnp.where(
        rows >= FIELDS, jnp.where(rows == FIELDS + 1, log_lo, log_hi), scaled
    )


def step_kernel(
    place_ref, near_ref, plan_ref, level_ref, next_level_ref,
    queue_ref, fresh_ref, ring_ref, next_frames_ref, next_ring_ref, far_ref,
    taps_ref, lift_ref, qkv_ref, attend_ref, decode_ref,
    out_ref, states, rings, spread_ref, hidden_all, qkv_all, context_all,
):
    me = place_ref[0]
    group = place_ref[1]
    is_last = group == place_ref[2] - 1
    is_second_last = group == place_ref[2] - 2
    north_here = (near_ref[me, 2] >= 0).astype(F32)
    south_here = (near_ref[me, 3] >= 0).astype(F32)

    def sigma_at(p, lanes=128):
        level = jnp.where(p < FR_DEV, level_ref[p % FR_DEV], next_level_ref[p % FR_DEV])
        return jnp.full((1, lanes), plan_ref[level], F32)

    for p in range(FR_DEV - 1):
        states[p, 64:ROWS, :] = jnp.zeros((ROWS - 64, CELLS), F32)
        states[p, 0:FIELDS, :] = queue_ref[p + 1]
        rings[p] = ring_ref[p + 1].astype(F32)
    lane = iota((ROWS, 128), 1)
    for f in range(FR_DEV):
        states[FR_DEV - 1 + f] = next_frames_ref[f].astype(F32)
        pair = next_ring_ref[f // 2].astype(F32)
        rings[FR_DEV - 1 + f] = pair if f % 2 == 0 else pltpu.roll(pair, 64, 1)
    states[2 * FR_DEV - 1] = far_ref[:, 0:CELLS].astype(F32)
    rings[2 * FR_DEV - 1] = far_ref[:, CELLS : CELLS + 128].astype(F32)

    def enter(p):
        amount = sigma_at(p)
        states[p, 64:ROWS, :] = jnp.zeros((ROWS - 64, CELLS), F32)
        states[p, 0:FIELDS, :] = fresh_ref[0] * sigma_at(p, CELLS)
        rings[p] = ring_ref[FR_DEV].astype(F32) * amount

    @pl.when(is_last)
    def _():
        enter(FR_DEV - 1)

    @pl.when(is_second_last)
    def _():
        enter(2 * FR_DEV - 1)

    across = iota((ROWS, CELLS), 1) % TILE
    down = iota((ROWS, CELLS), 1) // TILE
    ring_row = iota((128, 4 * CELLS), 0)
    column = iota((128, 4 * CELLS), 1)
    shift = column // CELLS - 2
    cell_x = column % TILE
    cell_y = (column % CELLS) // TILE
    line_x = cell_x + shift
    from_line = jnp.where(
        line_x < 0, 3 * TILE, jnp.where(line_x >= TILE, 3 * TILE + 1, 2 * TILE + line_x)
    )
    from_side = jnp.where(cell_x == 0, cell_y, TILE + cell_y)
    spread_ref[...] = (ring_row == jnp.where(column < CELLS, from_side, from_line)).astype(BF)

    def features(p):
        sigma = sigma_at(p)
        scale = 1.0 / jnp.sqrt(sigma * sigma + 1.0)
        log_hi, log_lo = split_hi_lo(jnp.log(sigma))
        scale2 = jnp.concatenate([scale, scale], axis=1)
        log_hi2 = jnp.concatenate([log_hi, log_hi], axis=1)
        log_lo2 = jnp.concatenate([log_lo, log_lo], axis=1)
        inner = with_log_rows(states[p] * scale2, log_hi2, log_lo2, CELLS)
        ring = with_log_rows(rings[p] * scale, log_hi, log_lo, 128)
        inner_low = inner.astype(BF)
        inner = inner_low.astype(F32)
        image = mm(ring.astype(BF), spread_ref[...])
        sides = image[:, 0:CELLS]
        shifted = (
            jnp.where(across == 0, sides, pltpu.roll(inner, 1, 1)),
            inner,
            jnp.where(across == TILE - 1, sides, pltpu.roll(inner, CELLS - 1, 1)),
        )
        up = []
        low = []
        for b in range(3):
            line = image[:, (b + 1) * CELLS : (b + 2) * CELLS]
            up.append(jnp.where(down == 0, line * north_here, pltpu.roll(shifted[b], TILE, 1)))
            low.append(
                jnp.where(
                    down == TILE - 1, line * south_here, pltpu.roll(shifted[b], CELLS - TILE, 1)
                )
            )
        windows = jnp.concatenate([*up, *shifted, *low], axis=0).astype(BF)
        convolved = mm(taps_ref[...], windows)
        lifted = mm(lift_ref[...], inner_low)
        hidden = lifted + convolved / (1.0 + jnp.exp(-convolved))
        power = jnp.mean(hidden * hidden, axis=0, keepdims=True)
        return hidden, (hidden * lax.rsqrt(power + 1e-06)).astype(BF)

    def own(p, carry):
        hidden, normed = features(p)
        hidden_all[p] = hidden
        qkv_all[p] = mm(qkv_ref[...], normed).reshape(3 * HEAD, HEADS, CELLS)
        return carry

    def following(p, carry):
        _, normed = features(p)
        qkv_all[p, HEAD : 3 * HEAD] = mm(qkv_ref[WIDTH : 3 * WIDTH, :], normed).reshape(
            2 * HEAD, HEADS, CELLS
        )
        return carry

    lax.fori_loop(0, FR_DEV, own, 0)
    lax.fori_loop(FR_DEV, 2 * FR_DEV, following, 0)

    hide = jnp.where(is_last, -jnp.inf, 0.0)
    for half in range(2):
        lanes = slice(half * 128, half * 128 + 128)

        def score(d, sums):
            keys = qkv_all[:, HEAD + d, :, lanes]
            return tuple(
                sums[i] + qkv_all[i, d, :, lanes][None] * keys for i in range(FR_DEV)
            )

        zero = jnp.zeros((2 * FR_DEV, HEADS, 128), F32)
        sums = lax.fori_loop(0, HEAD, score, (zero,) * FR_DEV, unroll=4)
        later = iota((2 * FR_DEV, HEADS, 128), 0) >= FR_DEV
        weights = []
        for i in range(FR_DEV):
            scores = sums[i] * HEAD ** (-0.5) + jnp.where(later, hide, 0.0)
            top = jnp.max(scores, axis=0, keepdims=True)
            raised = jnp.exp(scores - top)
            weights.append(raised / jnp.sum(raised, axis=0, keepdims=True))

        def combine(d, carry):
            values = qkv_all[:, 2 * HEAD + d, :, lanes]
            for i in range(FR_DEV):
                context_all[i, d, :, lanes] = jnp.sum(weights[i] * values, axis=0)
            return carry

        lax.fori_loop(0, HEAD, combine, 0, unroll=4)

    def finish(p, carry):
        context = context_all[p].reshape(WIDTH, CELLS).astype(BF)
        refined = (hidden_all[p] + mm(attend_ref[...], context)).astype(BF)
        projected = mm(decode_ref[...], refined)
        sigma = sigma_at(p, CELLS)
        sigma_next = jnp.full((1, CELLS), plan_ref[level_ref[p] + 1], F32)
        spread = sigma * sigma + 1.0
        slope = (sigma_next - sigma) / sigma
        state = states[p]
        denoised = state / spread + sigma / jnp.sqrt(spread) * projected
        out_ref[p] = (state + slope * (state - denoised))[0:FIELDS]
        return carry

    lax.fori_loop(0, FR_DEV, finish, 0)


def rolling_step(place, near, plan, levels, next_levels, queue, fresh, weights):
    groups = lax.axis_size("noise")
    from_next = [(i + 1, i) for i in range(groups - 1)]
    from_second = [(i + 2, i) for i in range(groups - 2)]
    frames, slots = border_lines(place, near, queue, fresh)
    next_frames = lax.ppermute(frames, "noise", from_next)
    slots = lax.all_to_all(slots, TILE_AXES, split_axis=0, concat_axis=0, tiled=True)
    rings, pair_rings, far = ring_cells(place, near, slots, frames)
    next_rings = lax.ppermute(pair_rings, "noise", from_next)
    far = lax.ppermute(far, "noise", from_second)
    return pl.pallas_call(
        step_kernel,
        out_shape=jax.ShapeDtypeStruct((FR_DEV, FIELDS, CELLS), F32),
        in_specs=[SMEM] * 5 + [VMEM] * 11,
        out_specs=VMEM,
        scratch_shapes=[
            pltpu.VMEM((2 * FR_DEV, ROWS, CELLS), F32),
            pltpu.VMEM((2 * FR_DEV, ROWS, 128), F32),
            pltpu.VMEM((128, 4 * CELLS), BF),
            pltpu.VMEM((FR_DEV, WIDTH, CELLS), F32),
            pltpu.VMEM((2 * FR_DEV, 3 * HEAD, HEADS, CELLS), F32),
            pltpu.VMEM((FR_DEV, HEAD, HEADS, CELLS), F32),
        ],
        name="step",
    )(
        place, near, plan, levels, next_levels,
        queue, fresh, rings, next_frames, next_rings, far, *weights,
    )


def shards(
    queue_state, fresh_noise, plan, levels, neighbours, in_weight, level_embed, conv_weight,
    norm_gain, query_weight, memory_weight, attend_out, decode_weight,
):
    groups = lax.axis_size("noise")
    place = jnp.stack(
        [lax.axis_index(TILE_AXES), lax.axis_index("noise"), jnp.int32(groups)]
    ).astype(jnp.int32)
    next_levels = lax.ppermute(levels, "noise", [(i + 1, i) for i in range(groups - 1)])
    weights = prepare_weights(
        in_weight, level_embed, conv_weight, norm_gain, query_weight, memory_weight,
        attend_out, decode_weight,
    )
    queue = queue_state.reshape(FR_DEV, FIELDS, CELLS)
    noise = fresh_noise.reshape(STEPS, FIELDS, CELLS)
    for step in range(STEPS):
        queue = rolling_step(
            place, neighbours, plan, levels, next_levels, queue, noise[step : step + 1], weights
        )
    return queue.reshape(queue_state.shape)


def solution(mesh):
    split = Mesh(
        mesh.devices.reshape(mesh.shape["noise"], 2, 4, 2), ("noise", "tile_0", "tile_1", "tile_2")
    )
    placed = (
        P("noise", None, TILE_AXES, None),
        P(None, None, TILE_AXES, None),
        P(),
        P("noise"),
        P(),
        P(),
        P(),
        P(),
        P(),
        P(),
        P(),
        P(),
        P(),
    )
    return jax.shard_map(
        shards,
        mesh=split,
        in_specs=placed,
        out_specs=P("noise", None, TILE_AXES, None),
        check_vma=False,
    )
```

```python
import functools

import jax
import jax.numpy as jnp
from jax import lax
from jax.experimental import pallas as pl
from jax.experimental.pallas import tpu as pltpu
from jax.sharding import Mesh
from jax.sharding import PartitionSpec as P

FIELDS = 69
ROWS = 72
WIDTH = 256
HEADS = 8
HEAD = WIDTH // HEADS
TILE = 16
CELLS = TILE * TILE
TAPS = 9
UNROLL = 4
FR_DEV = 4
STEPS = 2
NTILES = 16
TILE_AXES = ("tile_0", "tile_1", "tile_2")
BF = jnp.bfloat16
F32 = jnp.float32

VMEM = pl.BlockSpec(memory_space=pltpu.VMEM)
SMEM = pl.BlockSpec(memory_space=pltpu.SMEM)


def iota(shape, dim):
    return lax.broadcasted_iota(jnp.int32, shape, dim)


def mm(a, b):
    return jnp.dot(a, b, preferred_element_type=F32)


def mm_nt(a, b):
    return lax.dot_general(a, b, (((1,), (1,)), ((), ())), preferred_element_type=F32)


def split_hi_lo(v):
    hi = v.astype(BF).astype(F32)
    return hi, v - hi


def weights_kernel(
    in_ref, embed_ref, conv_ref, gain_ref, query_ref, memory_ref, out_ref, decode_ref, after_ref,
    taps_out, lift_out, qkv_out, attend_out, decode_out, folded,
):
    rows = iota((ROWS, WIDTH), 0)
    unit = (iota((ROWS, FIELDS), 0) == iota((ROWS, FIELDS), 1)).astype(BF)
    lift_t = mm(unit, in_ref[...])
    embed = jnp.broadcast_to(embed_ref[...], (ROWS, WIDTH))
    embed_hi, embed_lo = split_hi_lo(embed)
    stacked = jnp.where(
        rows == FIELDS, embed_hi, jnp.where(rows == FIELDS + 1, embed_lo, lift_t)
    ).astype(BF)
    lift_rows = jnp.where(
        rows >= FIELDS, jnp.where(rows == FIELDS + 2, embed_lo, embed_hi), lift_t
    )
    lift_out[...] = jnp.transpose(lift_rows).astype(BF)
    for tap in range(TAPS):
        both = mm_nt(stacked, conv_ref[tap])
        whole = jnp.broadcast_to(
            both[FIELDS : FIELDS + 1] + both[FIELDS + 1 : FIELDS + 2], (ROWS, WIDTH)
        )
        hi, lo = split_hi_lo(whole)
        folded[pl.ds(tap * ROWS, ROWS), :] = jnp.where(
            rows >= FIELDS, jnp.where(rows == FIELDS + 2, lo, hi), both
        )
    taps_out[...] = jnp.transpose(folded[...]).astype(BF)
    place = iota((WIDTH, WIDTH), 0)
    order = ((place % HEADS) * HEAD + place // HEADS == iota((WIDTH, WIDTH), 1)).astype(BF)
    gain = gain_ref[...]
    qkv_out[0:WIDTH, :] = (mm(order, query_ref[...]) * gain).astype(BF)
    for part in range(2):
        qkv_out[pl.ds((part + 1) * WIDTH, WIDTH), :] = (
            mm(order, memory_ref[pl.ds(part * WIDTH, WIDTH), :]) * gain
        ).astype(BF)
    attend_out[...] = mm_nt(out_ref[...], order).astype(BF)
    decode_out[...] = mm(unit, decode_ref[...]).astype(BF)


def prepare_weights(in_weight, embed, conv, gain, query, memory, attend, decode, after):
    return pl.pallas_call(
        weights_kernel,
        out_shape=(
            jax.ShapeDtypeStruct((WIDTH, TAPS * ROWS), BF),
            jax.ShapeDtypeStruct((WIDTH, ROWS), BF),
            jax.ShapeDtypeStruct((3 * WIDTH, WIDTH), BF),
            jax.ShapeDtypeStruct((WIDTH, WIDTH), BF),
            jax.ShapeDtypeStruct((ROWS, WIDTH), BF),
        ),
        in_specs=[VMEM] * 8 + [SMEM],
        out_specs=(VMEM,) * 5,
        scratch_shapes=[pltpu.VMEM((TAPS * ROWS, WIDTH), F32)],
        name="weights",
    )(
        in_weight.T, embed.reshape(1, WIDTH), conv, gain.reshape(1, WIDTH), query, memory, attend,
        decode, after,
    )


def frame_rows(queue_ref, frame):
    halves = [
        queue_ref[pl.ds(frame * 2 * FIELDS + half, FIELDS, stride=2), :] for half in range(2)
    ]
    return jnp.concatenate(halves, axis=1)


def border_kernel(
    step, near_ref, plan_ref, level_ref, queue_ref, fresh_ref,
    frames_out, slots_out, after_out, full, lines,
):
    me = lax.axis_index(TILE_AXES)
    after_out[0] = 0
    low_row = iota((8, CELLS), 0)
    for f in range(FR_DEV):
        sigma = jnp.full((8, CELLS), plan_ref[level_ref[f]], F32)
        first, rest = split_hi_lo(sigma)
        second, third = split_hi_lo(rest)
        full[pl.ds(f * ROWS + 64, 8), :] = jnp.where(
            low_row == 5, first, jnp.where(low_row == 6, second, third)
        )
        full[pl.ds(f * ROWS, FIELDS), :] = frame_rows(queue_ref, f)
    full[pl.ds(FR_DEV * ROWS + 64, 8), :] = jnp.zeros((8, CELLS), F32)
    full[pl.ds(FR_DEV * ROWS, FIELDS), :] = fresh_ref[step, :, 0, :]
    frames = full[...].astype(BF)
    for f in range(FR_DEV):
        frames_out[f] = full[pl.ds(f * ROWS, ROWS), :].astype(BF)
    cell = iota((CELLS, 128), 0)
    want = iota((CELLS, 128), 1)
    line = want // TILE
    along = want % TILE
    source = jnp.where(
        line == 0,
        along * TILE + TILE - 1,
        jnp.where(
            line == 1,
            along * TILE,
            jnp.where(line == 2, (TILE - 1) * TILE + along, along),
        ),
    )
    pick = jnp.logical_and(cell == source, line < 4).astype(BF)
    found = mm(frames, pick)
    lane_block = iota((ROWS, 128), 1) // TILE
    for r in range(4):
        packed = jnp.zeros((ROWS, 128), F32)
        for f in range(FR_DEV + 1):
            one = found[f * ROWS : (f + 1) * ROWS]
            turn = (TILE * (f - r)) % 128
            if turn:
                one = pltpu.roll(one, turn, 1)
            packed = jnp.where(lane_block == f, one, packed)
        lines[r] = packed.astype(BF)
    for j in range(NTILES):
        north = near_ref[2, j]
        beside = jnp.maximum(north, near_ref[3, j])
        from_west = jnp.logical_or(near_ref[0, j] == me, near_ref[0, beside] == me)
        from_east = jnp.logical_or(near_ref[1, j] == me, near_ref[1, beside] == me)
        vertical = jnp.where(north >= 0, 2, 3)
        code = jnp.where(from_west, 0, jnp.where(from_east, 1, vertical))
        slots_out[j] = lines[code]


def border_lines(step, near, plan, levels, queue, fresh):
    return pl.pallas_call(
        functools.partial(border_kernel, step),
        out_shape=(
            jax.ShapeDtypeStruct((FR_DEV, ROWS, CELLS), BF),
            jax.ShapeDtypeStruct((NTILES, ROWS, 128), BF),
            jax.ShapeDtypeStruct((1,), jnp.int32),
        ),
        in_specs=[SMEM, SMEM, SMEM, VMEM, VMEM],
        out_specs=(VMEM, VMEM, SMEM),
        scratch_shapes=[
            pltpu.VMEM(((FR_DEV + 1) * ROWS, CELLS), F32),
            pltpu.VMEM((4, ROWS, 128), BF),
        ],
        name="border",
    )(near, plan, levels, queue, fresh)


def ring_kernel(near_ref, slots_ref, frames_ref, wait_ref, ring_out, near_out, far_out):
    me = lax.axis_index(TILE_AXES)
    north = near_ref[2, me]
    beside = jnp.maximum(north, near_ref[3, me])
    west = slots_ref[near_ref[0, me]].astype(F32)
    east = slots_ref[near_ref[1, me]].astype(F32)
    line = slots_ref[beside].astype(F32)
    corner_west = slots_ref[near_ref[0, beside]].astype(F32)
    corner_east = slots_ref[near_ref[1, beside]].astype(F32)
    lane = iota((ROWS, 128), 1)
    below = north >= 0
    west_end = jnp.where(below, pltpu.roll(corner_west, 128 - (TILE - 1), 1), corner_west)
    east_end = jnp.where(below, pltpu.roll(corner_east, 128 - (TILE - 1), 1), corner_east)
    ends = jnp.where(lane % TILE == 0, west_end, pltpu.roll(east_end, 1, 1))
    sides = (west, east, line, ends)
    rings = []
    for f in range(FR_DEV + 1):
        ring = jnp.zeros((ROWS, 128), F32)
        for r in range(4):
            turn = (TILE * (r - f)) % 128
            one = pltpu.roll(sides[r], turn, 1) if turn else sides[r]
            keep = lane // TILE == r if r < 3 else jnp.logical_and(lane >= 48, lane < 50)
            ring = jnp.where(keep, one, ring)
        rings.append(ring)
        ring_out[f] = ring.astype(BF)
    for pair in range(2):
        near_out[pair] = jnp.where(
            lane < 64, rings[2 * pair], pltpu.roll(rings[2 * pair + 1], 64, 1)
        ).astype(BF)
    far_out[:, 0:CELLS] = frames_ref[0]
    far_out[:, CELLS : CELLS + 128] = rings[0].astype(BF)


def ring_cells(near, slots, frames, wait):
    return pl.pallas_call(
        ring_kernel,
        out_shape=(
            jax.ShapeDtypeStruct((FR_DEV + 1, ROWS, 128), BF),
            jax.ShapeDtypeStruct((2, ROWS, 128), BF),
            jax.ShapeDtypeStruct((ROWS, CELLS + 128), BF),
        ),
        in_specs=[SMEM, VMEM, VMEM, pl.BlockSpec(memory_space=pl.ANY)],
        out_specs=(VMEM,) * 3,
        name="ring",
    )(near, slots, frames, wait)


def with_log_rows(scaled, log_hi, log_lo, lanes):
    rows = iota((ROWS, lanes), 0)
    return jnp.where(
        rows >= FIELDS, jnp.where(rows == FIELDS + 1, log_lo, log_hi), scaled
    )


def step_kernel(
    step, near_ref, plan_ref, level_ref,
    queue_ref, fresh_ref, ring_ref, next_frames_ref, next_ring_ref, far_ref,
    taps_ref, lift_ref, qkv_ref, attend_ref, decode_ref,
    out_ref, states, rings, sigmas, images, hidden_all, qkv_all, context_all,
):
    me = lax.axis_index(TILE_AXES)
    group = lax.axis_index("noise")
    groups = lax.axis_size("noise")
    is_last = group == groups - 1
    is_second_last = group == groups - 2
    north_here = (near_ref[2, me] >= 0).astype(F32)
    south_here = (near_ref[3, me] >= 0).astype(F32)

    for p in range(FR_DEV - 1):
        states[p, 64:ROWS, :] = jnp.zeros((ROWS - 64, CELLS), F32)
        states[p, 0:FIELDS, :] = frame_rows(queue_ref, p + 1)
        rings[p] = ring_ref[p + 1].astype(F32)
    for f in range(FR_DEV):
        came = next_frames_ref[f].astype(F32)
        states[FR_DEV - 1 + f] = came
        parts = came[FIELDS : FIELDS + 1] + came[FIELDS + 1 : FIELDS + 2]
        parts = parts + came[FIELDS + 2 : FIELDS + 3]
        sigmas[FR_DEV + f] = jnp.where(is_last, 1.0, parts)
        sigmas[f] = jnp.full((1, CELLS), plan_ref[level_ref[f]], F32)
        pair = next_ring_ref[f // 2].astype(F32)
        rings[FR_DEV - 1 + f] = pair if f % 2 == 0 else pltpu.roll(pair, 64, 1)
    states[2 * FR_DEV - 1] = far_ref[:, 0:CELLS].astype(F32)
    rings[2 * FR_DEV - 1] = far_ref[:, CELLS : CELLS + 128].astype(F32)

    def enter(p):
        states[p, 64:ROWS, :] = jnp.zeros((ROWS - 64, CELLS), F32)
        states[p, 0:FIELDS, :] = fresh_ref[step, :, 0, :] * sigmas[p]
        rings[p] = ring_ref[FR_DEV].astype(F32) * sigmas[p][:, 0:128]

    @pl.when(is_last)
    def _():
        enter(FR_DEV - 1)

    @pl.when(is_second_last)
    def _():
        enter(2 * FR_DEV - 1)

    def scales(p, lanes):
        sigma = sigmas[p][:, 0:lanes]
        log_hi, log_lo = split_hi_lo(jnp.log(sigma))
        return 1.0 / jnp.sqrt(sigma * sigma + 1.0), log_hi, log_lo

    across = iota((ROWS, CELLS), 1) % TILE
    down = iota((ROWS, CELLS), 1) // TILE
    ring_row = iota((128, 4 * CELLS), 0)
    column = iota((128, 4 * CELLS), 1)
    shift = column // CELLS - 2
    cell_x = column % TILE
    cell_y = (column % CELLS) // TILE
    line_x = cell_x + shift
    from_line = jnp.where(
        line_x < 0, 3 * TILE, jnp.where(line_x >= TILE, 3 * TILE + 1, 2 * TILE + line_x)
    )
    from_side = jnp.where(cell_x == 0, cell_y, TILE + cell_y)
    spread = (ring_row == jnp.where(column < CELLS, from_side, from_line)).astype(BF)
    ring_low = []
    for p in range(2 * FR_DEV):
        scale, log_hi, log_lo = scales(p, 128)
        ring_low.append(with_log_rows(rings[p] * scale, log_hi, log_lo, 128))
    images[...] = mm(jnp.concatenate(ring_low, axis=0).astype(BF), spread).reshape(
        2 * FR_DEV, ROWS, 4 * CELLS
    )

    def features(p):
        scale, log_hi, log_lo = scales(p, CELLS)
        inner = with_log_rows(states[p] * scale, log_hi, log_lo, CELLS)
        inner_low = inner.astype(BF)
        inner = inner_low.astype(F32)
        sides = images[p, :, 0:CELLS]
        shifted = (
            jnp.where(across == 0, sides, pltpu.roll(inner, 1, 1)),
            inner,
            jnp.where(across == TILE - 1, sides, pltpu.roll(inner, CELLS - 1, 1)),
        )
        up = []
        low = []
        for b in range(3):
            line = images[p, :, (b + 1) * CELLS : (b + 2) * CELLS]
            up.append(jnp.where(down == 0, line * north_here, pltpu.roll(shifted[b], TILE, 1)))
            low.append(
                jnp.where(
                    down == TILE - 1, line * south_here, pltpu.roll(shifted[b], CELLS - TILE, 1)
                )
            )
        windows = jnp.concatenate([*up, *shifted, *low], axis=0).astype(BF)
        convolved = mm(taps_ref[...], windows)
        lifted = mm(lift_ref[...], inner_low)
        hidden = lifted + convolved / (1.0 + jnp.exp(-convolved))
        power = jnp.mean(hidden * hidden, axis=0, keepdims=True)
        return hidden, (hidden * lax.rsqrt(power + 1e-06)).astype(BF)

    def own(p, carry):
        hidden, normed = features(p)
        hidden_all[p] = hidden
        qkv_all[p] = mm(qkv_ref[...], normed).reshape(3 * HEAD, HEADS, CELLS)
        return carry

    def following(p, carry):
        _, normed = features(p)
        qkv_all[p, HEAD : 3 * HEAD] = mm(qkv_ref[WIDTH : 3 * WIDTH, :], normed).reshape(
            2 * HEAD, HEADS, CELLS
        )
        return carry

    lax.fori_loop(0, FR_DEV, own, 0, unroll=UNROLL)
    lax.fori_loop(FR_DEV, 2 * FR_DEV, following, 0, unroll=UNROLL)

    hide = jnp.where(is_last, -jnp.inf, 0.0)
    for half in range(2):
        lanes = slice(half * 128, half * 128 + 128)

        def score(d, sums):
            keys = qkv_all[:, HEAD + d, :, lanes]
            return tuple(
                sums[i] + qkv_all[i, d, :, lanes][None] * keys for i in range(FR_DEV)
            )

        zero = jnp.zeros((2 * FR_DEV, HEADS, 128), F32)
        sums = lax.fori_loop(0, HEAD, score, (zero,) * FR_DEV, unroll=4)
        later = iota((2 * FR_DEV, HEADS, 128), 0) >= FR_DEV
        weights = []
        for i in range(FR_DEV):
            scores = sums[i] * HEAD ** (-0.5) + jnp.where(later, hide, 0.0)
            top = jnp.max(scores, axis=0, keepdims=True)
            raised = jnp.exp(scores - top)
            weights.append(raised / jnp.sum(raised, axis=0, keepdims=True))

        def combine(d, carry):
            values = qkv_all[:, 2 * HEAD + d, :, lanes]
            for i in range(FR_DEV):
                context_all[i, d, :, lanes] = jnp.sum(weights[i] * values, axis=0)
            return carry

        lax.fori_loop(0, HEAD, combine, 0, unroll=4)

    def finish(p, carry):
        context = context_all[p].reshape(WIDTH, CELLS).astype(BF)
        refined = (hidden_all[p] + mm(attend_ref[...], context)).astype(BF)
        projected = mm(decode_ref[...], refined)
        sigma = sigmas[p]
        sigma_next = jnp.full((1, CELLS), plan_ref[level_ref[p] + 1], F32)
        spread = sigma * sigma + 1.0
        slope = (sigma_next - sigma) / sigma
        state = states[p]
        denoised = state / spread + sigma / jnp.sqrt(spread) * projected
        moved = (state + slope * (state - denoised))[0:FIELDS]
        for half in range(2):
            out_ref[pl.ds(p * 2 * FIELDS + half, FIELDS, stride=2), :] = moved[
                :, half * 128 : half * 128 + 128
            ]
        return carry

    lax.fori_loop(0, FR_DEV, finish, 0, unroll=UNROLL)


def rolling_step(step, near, plan, levels, queue, fresh, raw_weights, weights):
    groups = lax.axis_size("noise")
    from_next = [(i + 1, i) for i in range(groups - 1)]
    from_second = [(i + 2, i) for i in range(groups - 2)]
    frames, slots, after = border_lines(step, near, plan, levels, queue, fresh)
    next_frames = lax.ppermute(frames, "noise", from_next)
    slots = lax.all_to_all(slots, TILE_AXES, split_axis=0, concat_axis=0, tiled=True)
    if weights is None:
        weights = prepare_weights(*raw_weights, after)
    rings, pair_rings, far = ring_cells(near, slots, frames, weights[1])
    next_rings = lax.ppermute(pair_rings, "noise", from_next)
    far = lax.ppermute(far, "noise", from_second)
    moved = pl.pallas_call(
        functools.partial(step_kernel, step),
        out_shape=jax.ShapeDtypeStruct((FR_DEV * FIELDS * 2, 128), F32),
        in_specs=[SMEM] * 3 + [VMEM] * 11,
        out_specs=VMEM,
        scratch_shapes=[
            pltpu.VMEM((2 * FR_DEV, ROWS, CELLS), F32),
            pltpu.VMEM((2 * FR_DEV, ROWS, 128), F32),
            pltpu.VMEM((2 * FR_DEV, 1, CELLS), F32),
            pltpu.VMEM((2 * FR_DEV, ROWS, 4 * CELLS), F32),
            pltpu.VMEM((FR_DEV, WIDTH, CELLS), F32),
            pltpu.VMEM((2 * FR_DEV, 3 * HEAD, HEADS, CELLS), F32),
            pltpu.VMEM((FR_DEV, HEAD, HEADS, CELLS), F32),
        ],
        name="step",
    )(near, plan, levels, queue, fresh, rings, next_frames, next_rings, far, *weights)
    return moved, weights


def shards(
    queue_state, fresh_noise, plan, levels, neighbours, in_weight, level_embed, conv_weight,
    norm_gain, query_weight, memory_weight, attend_out, decode_weight,
):
    raw_weights = (
        in_weight, level_embed, conv_weight, norm_gain, query_weight, memory_weight,
        attend_out, decode_weight,
    )
    queue = queue_state.reshape(FR_DEV * FIELDS * 2, 128)
    weights = None
    for step in range(STEPS):
        queue, weights = rolling_step(
            step, neighbours.T, plan, levels, queue, fresh_noise, raw_weights, weights
        )
    return queue.reshape(queue_state.shape)


def solution(mesh):
    split = Mesh(
        mesh.devices.reshape(mesh.shape["noise"], 2, 4, 2), ("noise", "tile_0", "tile_1", "tile_2")
    )
    placed = (
        P("noise", None, TILE_AXES, None),
        P(None, None, TILE_AXES, None),
        P(),
        P("noise"),
        P(),
        P(),
        P(),
        P(),
        P(),
        P(),
        P(),
        P(),
        P(),
    )
    return jax.shard_map(
        shards,
        mesh=split,
        in_specs=placed,
        out_specs=P("noise", None, TILE_AXES, None),
        check_vma=False,
    )
```

```python
import functools

import jax
import jax.numpy as jnp
from jax import lax
from jax.experimental import pallas as pl
from jax.experimental.pallas import tpu as pltpu
from jax.sharding import Mesh
from jax.sharding import PartitionSpec as P

FIELDS = 69
ROWS = 72
WIDTH = 256
HEADS = 8
HEAD = WIDTH // HEADS
TILE = 16
CELLS = TILE * TILE
TAPS = 9
SLOT = 80
UNROLL = 4
FR_DEV = 4
STEPS = 2
NTILES = 16
TILE_AXES = ("tile_0", "tile_1", "tile_2")
BF = jnp.bfloat16
F32 = jnp.float32

VMEM = pl.BlockSpec(memory_space=pltpu.VMEM)
SMEM = pl.BlockSpec(memory_space=pltpu.SMEM)


def iota(shape, dim):
    return lax.broadcasted_iota(jnp.int32, shape, dim)


def mm(a, b):
    return jnp.dot(a, b, preferred_element_type=F32)


def mm_nt(a, b):
    return lax.dot_general(a, b, (((1,), (1,)), ((), ())), preferred_element_type=F32)


def split_hi_lo(v):
    hi = v.astype(BF).astype(F32)
    return hi, v - hi


def weights_kernel(
    in_ref, embed_ref, conv_ref, gain_ref, query_ref, memory_ref, out_ref, decode_ref, after_ref,
    taps_out, lift_out, qkv_out, attend_out, decode_out, folded,
):
    rows = iota((ROWS, WIDTH), 0)
    unit = (iota((ROWS, FIELDS), 0) == iota((ROWS, FIELDS), 1)).astype(BF)
    lift_t = mm(unit, in_ref[...])
    embed = jnp.broadcast_to(embed_ref[...], (ROWS, WIDTH))
    embed_hi, embed_lo = split_hi_lo(embed)
    stacked = jnp.where(
        rows == FIELDS, embed_hi, jnp.where(rows == FIELDS + 1, embed_lo, lift_t)
    ).astype(BF)
    lift_rows = jnp.where(
        rows >= FIELDS, jnp.where(rows == FIELDS + 2, embed_lo, embed_hi), lift_t
    )
    lift_out[...] = jnp.transpose(lift_rows).astype(BF)
    for tap in range(TAPS):
        both = mm_nt(stacked, conv_ref[tap])
        whole = jnp.broadcast_to(
            both[FIELDS : FIELDS + 1] + both[FIELDS + 1 : FIELDS + 2], (ROWS, WIDTH)
        )
        hi, lo = split_hi_lo(whole)
        folded[pl.ds(tap * ROWS, ROWS), :] = jnp.where(
            rows >= FIELDS, jnp.where(rows == FIELDS + 2, lo, hi), both
        )
    taps_out[...] = jnp.transpose(folded[...]).astype(BF)
    place = iota((WIDTH, WIDTH), 0)
    order = ((place % HEADS) * HEAD + place // HEADS == iota((WIDTH, WIDTH), 1)).astype(BF)
    gain = gain_ref[...]
    qkv_out[0:WIDTH, :] = (mm(order, query_ref[...]) * gain).astype(BF)
    for part in range(2):
        qkv_out[pl.ds((part + 1) * WIDTH, WIDTH), :] = (
            mm(order, memory_ref[pl.ds(part * WIDTH, WIDTH), :]) * gain
        ).astype(BF)
    attend_out[...] = mm_nt(out_ref[...], order).astype(BF)
    decode_out[...] = mm(unit, decode_ref[...]).astype(BF)


def prepare_weights(in_weight, embed, conv, gain, query, memory, attend, decode, after):
    return pl.pallas_call(
        weights_kernel,
        out_shape=(
            jax.ShapeDtypeStruct((WIDTH, TAPS * ROWS), BF),
            jax.ShapeDtypeStruct((WIDTH, ROWS), BF),
            jax.ShapeDtypeStruct((3 * WIDTH, WIDTH), BF),
            jax.ShapeDtypeStruct((WIDTH, WIDTH), BF),
            jax.ShapeDtypeStruct((ROWS, WIDTH), BF),
        ),
        in_specs=[VMEM] * 8 + [SMEM],
        out_specs=(VMEM,) * 5,
        scratch_shapes=[pltpu.VMEM((TAPS * ROWS, WIDTH), F32)],
        name="weights",
    )(
        in_weight.T, embed.reshape(1, WIDTH), conv, gain.reshape(1, WIDTH), query, memory, attend,
        decode, after,
    )


def frame_rows(queue_ref, frame):
    halves = [
        queue_ref[pl.ds(frame * 2 * FIELDS + half, FIELDS, stride=2), :] for half in range(2)
    ]
    return jnp.concatenate(halves, axis=1)


def sigma_rows(sigma, lanes):
    rows = iota((8, lanes), 0)
    first, rest = split_hi_lo(jnp.broadcast_to(sigma, (8, lanes)))
    second, third = split_hi_lo(rest)
    return jnp.where(rows == 5, first, jnp.where(rows == 6, second, third))


def border_kernel(
    near_ref, plan_ref, level_ref, queue_ref, fresh_ref,
    frames_out, slots_out, after_out, full, folded, later, lines,
):
    me = lax.axis_index(TILE_AXES)
    after_out[0] = 0
    for f in range(FR_DEV):
        sigma = jnp.full((8, CELLS), plan_ref[level_ref[f]], F32)
        full[pl.ds(f * ROWS + 64, 8), :] = sigma_rows(sigma, CELLS)
        full[pl.ds(f * ROWS, FIELDS), :] = frame_rows(queue_ref, f)
    full[pl.ds(FR_DEV * ROWS + 64, 8), :] = jnp.zeros((8, CELLS), F32)
    full[pl.ds(FR_DEV * ROWS, FIELDS), :] = fresh_ref[1, :, 0, :]

    @pl.when(lax.axis_index("noise") == 0)
    def _():
        full[0:FIELDS, :] = fresh_ref[0, :, 0, :]

    frames = full[...].astype(BF)
    for f in range(FR_DEV):
        frames_out[f] = full[pl.ds(f * ROWS, ROWS), :].astype(BF)
    cell = iota((CELLS, 128), 0)
    want = iota((CELLS, 128), 1)
    line = want // (2 * TILE)
    depth = want % (2 * TILE) // TILE
    along = want % TILE
    source = jnp.where(
        line == 0,
        along * TILE + TILE - 1 - depth,
        jnp.where(
            line == 1,
            along * TILE + depth,
            jnp.where(line == 2, (TILE - 1 - depth) * TILE + along, depth * TILE + along),
        ),
    )
    found = mm(frames, (cell == source).astype(BF))
    later[...] = found[FR_DEV * ROWS :]
    lane = iota((ROWS, 128), 1)
    lane9 = iota((9, 128), 1)
    folded[ROWS:SLOT, :] = jnp.zeros((SLOT - ROWS, 128), F32)
    for r in range(4):
        packed = jnp.zeros((ROWS, 128), F32)
        for f in range(FR_DEV):
            one = found[f * ROWS : (f + 1) * ROWS]
            turn = (2 * TILE * (f - r)) % 128
            if turn:
                one = pltpu.roll(one, turn, 1)
            packed = jnp.where(lane // (2 * TILE) == f, one, packed)
        folded[0:ROWS, :] = packed
        packed = jnp.zeros((9, 128), F32)
        for k in range(8):
            one = later[pl.ds(9 * k, 9), :]
            turn = (TILE * k - 2 * TILE * r) % 128
            if turn:
                one = pltpu.roll(one, turn, 1)
            packed = jnp.where(lane9 // TILE == k, one, packed)
        folded[FIELDS : FIELDS + 9, :] = packed
        lines[r] = folded[...].astype(BF)
    for j in range(NTILES):
        north = near_ref[2, j]
        beside = jnp.maximum(north, near_ref[3, j])
        from_west = jnp.logical_or(near_ref[0, j] == me, near_ref[0, beside] == me)
        from_east = jnp.logical_or(near_ref[1, j] == me, near_ref[1, beside] == me)
        vertical = jnp.where(north >= 0, 2, 3)
        code = jnp.where(from_west, 0, jnp.where(from_east, 1, vertical))
        slots_out[j] = lines[code]


def border_lines(near, plan, levels, queue, fresh):
    return pl.pallas_call(
        border_kernel,
        out_shape=(
            jax.ShapeDtypeStruct((FR_DEV, ROWS, CELLS), BF),
            jax.ShapeDtypeStruct((NTILES, SLOT, 128), BF),
            jax.ShapeDtypeStruct((1,), jnp.int32),
        ),
        in_specs=[SMEM, SMEM, SMEM, VMEM, VMEM],
        out_specs=(VMEM, VMEM, SMEM),
        scratch_shapes=[
            pltpu.VMEM(((FR_DEV + 1) * ROWS, CELLS), F32),
            pltpu.VMEM((SLOT, 128), F32),
            pltpu.VMEM((ROWS, 128), F32),
            pltpu.VMEM((4, SLOT, 128), BF),
        ],
        name="border",
    )(near, plan, levels, queue, fresh)


def halo_lane(row, column, near_row, far_row):
    west = jnp.where(column == -1, row, 64 + row)
    east = jnp.where(column == TILE, TILE + row, 80 + row)
    sides = jnp.where(column < 0, west, east)
    near_line = jnp.where(
        column == -1,
        48,
        jnp.where(column == TILE, 49, jnp.where(column < 0, 112, jnp.where(column > TILE, 115, 32 + column))),
    )
    far_line = jnp.where(
        column == -1,
        113,
        jnp.where(column == TILE, 116, jnp.where(column < 0, 114, jnp.where(column > TILE, 117, 96 + column))),
    )
    inside = jnp.logical_and(row >= 0, row < TILE)
    return jnp.where(
        inside,
        sides,
        jnp.where(row == near_row, near_line, jnp.where(row == far_row, far_line, -1)),
    )


def ring_kernel(near_ref, slots_ref, frames_ref, wait_ref, halo_out, later_out, far_out, picked, spare):
    me = lax.axis_index(TILE_AXES)
    north = near_ref[2, me]
    beside = jnp.maximum(north, near_ref[3, me])
    picked[:, 0:128] = slots_ref[near_ref[0, me]].astype(F32)
    picked[:, 128:256] = slots_ref[near_ref[1, me]].astype(F32)
    picked[:, 256:384] = slots_ref[beside].astype(F32)
    picked[:, 384:512] = slots_ref[near_ref[0, beside]].astype(F32)
    picked[:, 512:640] = slots_ref[near_ref[1, beside]].astype(F32)
    low = picked[...].astype(BF)
    is_north = (north >= 0).astype(jnp.int32)
    near_place = is_north * (TILE - 1)
    far_place = is_north * (TILE - 2) + (1 - is_north)

    def source(lane):
        block = lane // TILE
        along = lane % TILE
        side = jnp.where(block < 3, block, block - 4)
        deep = (lane >= 64).astype(jnp.int32)
        corner = jnp.logical_or(block == 3, block == 7)
        east_corner = jnp.where(block == 3, along, (along >= 3).astype(jnp.int32))
        which = jnp.where(block == 3, 0, 1 + along % 3)
        corner_deep = jnp.logical_or(which == 1, which == 3).astype(jnp.int32)
        corner_place = jnp.where(which >= 2, far_place, near_place)
        known = along < jnp.where(block == 3, 2, 6)
        plain = side * 128 + deep * TILE + along
        ends = (3 + east_corner) * 128 + corner_deep * TILE + corner_place
        lost = jnp.logical_and(corner, jnp.logical_not(known))
        later = jnp.where(corner, (3 + east_corner) * 128 + corner_place, side * 128 + along)
        return (
            jnp.where(lost, -10000, jnp.where(corner, ends, plain)),
            jnp.where(lost, -10000, later),
        )

    column = iota((8, FR_DEV * 128), 1)
    spot = source(column % 128)[0] + 2 * TILE * (column // 128)
    pick = (iota((5 * 128, FR_DEV * 128), 0) == spot[0:1]).astype(BF)
    halos = mm(low[0:ROWS], pick)
    for f in range(FR_DEV):
        halo_out[f] = halos[:, f * 128 : (f + 1) * 128].astype(BF)
    far_out[:, 0:CELLS] = frames_ref[0]
    far_out[:, CELLS : CELLS + 128] = halos[:, 0:128].astype(BF)
    column = iota((8, 8 * 64), 1)
    spot = source(column % 64)[1] + TILE * (column // 64)
    pick = (iota((5 * 128, 8 * 64), 0) == spot[0:1]).astype(BF)
    spare[...] = jnp.zeros_like(spare)
    blocks = mm(picked[64:SLOT].astype(BF), pick)
    for k in range(8):
        one = blocks[5:14, (k // 2) * 128 : (k // 2 + 1) * 128]
        spare[pl.ds(9 * k, 9), :] = pltpu.roll(one, 64, 1) if k % 2 else one
    later_out[...] = spare[...].astype(BF)


def halo_cells(near, slots, frames, wait):
    return pl.pallas_call(
        ring_kernel,
        out_shape=(
            jax.ShapeDtypeStruct((FR_DEV, ROWS, 128), BF),
            jax.ShapeDtypeStruct((ROWS, 128), BF),
            jax.ShapeDtypeStruct((ROWS, CELLS + 128), BF),
        ),
        in_specs=[SMEM, VMEM, VMEM, pl.BlockSpec(memory_space=pl.ANY)],
        out_specs=(VMEM,) * 3,
        scratch_shapes=[pltpu.VMEM((SLOT, 5 * 128), F32), pltpu.VMEM((ROWS, 128), F32)],
        name="ring",
    )(near, slots, frames, wait)


def with_log_rows(scaled, log_hi, log_lo, lanes):
    rows = iota((ROWS, lanes), 0)
    return jnp.where(
        rows >= FIELDS, jnp.where(rows == FIELDS + 1, log_lo, log_hi), scaled
    )


def wide(row, lanes):
    return jnp.concatenate([row] * (lanes // 128), axis=1)


def denoise(
    lanes, near_ref, plan_ref, level_ref, weights, states, sigmas, scaled, images, ring_windows,
    hidden_all, qkv_all, context_all, finished,
):
    taps_ref, lift_ref, qkv_ref, attend_ref, decode_ref = weights
    me = lax.axis_index(TILE_AXES)
    is_last = lax.axis_index("noise") == lax.axis_size("noise") - 1
    at_north = near_ref[2, me] >= 0
    north_here = at_north.astype(F32)
    south_here = 1.0 - north_here
    extended = lanes > CELLS

    for p in range(2 * FR_DEV):
        sigma = sigmas[p]
        log_hi, log_lo = split_hi_lo(jnp.log(sigma))
        scale = 1.0 / jnp.sqrt(sigma * sigma + 1.0)
        total = CELLS + 128
        scaled[p] = with_log_rows(
            states[p] * wide(scale, total), wide(log_hi, total), wide(log_lo, total), total
        )
    ring_row = iota((128, 4 * CELLS), 0)
    column = iota((8, 4 * CELLS), 1)
    shift = column // CELLS - 2
    cell_x = column % TILE
    cell_y = (column % CELLS) // TILE
    line_x = cell_x + shift
    from_line = jnp.where(
        line_x < 0, 3 * TILE, jnp.where(line_x >= TILE, 3 * TILE + 1, 2 * TILE + line_x)
    )
    from_side = jnp.where(cell_x == 0, cell_y, TILE + cell_y)
    spot = jnp.where(column < CELLS, from_side, from_line)
    spread = (ring_row == spot[0:1]).astype(BF)
    low = scaled[...].reshape(2 * FR_DEV * ROWS, CELLS + 128).astype(BF)
    images[...] = mm(low[:, CELLS:], spread).reshape(2 * FR_DEV, ROWS, 4 * CELLS)
    if extended:
        near_row = jnp.where(at_north, -1, TILE)
        far_row = jnp.where(at_north, -2, TILE + 1)
        column = iota((8, 5 * 128), 1)
        tap = column // 64
        cell = column % 64
        block = cell // TILE
        along = cell % TILE
        row = jnp.where(block < 2, along, near_row) + tap // 3 - 1
        col = jnp.where(
            block == 0,
            -1,
            jnp.where(block == 1, TILE, jnp.where(block == 2, along, jnp.where(along == 0, -1, TILE))),
        )
        col = col + tap % 3 - 1
        in_tile = jnp.logical_and(
            jnp.logical_and(row >= 0, row < TILE), jnp.logical_and(col >= 0, col < TILE)
        )
        halo = halo_lane(row, col, near_row, far_row)
        spot = jnp.where(
            in_tile, row * TILE + col, jnp.where(halo >= 0, CELLS + halo, -1)
        )
        spot = jnp.where(cell < 50, spot, -1)
        pick = (iota((CELLS + 128, 5 * 128), 0) == spot[0:1]).astype(BF)
        ring_windows[...] = mm(low, pick).reshape(2 * FR_DEV, ROWS, 5 * 128)

    across = iota((ROWS, CELLS), 1) % TILE
    down = iota((ROWS, CELLS), 1) // TILE

    def features(p):
        inner = scaled[p, :, 0:CELLS].astype(BF).astype(F32)
        sides = images[p, :, 0:CELLS]
        shifted = (
            jnp.where(across == 0, sides, pltpu.roll(inner, 1, 1)),
            inner,
            jnp.where(across == TILE - 1, sides, pltpu.roll(inner, CELLS - 1, 1)),
        )
        up = []
        low = []
        for b in range(3):
            line = images[p, :, (b + 1) * CELLS : (b + 2) * CELLS]
            up.append(jnp.where(down == 0, line * north_here, pltpu.roll(shifted[b], TILE, 1)))
            low.append(
                jnp.where(
                    down == TILE - 1, line * south_here, pltpu.roll(shifted[b], CELLS - TILE, 1)
                )
            )
        windows = jnp.concatenate([*up, *shifted, *low], axis=0)
        if extended:
            beyond = []
            for tap in range(TAPS):
                one = ring_windows[p, :, (tap // 2) * 128 : (tap // 2 + 1) * 128]
                beyond.append(pltpu.roll(one, 64, 1) if tap % 2 else one)
            windows = jnp.concatenate([windows, jnp.concatenate(beyond, axis=0)], axis=1)
        convolved = mm(taps_ref[...], windows.astype(BF))
        lifted = mm(lift_ref[...], scaled[p, :, 0:lanes].astype(BF))
        hidden = lifted + convolved / (1.0 + jnp.exp(-convolved))
        power = jnp.mean(hidden * hidden, axis=0, keepdims=True)
        return hidden, (hidden * lax.rsqrt(power + 1e-06)).astype(BF)

    def own(p, carry):
        hidden, normed = features(p)
        hidden_all[p] = hidden
        qkv_all[p] = mm(qkv_ref[...], normed).reshape(3 * HEAD, HEADS, lanes)
        return carry

    def following(p, carry):
        _, normed = features(p)
        qkv_all[p, HEAD : 3 * HEAD] = mm(qkv_ref[WIDTH : 3 * WIDTH, :], normed).reshape(
            2 * HEAD, HEADS, lanes
        )
        return carry

    lax.fori_loop(0, FR_DEV, own, 0, unroll=UNROLL)
    lax.fori_loop(FR_DEV, 2 * FR_DEV, following, 0, unroll=UNROLL)

    hide = jnp.where(is_last, -jnp.inf, 0.0)
    for part in range(lanes // 128):
        at = slice(part * 128, part * 128 + 128)

        def score(d, sums):
            keys = qkv_all[:, HEAD + d, :, at]
            return tuple(sums[i] + qkv_all[i, d, :, at][None] * keys for i in range(FR_DEV))

        zero = jnp.zeros((2 * FR_DEV, HEADS, 128), F32)
        sums = lax.fori_loop(0, HEAD, score, (zero,) * FR_DEV, unroll=4)
        second_half = iota((2 * FR_DEV, HEADS, 128), 0) >= FR_DEV
        weights = []
        for i in range(FR_DEV):
            scores = sums[i] * HEAD ** (-0.5) + jnp.where(second_half, hide, 0.0)
            top = jnp.max(scores, axis=0, keepdims=True)
            raised = jnp.exp(scores - top)
            weights.append(raised / jnp.sum(raised, axis=0, keepdims=True))

        def combine(d, carry):
            values = qkv_all[:, 2 * HEAD + d, :, at]
            for i in range(FR_DEV):
                context_all[i, d, :, at] = jnp.sum(weights[i] * values, axis=0)
            return carry

        lax.fori_loop(0, HEAD, combine, 0, unroll=4)

    for p in range(FR_DEV):
        context = context_all[p].reshape(WIDTH, lanes).astype(BF)
        refined = (hidden_all[p] + mm(attend_ref[...], context)).astype(BF)
        projected = mm(decode_ref[...], refined)
        sigma = wide(sigmas[p], lanes)
        sigma_next = jnp.full((1, lanes), plan_ref[level_ref[p] + 1], F32)
        spread_of = sigma * sigma + 1.0
        slope = (sigma_next - sigma) / sigma
        state = states[p, :, 0:lanes]
        denoised = state / spread_of + sigma / jnp.sqrt(spread_of) * projected
        finished(p, state + slope * (state - denoised))


def fill_sigmas(plan_ref, level_ref, next_frames_ref, sigmas):
    for f in range(FR_DEV):
        came = next_frames_ref[f, 64:ROWS, 0:128].astype(F32)
        sigmas[f] = jnp.full((1, 128), plan_ref[level_ref[f]], F32)
        sigmas[FR_DEV + f] = came[5:6] + came[6:7] + came[7:8]


def scale_entering(states, sigmas):
    group = lax.axis_index("noise")
    groups = lax.axis_size("noise")
    for p, holder in ((FR_DEV - 1, groups - 1), (2 * FR_DEV - 1, groups - 2)):

        @pl.when(group == holder)
        def _(p=p):
            states[p] = states[p] * wide(sigmas[p], CELLS + 128)


def first_kernel(
    near_ref, plan_ref, level_ref, queue_ref, fresh_ref, halo_ref, later_ref, next_frames_ref,
    next_halo_ref, far_ref, taps_ref, lift_ref, qkv_ref, attend_ref, decode_ref,
    own_out, near_out, far_out,
    states, sigmas, scaled, images, ring_windows, hidden_all, qkv_all, context_all, message,
):
    fill_sigmas(plan_ref, level_ref, next_frames_ref, sigmas)
    for p in range(FR_DEV - 1):
        states[p, 64:ROWS, 0:CELLS] = jnp.zeros((ROWS - 64, CELLS), F32)
        states[p, 0:FIELDS, 0:CELLS] = frame_rows(queue_ref, p + 1)
        states[p, :, CELLS:] = halo_ref[p + 1].astype(F32)
    for f in range(FR_DEV):
        states[FR_DEV - 1 + f, :, 0:CELLS] = next_frames_ref[f].astype(F32)
        states[FR_DEV - 1 + f, :, CELLS:] = next_halo_ref[f].astype(F32)
    states[2 * FR_DEV - 1] = far_ref[...].astype(F32)
    scale_entering(states, sigmas)

    def finished(p, moved):
        own_out[p] = moved
        message[p, 0:64] = moved[0:64]
        rows = iota((8, CELLS + 128), 0)
        message[p, 64:ROWS] = jnp.where(
            rows >= FIELDS - 64, sigma_rows(wide(sigmas[p], CELLS + 128), CELLS + 128), moved[64:ROWS]
        )

    denoise(
        CELLS + 128, near_ref, plan_ref, level_ref,
        (taps_ref, lift_ref, qkv_ref, attend_ref, decode_ref),
        states, sigmas, scaled, images, ring_windows, hidden_all, qkv_all, context_all, finished,
    )

    @pl.when(lax.axis_index("noise") == 0)
    def _():
        message[0, 0:FIELDS, 0:CELLS] = fresh_ref[1, :, 0, :]
        message[0, 0:FIELDS, CELLS:] = later_ref[...].astype(F32)[0:FIELDS]

    lane = iota((ROWS, 128), 1)
    for f in range(FR_DEV):
        near_out[f] = message[f, :, 0:CELLS].astype(BF)
    for pair in range(2):
        near_out[FR_DEV, :, pair * 128 : pair * 128 + 128] = jnp.where(
            lane < 64,
            message[2 * pair, :, CELLS:],
            pltpu.roll(message[2 * pair + 1, :, CELLS:], 64, 1),
        ).astype(BF)
    far_out[...] = message[0].astype(BF)


def second_kernel(
    near_ref, plan_ref, level_ref, own_ref, came_ref, far_ref,
    taps_ref, lift_ref, qkv_ref, attend_ref, decode_ref,
    out_ref, states, sigmas, scaled, images, hidden_all, qkv_all, context_all,
):
    fill_sigmas(plan_ref, level_ref, came_ref, sigmas)
    for p in range(FR_DEV - 1):
        states[p] = own_ref[p + 1]
    for f in range(FR_DEV):
        states[FR_DEV - 1 + f, :, 0:CELLS] = came_ref[f].astype(F32)
        pair = came_ref[FR_DEV, :, (f // 2) * 128 : (f // 2 + 1) * 128].astype(F32)
        states[FR_DEV - 1 + f, :, CELLS:] = pltpu.roll(pair, 64, 1) if f % 2 else pair
    states[2 * FR_DEV - 1] = far_ref[...].astype(F32)
    scale_entering(states, sigmas)

    def finished(p, moved):
        for half in range(2):
            out_ref[pl.ds(p * 2 * FIELDS + half, FIELDS, stride=2), :] = moved[
                0:FIELDS, half * 128 : half * 128 + 128
            ]

    denoise(
        CELLS, near_ref, plan_ref, level_ref,
        (taps_ref, lift_ref, qkv_ref, attend_ref, decode_ref),
        states, sigmas, scaled, images, None, hidden_all, qkv_all, context_all, finished,
    )


def common_scratch(lanes):
    frames = 2 * FR_DEV
    return [
        pltpu.VMEM((frames, ROWS, CELLS + 128), F32),
        pltpu.VMEM((frames, 1, 128), F32),
        pltpu.VMEM((frames, ROWS, CELLS + 128), F32),
        pltpu.VMEM((frames, ROWS, 4 * CELLS), F32),
    ], [
        pltpu.VMEM((FR_DEV, WIDTH, lanes), F32),
        pltpu.VMEM((frames, 3 * HEAD, HEADS, lanes), F32),
        pltpu.VMEM((FR_DEV, HEAD, HEADS, lanes), F32),
    ]


def shards(
    queue_state, fresh_noise, plan, levels, neighbours, in_weight, level_embed, conv_weight,
    norm_gain, query_weight, memory_weight, attend_out, decode_weight,
):
    groups = lax.axis_size("noise")
    from_next = [((i + 1) % groups, i) for i in range(groups)]
    from_second = [((i + 2) % groups, i) for i in range(groups)]
    near = neighbours.T
    queue = queue_state.reshape(FR_DEV * FIELDS * 2, 128)
    frames, slots, after = border_lines(near, plan, levels, queue, fresh_noise)
    next_frames = lax.ppermute(frames, "noise", from_next)
    slots = lax.all_to_all(slots, TILE_AXES, split_axis=0, concat_axis=0, tiled=True)
    weights = prepare_weights(
        in_weight, level_embed, conv_weight, norm_gain, query_weight, memory_weight,
        attend_out, decode_weight, after,
    )
    halos, later, far = halo_cells(near, slots, frames, weights[1])
    next_halos = lax.ppermute(halos, "noise", from_next)
    far = lax.ppermute(far, "noise", from_second)
    before, after_features = common_scratch(CELLS + 128)
    own, near_message, far_message = pl.pallas_call(
        first_kernel,
        out_shape=(
            jax.ShapeDtypeStruct((FR_DEV, ROWS, CELLS + 128), F32),
            jax.ShapeDtypeStruct((FR_DEV + 1, ROWS, CELLS), BF),
            jax.ShapeDtypeStruct((ROWS, CELLS + 128), BF),
        ),
        in_specs=[SMEM] * 3 + [VMEM] * 12,
        out_specs=(VMEM,) * 3,
        scratch_shapes=[
            *before,
            pltpu.VMEM((2 * FR_DEV, ROWS, 5 * 128), F32),
            *after_features,
            pltpu.VMEM((FR_DEV, ROWS, CELLS + 128), F32),
        ],
        name="first",
    )(
        near, plan, levels, queue, fresh_noise, halos, later, next_frames, next_halos, far, *weights
    )
    came = lax.ppermute(near_message, "noise", from_next)
    far = lax.ppermute(far_message, "noise", from_second)
    before, after_features = common_scratch(CELLS)
    moved = pl.pallas_call(
        second_kernel,
        out_shape=jax.ShapeDtypeStruct((FR_DEV * FIELDS * 2, 128), F32),
        in_specs=[SMEM] * 3 + [VMEM] * 8,
        out_specs=VMEM,
        scratch_shapes=[*before, *after_features],
        name="second",
    )(near, plan, levels, own, came, far, *weights)
    return moved.reshape(queue_state.shape)


def solution(mesh):
    split = Mesh(
        mesh.devices.reshape(mesh.shape["noise"], 2, 4, 2), ("noise", "tile_0", "tile_1", "tile_2")
    )
    placed = (
        P("noise", None, TILE_AXES, None),
        P(None, None, TILE_AXES, None),
        P(),
        P("noise"),
        P(),
        P(),
        P(),
        P(),
        P(),
        P(),
        P(),
        P(),
        P(),
    )
    return jax.shard_map(
        shards,
        mesh=split,
        in_specs=placed,
        out_specs=P("noise", None, TILE_AXES, None),
        check_vma=False,
    )
```

```python
import jax
import jax.numpy as jnp
from jax import lax
from jax.experimental import pallas as pl
from jax.experimental.pallas import tpu as pltpu
from jax.sharding import Mesh
from jax.sharding import PartitionSpec as P

FIELDS = 69
ROWS = 72
WIDTH = 256
HEADS = 8
HEAD = WIDTH // HEADS
TILE = 16
CELLS = TILE * TILE
TAPS = 9
SLOT = 80
FR_DEV = 4
NTILES = 16
TILE_AXES = ("tile_0", "tile_1", "tile_2")
BF = jnp.bfloat16
F32 = jnp.float32

VMEM = pl.BlockSpec(memory_space=pltpu.VMEM)
SMEM = pl.BlockSpec(memory_space=pltpu.SMEM)


def near_core(array):
    return pltpu.with_memory_space_constraint(array, pltpu.VMEM)


def far_from_core(array):
    return pltpu.with_memory_space_constraint(array, pltpu.HBM)


def iota(shape, dim):
    return lax.broadcasted_iota(jnp.int32, shape, dim)


def mm(a, b):
    return jnp.dot(a, b, preferred_element_type=F32)


def mm_nt(a, b):
    return lax.dot_general(a, b, (((1,), (1,)), ((), ())), preferred_element_type=F32)


def split_hi_lo(v):
    hi = v.astype(BF).astype(F32)
    return hi, v - hi


def weights_kernel(
    in_ref, embed_ref, conv_ref, gain_ref, query_ref, memory_ref, out_ref, decode_ref, after_ref,
    taps_out, lift_out, qkv_out, attend_out, decode_out, folded,
):
    rows = iota((ROWS, WIDTH), 0)
    unit = (iota((ROWS, FIELDS), 0) == iota((ROWS, FIELDS), 1)).astype(BF)
    lift_t = mm(unit, in_ref[...])
    embed = jnp.broadcast_to(embed_ref[...], (ROWS, WIDTH))
    embed_hi, embed_lo = split_hi_lo(embed)
    stacked = jnp.where(
        rows == FIELDS, embed_hi, jnp.where(rows == FIELDS + 1, embed_lo, lift_t)
    ).astype(BF)
    lift_rows = jnp.where(
        rows >= FIELDS, jnp.where(rows == FIELDS + 2, embed_lo, embed_hi), lift_t
    )
    lift_out[...] = jnp.transpose(lift_rows).astype(BF)
    for tap in range(TAPS):
        both = mm_nt(stacked, conv_ref[tap])
        whole = jnp.broadcast_to(
            both[FIELDS : FIELDS + 1] + both[FIELDS + 1 : FIELDS + 2], (ROWS, WIDTH)
        )
        hi, lo = split_hi_lo(whole)
        folded[pl.ds(tap * ROWS, ROWS), :] = jnp.where(
            rows >= FIELDS, jnp.where(rows == FIELDS + 2, lo, hi), both
        )
    taps_out[...] = jnp.transpose(folded[...]).astype(BF)
    place = iota((WIDTH, WIDTH), 0)
    order = ((place % HEADS) * HEAD + place // HEADS == iota((WIDTH, WIDTH), 1)).astype(BF)
    gain = gain_ref[...]
    qkv_out[0:WIDTH, :] = (mm(order, query_ref[...]) * gain).astype(BF)
    for part in range(2):
        qkv_out[pl.ds((part + 1) * WIDTH, WIDTH), :] = (
            mm(order, memory_ref[pl.ds(part * WIDTH, WIDTH), :]) * gain
        ).astype(BF)
    attend_out[...] = mm_nt(out_ref[...], order).astype(BF)
    decode_out[...] = mm(unit, decode_ref[...]).astype(BF)


def prepare_weights(in_weight, embed, conv, gain, query, memory, attend, decode, after):
    return pl.pallas_call(
        weights_kernel,
        out_shape=(
            pltpu.VMEM((WIDTH, TAPS * ROWS), BF),
            pltpu.VMEM((WIDTH, ROWS), BF),
            pltpu.VMEM((3 * WIDTH, WIDTH), BF),
            pltpu.VMEM((WIDTH, WIDTH), BF),
            pltpu.VMEM((ROWS, WIDTH), BF),
        ),
        in_specs=[VMEM] * 8 + [SMEM],
        out_specs=(VMEM,) * 5,
        scratch_shapes=[pltpu.VMEM((TAPS * ROWS, WIDTH), F32)],
        compiler_params=pltpu.CompilerParams(vmem_limit_bytes=40 << 20),
        name="weights",
    )(
        *map(
            far_from_core,
            (
                in_weight.T, embed.reshape(1, WIDTH), conv, gain.reshape(1, WIDTH), query, memory,
                attend, decode,
            ),
        ),
        after,
    )


def frame_rows(queue_ref, frame):
    halves = [
        queue_ref[pl.ds(frame * 2 * FIELDS + half, FIELDS, stride=2), :] for half in range(2)
    ]
    return jnp.concatenate(halves, axis=1)


def sigma_rows(sigma, lanes):
    rows = iota((8, lanes), 0)
    first, rest = split_hi_lo(jnp.broadcast_to(sigma, (8, lanes)))
    second, third = split_hi_lo(rest)
    return jnp.where(rows == 5, first, jnp.where(rows == 6, second, third))


def border_kernel(
    near_ref, plan_ref, level_ref, queue_ref, fresh_ref,
    frames_out, front_out, slots_out, after_out, full, folded, later, lines,
):
    me = lax.axis_index(TILE_AXES)
    after_out[0] = 0
    for f in range(FR_DEV):
        sigma = jnp.full((8, CELLS), plan_ref[level_ref[f]], F32)
        full[pl.ds(f * ROWS + 64, 8), :] = sigma_rows(sigma, CELLS)
        full[pl.ds(f * ROWS, FIELDS), :] = frame_rows(queue_ref, f)
    full[pl.ds(FR_DEV * ROWS + 64, 8), :] = jnp.zeros((8, CELLS), F32)
    full[pl.ds(FR_DEV * ROWS, FIELDS), :] = fresh_ref[1, :, 0, :]

    @pl.when(lax.axis_index("noise") == 0)
    def _():
        full[0:FIELDS, :] = fresh_ref[0, :, 0, :]

    frames = full[...].astype(BF)
    for f in range(FR_DEV):
        frames_out[f] = full[pl.ds(f * ROWS, ROWS), :].astype(BF)
    front_out[...] = full[0:ROWS, :].astype(BF)
    cell = iota((CELLS, 128), 0)
    want = iota((CELLS, 128), 1)
    line = want // (2 * TILE)
    depth = want % (2 * TILE) // TILE
    along = want % TILE
    source = jnp.where(
        line == 0,
        along * TILE + TILE - 1 - depth,
        jnp.where(
            line == 1,
            along * TILE + depth,
            jnp.where(line == 2, (TILE - 1 - depth) * TILE + along, depth * TILE + along),
        ),
    )
    found = mm(frames, (cell == source).astype(BF))
    later[...] = found[FR_DEV * ROWS :]
    lane = iota((ROWS, 128), 1)
    lane9 = iota((9, 128), 1)
    folded[ROWS:SLOT, :] = jnp.zeros((SLOT - ROWS, 128), F32)
    for r in range(4):
        packed = jnp.zeros((ROWS, 128), F32)
        for f in range(FR_DEV):
            one = found[f * ROWS : (f + 1) * ROWS]
            turn = (2 * TILE * (f - r)) % 128
            if turn:
                one = pltpu.roll(one, turn, 1)
            packed = jnp.where(lane // (2 * TILE) == f, one, packed)
        folded[0:ROWS, :] = packed
        packed = jnp.zeros((9, 128), F32)
        for k in range(8):
            one = later[pl.ds(9 * k, 9), :]
            turn = (TILE * k - 2 * TILE * r) % 128
            if turn:
                one = pltpu.roll(one, turn, 1)
            packed = jnp.where(lane9 // TILE == k, one, packed)
        folded[FIELDS : FIELDS + 9, :] = packed
        lines[r] = folded[...].astype(BF)
    for j in range(NTILES):
        north = near_ref[2, j]
        beside = jnp.maximum(north, near_ref[3, j])
        from_west = jnp.logical_or(near_ref[0, j] == me, near_ref[0, beside] == me)
        from_east = jnp.logical_or(near_ref[1, j] == me, near_ref[1, beside] == me)
        vertical = jnp.where(north >= 0, 2, 3)
        code = jnp.where(from_west, 0, jnp.where(from_east, 1, vertical))
        slots_out[j] = lines[code]


def border_lines(near, plan, levels, queue, fresh):
    return pl.pallas_call(
        border_kernel,
        out_shape=(
            jax.ShapeDtypeStruct((FR_DEV, ROWS, CELLS), BF),
            jax.ShapeDtypeStruct((ROWS, CELLS), BF),
            jax.ShapeDtypeStruct((NTILES, SLOT, 128), BF),
            jax.ShapeDtypeStruct((1,), jnp.int32),
        ),
        in_specs=[SMEM, SMEM, SMEM, VMEM, VMEM],
        out_specs=(VMEM, VMEM, VMEM, SMEM),
        scratch_shapes=[
            pltpu.VMEM(((FR_DEV + 1) * ROWS, CELLS), F32),
            pltpu.VMEM((SLOT, 128), F32),
            pltpu.VMEM((ROWS, 128), F32),
            pltpu.VMEM((4, SLOT, 128), BF),
        ],
        compiler_params=pltpu.CompilerParams(vmem_limit_bytes=40 << 20),
        name="border",
    )(near, plan, levels, queue, fresh)


def halo_lane(row, column, near_row, far_row):
    west = jnp.where(column == -1, row, 64 + row)
    east = jnp.where(column == TILE, TILE + row, 80 + row)
    sides = jnp.where(column < 0, west, east)
    near_line = jnp.where(
        column == -1,
        48,
        jnp.where(column == TILE, 49, jnp.where(column < 0, 112, jnp.where(column > TILE, 115, 32 + column))),
    )
    far_line = jnp.where(
        column == -1,
        113,
        jnp.where(column == TILE, 116, jnp.where(column < 0, 114, jnp.where(column > TILE, 117, 96 + column))),
    )
    inside = jnp.logical_and(row >= 0, row < TILE)
    return jnp.where(
        inside,
        sides,
        jnp.where(row == near_row, near_line, jnp.where(row == far_row, far_line, -1)),
    )


def ring_kernel(near_ref, slots_ref, wait_ref, halo_out, front_out, later_out, picked, spare):
    me = lax.axis_index(TILE_AXES)
    north = near_ref[2, me]
    beside = jnp.maximum(north, near_ref[3, me])
    picked[:, 0:128] = slots_ref[near_ref[0, me]].astype(F32)
    picked[:, 128:256] = slots_ref[near_ref[1, me]].astype(F32)
    picked[:, 256:384] = slots_ref[beside].astype(F32)
    picked[:, 384:512] = slots_ref[near_ref[0, beside]].astype(F32)
    picked[:, 512:640] = slots_ref[near_ref[1, beside]].astype(F32)
    low = picked[...].astype(BF)
    is_north = (north >= 0).astype(jnp.int32)
    near_place = is_north * (TILE - 1)
    far_place = is_north * (TILE - 2) + (1 - is_north)

    def source(lane):
        block = lane // TILE
        along = lane % TILE
        side = jnp.where(block < 3, block, block - 4)
        deep = (lane >= 64).astype(jnp.int32)
        corner = jnp.logical_or(block == 3, block == 7)
        east_corner = jnp.where(block == 3, along, (along >= 3).astype(jnp.int32))
        which = jnp.where(block == 3, 0, 1 + along % 3)
        corner_deep = jnp.logical_or(which == 1, which == 3).astype(jnp.int32)
        corner_place = jnp.where(which >= 2, far_place, near_place)
        known = along < jnp.where(block == 3, 2, 6)
        plain = side * 128 + deep * TILE + along
        ends = (3 + east_corner) * 128 + corner_deep * TILE + corner_place
        lost = jnp.logical_and(corner, jnp.logical_not(known))
        later = jnp.where(corner, (3 + east_corner) * 128 + corner_place, side * 128 + along)
        return (
            jnp.where(lost, -10000, jnp.where(corner, ends, plain)),
            jnp.where(lost, -10000, later),
        )

    column = iota((8, FR_DEV * 128), 1)
    spot = source(column % 128)[0] + 2 * TILE * (column // 128)
    pick = (iota((5 * 128, FR_DEV * 128), 0) == spot[0:1]).astype(BF)
    halos = mm(low[0:ROWS], pick)
    for f in range(FR_DEV):
        halo_out[f] = halos[:, f * 128 : (f + 1) * 128].astype(BF)
    front_out[...] = halos[:, 0:128].astype(BF)
    column = iota((8, 8 * 64), 1)
    spot = source(column % 64)[1] + TILE * (column // 64)
    pick = (iota((5 * 128, 8 * 64), 0) == spot[0:1]).astype(BF)
    spare[...] = jnp.zeros_like(spare)
    blocks = mm(picked[64:SLOT].astype(BF), pick)
    for k in range(8):
        one = blocks[5:14, (k // 2) * 128 : (k // 2 + 1) * 128]
        spare[pl.ds(9 * k, 9), :] = pltpu.roll(one, 64, 1) if k % 2 else one
    later_out[...] = spare[...].astype(BF)


def halo_cells(near, slots, wait):
    return pl.pallas_call(
        ring_kernel,
        out_shape=(
            jax.ShapeDtypeStruct((FR_DEV, ROWS, 128), BF),
            jax.ShapeDtypeStruct((ROWS, 128), BF),
            jax.ShapeDtypeStruct((ROWS, 128), BF),
        ),
        in_specs=[SMEM, VMEM, pl.BlockSpec(memory_space=pl.ANY)],
        out_specs=(VMEM,) * 3,
        scratch_shapes=[pltpu.VMEM((SLOT, 5 * 128), F32), pltpu.VMEM((ROWS, 128), F32)],
        compiler_params=pltpu.CompilerParams(vmem_limit_bytes=40 << 20),
        name="ring",
    )(near, slots, wait)


def with_log_rows(scaled, log_hi, log_lo, lanes):
    rows = iota((ROWS, lanes), 0)
    return jnp.where(
        rows >= FIELDS, jnp.where(rows == FIELDS + 1, log_lo, log_hi), scaled
    )


def wide(row, lanes):
    return jnp.concatenate([row] * (lanes // 128), axis=1)


def features_of(
    frames, lanes, near_ref, taps_ref, lift_ref, states, sigmas, scaled, images, ring_windows
):
    me = lax.axis_index(TILE_AXES)
    at_north = near_ref[2, me] >= 0
    north_here = at_north.astype(F32)
    south_here = 1.0 - north_here
    extended = lanes > CELLS
    count = len(frames)
    begin = frames[0]
    total = CELLS + 128

    for p in frames:
        sigma = sigmas[p]
        log_hi, log_lo = split_hi_lo(jnp.log(sigma))
        scale = 1.0 / jnp.sqrt(sigma * sigma + 1.0)
        scaled[p] = with_log_rows(
            states[p] * wide(scale, total), wide(log_hi, total), wide(log_lo, total), total
        )
    ring_row = iota((128, 4 * CELLS), 0)
    column = iota((8, 4 * CELLS), 1)
    shift = column // CELLS - 2
    cell_x = column % TILE
    cell_y = (column % CELLS) // TILE
    line_x = cell_x + shift
    from_line = jnp.where(
        line_x < 0, 3 * TILE, jnp.where(line_x >= TILE, 3 * TILE + 1, 2 * TILE + line_x)
    )
    from_side = jnp.where(cell_x == 0, cell_y, TILE + cell_y)
    spot = jnp.where(column < CELLS, from_side, from_line)
    spread = (ring_row == spot[0:1]).astype(BF)
    low = scaled[begin : begin + count].reshape(count * ROWS, total).astype(BF)
    images[begin : begin + count] = mm(low[:, CELLS:], spread).reshape(count, ROWS, 4 * CELLS)
    if extended:
        near_row = jnp.where(at_north, -1, TILE)
        far_row = jnp.where(at_north, -2, TILE + 1)
        column = iota((8, 5 * 128), 1)
        tap = column // 64
        cell = column % 64
        block = cell // TILE
        along = cell % TILE
        row = jnp.where(block < 2, along, near_row) + tap // 3 - 1
        col = jnp.where(
            block == 0,
            -1,
            jnp.where(block == 1, TILE, jnp.where(block == 2, along, jnp.where(along == 0, -1, TILE))),
        )
        col = col + tap % 3 - 1
        in_tile = jnp.logical_and(
            jnp.logical_and(row >= 0, row < TILE), jnp.logical_and(col >= 0, col < TILE)
        )
        halo = halo_lane(row, col, near_row, far_row)
        spot = jnp.where(
            in_tile, row * TILE + col, jnp.where(halo >= 0, CELLS + halo, -1)
        )
        spot = jnp.where(cell < 50, spot, -1)
        pick = (iota((CELLS + 128, 5 * 128), 0) == spot[0:1]).astype(BF)
        ring_windows[begin : begin + count] = mm(low, pick).reshape(count, ROWS, 5 * 128)

    across = iota((ROWS, CELLS), 1) % TILE
    down = iota((ROWS, CELLS), 1) // TILE

    def features(p):
        inner = scaled[p, :, 0:CELLS].astype(BF).astype(F32)
        sides = images[p, :, 0:CELLS]
        shifted = (
            jnp.where(across == 0, sides, pltpu.roll(inner, 1, 1)),
            inner,
            jnp.where(across == TILE - 1, sides, pltpu.roll(inner, CELLS - 1, 1)),
        )
        up = []
        low = []
        for b in range(3):
            line = images[p, :, (b + 1) * CELLS : (b + 2) * CELLS]
            up.append(jnp.where(down == 0, line * north_here, pltpu.roll(shifted[b], TILE, 1)))
            low.append(
                jnp.where(
                    down == TILE - 1, line * south_here, pltpu.roll(shifted[b], CELLS - TILE, 1)
                )
            )
        windows = jnp.concatenate([*up, *shifted, *low], axis=0)
        if extended:
            beyond = []
            for tap in range(TAPS):
                one = ring_windows[p, :, (tap // 2) * 128 : (tap // 2 + 1) * 128]
                beyond.append(pltpu.roll(one, 64, 1) if tap % 2 else one)
            windows = jnp.concatenate([windows, jnp.concatenate(beyond, axis=0)], axis=1)
        convolved = mm(taps_ref[...], windows.astype(BF))
        lifted = mm(lift_ref[...], scaled[p, :, 0:lanes].astype(BF))
        hidden = lifted + convolved / (1.0 + jnp.exp(-convolved))
        power = jnp.mean(hidden * hidden, axis=0, keepdims=True)
        return hidden, (hidden * lax.rsqrt(power + 1e-06)).astype(BF)

    return features


OWN = range(FR_DEV - 1)
REST = range(FR_DEV - 1, 2 * FR_DEV)


def own_frames(lanes, near_ref, weights, states, sigmas, scratch, hidden_out, qkv_out):
    taps_ref, lift_ref, qkv_ref = weights
    features = features_of(OWN, lanes, near_ref, taps_ref, lift_ref, states, sigmas, *scratch)
    for p in OWN:
        hidden, normed = features(p)
        hidden_out[p] = hidden
        qkv_out[p] = mm(qkv_ref[...], normed).reshape(3 * HEAD, HEADS, lanes)


def denoise(
    lanes, near_ref, plan_ref, level_ref, weights, states, sigmas, scratch,
    hidden_own, qkv_own, hidden_all, qkv_all, context_all, arrived, finished,
):
    taps_ref, lift_ref, qkv_ref, attend_ref, decode_ref = weights
    is_last = lax.axis_index("noise") == lax.axis_size("noise") - 1
    held = len(OWN)
    copies = (
        pltpu.make_async_copy(qkv_own, qkv_all.at[pl.ds(0, held)], arrived.at[0]),
        pltpu.make_async_copy(hidden_own, hidden_all.at[pl.ds(0, held)], arrived.at[1]),
    )
    for copy in copies:
        copy.start()
    features = features_of(REST, lanes, near_ref, taps_ref, lift_ref, states, sigmas, *scratch)
    for p in REST:
        hidden, normed = features(p)
        if p < FR_DEV:
            hidden_all[p] = hidden
            qkv_all[p] = mm(qkv_ref[...], normed).reshape(3 * HEAD, HEADS, lanes)
        else:
            qkv_all[p, HEAD : 3 * HEAD] = mm(qkv_ref[WIDTH : 3 * WIDTH, :], normed).reshape(
                2 * HEAD, HEADS, lanes
            )
    for copy in copies:
        copy.wait()

    hide = jnp.where(is_last, -jnp.inf, 0.0)
    for part in range(lanes // 128):
        at = slice(part * 128, part * 128 + 128)

        def score(d, sums):
            keys = qkv_all[:, HEAD + d, :, at]
            return tuple(sums[i] + qkv_all[i, d, :, at][None] * keys for i in range(FR_DEV))

        zero = jnp.zeros((2 * FR_DEV, HEADS, 128), F32)
        sums = lax.fori_loop(0, HEAD, score, (zero,) * FR_DEV, unroll=4)
        second_half = iota((2 * FR_DEV, HEADS, 128), 0) >= FR_DEV
        weights = []
        for i in range(FR_DEV):
            scores = sums[i] * HEAD ** (-0.5) + jnp.where(second_half, hide, 0.0)
            top = jnp.max(scores, axis=0, keepdims=True)
            raised = jnp.exp(scores - top)
            weights.append(raised / jnp.sum(raised, axis=0, keepdims=True))

        def combine(d, carry):
            values = qkv_all[:, 2 * HEAD + d, :, at]
            for i in range(FR_DEV):
                context_all[i, d, :, at] = jnp.sum(weights[i] * values, axis=0)
            return carry

        lax.fori_loop(0, HEAD, combine, 0, unroll=4)

    for p in range(FR_DEV):
        context = context_all[p].reshape(WIDTH, lanes).astype(BF)
        refined = (hidden_all[p] + mm(attend_ref[...], context)).astype(BF)
        projected = mm(decode_ref[...], refined)
        sigma = wide(sigmas[p], lanes)
        sigma_next = jnp.full((1, lanes), plan_ref[level_ref[p] + 1], F32)
        spread_of = sigma * sigma + 1.0
        slope = (sigma_next - sigma) / sigma
        state = states[p, :, 0:lanes]
        denoised = state / spread_of + sigma / jnp.sqrt(spread_of) * projected
        finished(p, state + slope * (state - denoised))


def own_sigmas(plan_ref, level_ref, sigmas):
    for f in range(FR_DEV):
        sigmas[f] = jnp.full((1, 128), plan_ref[level_ref[f]], F32)


def next_sigmas(next_frames_ref, sigmas):
    for f in range(FR_DEV):
        came = next_frames_ref[f, 64:ROWS, 0:128].astype(F32)
        sigmas[FR_DEV + f] = came[5:6] + came[6:7] + came[7:8]


def scale_entering(states, sigmas):
    group = lax.axis_index("noise")
    groups = lax.axis_size("noise")
    for p, holder in ((FR_DEV - 1, groups - 1), (2 * FR_DEV - 1, groups - 2)):

        @pl.when(group == holder)
        def _(p=p):
            states[p] = states[p] * wide(sigmas[p], CELLS + 128)


def first_own_states(queue_ref, halo_ref, states):
    for p in OWN:
        states[p, 64:ROWS, 0:CELLS] = jnp.zeros((ROWS - 64, CELLS), F32)
        states[p, 0:FIELDS, 0:CELLS] = frame_rows(queue_ref, p + 1)
        states[p, :, CELLS:] = halo_ref[p + 1].astype(F32)


def first_own_kernel(
    near_ref, plan_ref, level_ref, queue_ref, halo_ref, taps_ref, lift_ref, qkv_ref,
    hidden_out, qkv_out, states, sigmas, *scratch,
):
    own_sigmas(plan_ref, level_ref, sigmas)
    first_own_states(queue_ref, halo_ref, states)
    own_frames(
        CELLS + 128, near_ref, (taps_ref, lift_ref, qkv_ref), states, sigmas, scratch,
        hidden_out, qkv_out,
    )


def first_kernel(
    near_ref, plan_ref, level_ref, queue_ref, fresh_ref, halo_ref, later_ref, next_frames_ref,
    next_halo_ref, far_ref, far_halo_ref, hidden_own, qkv_own,
    taps_ref, lift_ref, qkv_ref, attend_ref, decode_ref,
    own_out, near_out, far_out,
    states, sigmas, scaled, images, ring_windows, hidden_all, qkv_all, context_all, arrived, message,
):
    own_sigmas(plan_ref, level_ref, sigmas)
    next_sigmas(next_frames_ref, sigmas)
    first_own_states(queue_ref, halo_ref, states)
    for f in range(FR_DEV):
        states[FR_DEV - 1 + f, :, 0:CELLS] = next_frames_ref[f].astype(F32)
        states[FR_DEV - 1 + f, :, CELLS:] = next_halo_ref[f].astype(F32)
    states[2 * FR_DEV - 1, :, 0:CELLS] = far_ref[...].astype(F32)
    states[2 * FR_DEV - 1, :, CELLS:] = far_halo_ref[...].astype(F32)
    scale_entering(states, sigmas)

    def finished(p, moved):
        own_out[p] = moved
        message[p, 0:64] = moved[0:64]
        rows = iota((8, CELLS + 128), 0)
        message[p, 64:ROWS] = jnp.where(
            rows >= FIELDS - 64, sigma_rows(wide(sigmas[p], CELLS + 128), CELLS + 128), moved[64:ROWS]
        )

    denoise(
        CELLS + 128, near_ref, plan_ref, level_ref,
        (taps_ref, lift_ref, qkv_ref, attend_ref, decode_ref),
        states, sigmas, (scaled, images, ring_windows), hidden_own, qkv_own,
        hidden_all, qkv_all, context_all, arrived, finished,
    )

    @pl.when(lax.axis_index("noise") == 0)
    def _():
        message[0, 0:FIELDS, 0:CELLS] = fresh_ref[1, :, 0, :]
        message[0, 0:FIELDS, CELLS:] = later_ref[...].astype(F32)[0:FIELDS]

    lane = iota((ROWS, 128), 1)
    for f in range(FR_DEV):
        near_out[f] = message[f, :, 0:CELLS].astype(BF)
    for pair in range(2):
        near_out[FR_DEV, :, pair * 128 : pair * 128 + 128] = jnp.where(
            lane < 64,
            message[2 * pair, :, CELLS:],
            pltpu.roll(message[2 * pair + 1, :, CELLS:], 64, 1),
        ).astype(BF)
    far_out[...] = message[0].astype(BF)


def second_own_states(own_ref, states):
    for p in OWN:
        states[p] = own_ref[p + 1]


def second_own_kernel(
    near_ref, plan_ref, level_ref, own_ref, taps_ref, lift_ref, qkv_ref,
    hidden_out, qkv_out, states, sigmas, *scratch,
):
    own_sigmas(plan_ref, level_ref, sigmas)
    second_own_states(own_ref, states)
    own_frames(
        CELLS, near_ref, (taps_ref, lift_ref, qkv_ref), states, sigmas, (*scratch, None),
        hidden_out, qkv_out,
    )


def second_kernel(
    near_ref, plan_ref, level_ref, own_ref, came_ref, far_ref, hidden_own, qkv_own,
    taps_ref, lift_ref, qkv_ref, attend_ref, decode_ref,
    out_ref, states, sigmas, scaled, images, hidden_all, qkv_all, context_all, arrived,
):
    own_sigmas(plan_ref, level_ref, sigmas)
    next_sigmas(came_ref, sigmas)
    second_own_states(own_ref, states)
    for f in range(FR_DEV):
        states[FR_DEV - 1 + f, :, 0:CELLS] = came_ref[f].astype(F32)
        pair = came_ref[FR_DEV, :, (f // 2) * 128 : (f // 2 + 1) * 128].astype(F32)
        states[FR_DEV - 1 + f, :, CELLS:] = pltpu.roll(pair, 64, 1) if f % 2 else pair
    states[2 * FR_DEV - 1] = far_ref[...].astype(F32)
    scale_entering(states, sigmas)

    def finished(p, moved):
        for half in range(2):
            out_ref[pl.ds(p * 2 * FIELDS + half, FIELDS, stride=2), :] = moved[
                0:FIELDS, half * 128 : half * 128 + 128
            ]

    denoise(
        CELLS, near_ref, plan_ref, level_ref,
        (taps_ref, lift_ref, qkv_ref, attend_ref, decode_ref),
        states, sigmas, (scaled, images, None), hidden_own, qkv_own,
        hidden_all, qkv_all, context_all, arrived, finished,
    )


def window_scratch(lanes, frames):
    found = [
        pltpu.VMEM((frames, ROWS, CELLS + 128), F32),
        pltpu.VMEM((frames, 1, 128), F32),
        pltpu.VMEM((frames, ROWS, CELLS + 128), F32),
        pltpu.VMEM((frames, ROWS, 4 * CELLS), F32),
    ]
    if lanes > CELLS:
        found.append(pltpu.VMEM((frames, ROWS, 5 * 128), F32))
    return found


def attention_scratch(lanes):
    return [
        pltpu.VMEM((FR_DEV, WIDTH, lanes), F32),
        pltpu.VMEM((2 * FR_DEV, 3 * HEAD, HEADS, lanes), F32),
        pltpu.VMEM((FR_DEV, HEAD, HEADS, lanes), F32),
        pltpu.SemaphoreType.DMA((2,)),
    ]


def own_call(kernel, lanes, *operands):
    return pl.pallas_call(
        kernel,
        out_shape=(
            pltpu.VMEM((len(OWN), WIDTH, lanes), F32),
            pltpu.VMEM((len(OWN), 3 * HEAD, HEADS, lanes), F32),
        ),
        in_specs=[SMEM] * 3 + [VMEM] * (len(operands) - 3),
        out_specs=(VMEM, VMEM),
        scratch_shapes=window_scratch(lanes, FR_DEV),
        compiler_params=pltpu.CompilerParams(vmem_limit_bytes=40 << 20),
    )(*operands)


def shards(
    queue_state, fresh_noise, plan, levels, neighbours, in_weight, level_embed, conv_weight,
    norm_gain, query_weight, memory_weight, attend_out, decode_weight,
):
    groups = lax.axis_size("noise")
    from_next = [((i + 1) % groups, i) for i in range(groups)]
    from_second = [((i + 2) % groups, i) for i in range(groups)]
    near = far_from_core(neighbours.T)
    plan = far_from_core(plan)
    levels = far_from_core(levels)
    fresh_noise = far_from_core(fresh_noise)
    queue = far_from_core(queue_state.reshape(FR_DEV * FIELDS * 2, 128))
    frames, front, slots, after = border_lines(near, plan, levels, queue, fresh_noise)
    next_frames = near_core(lax.ppermute(frames, "noise", from_next))
    slots = near_core(lax.all_to_all(slots, TILE_AXES, split_axis=0, concat_axis=0, tiled=True))
    far = lax.ppermute(front, "noise", from_second)
    weights = prepare_weights(
        in_weight, level_embed, conv_weight, norm_gain, query_weight, memory_weight,
        attend_out, decode_weight, after,
    )
    far = near_core(far)
    halos, front_halo, later = halo_cells(near, slots, weights[1])
    next_halos = near_core(lax.ppermute(halos, "noise", from_next))
    far_halo = near_core(lax.ppermute(front_halo, "noise", from_second))
    both = (pl.BlockSpec(memory_space=pl.ANY),) * 2
    lanes = CELLS + 128
    own_part = own_call(first_own_kernel, lanes, near, plan, levels, queue, halos, *weights[:3])
    own, near_message, far_message = pl.pallas_call(
        first_kernel,
        out_shape=(
            jax.ShapeDtypeStruct((FR_DEV, ROWS, lanes), F32),
            jax.ShapeDtypeStruct((FR_DEV + 1, ROWS, CELLS), BF),
            jax.ShapeDtypeStruct((ROWS, lanes), BF),
        ),
        in_specs=[*([SMEM] * 3 + [VMEM] * 8), *both, *([VMEM] * 5)],
        out_specs=(VMEM,) * 3,
        scratch_shapes=[
            *window_scratch(lanes, 2 * FR_DEV),
            *attention_scratch(lanes),
            pltpu.VMEM((FR_DEV, ROWS, lanes), F32),
        ],
        compiler_params=pltpu.CompilerParams(vmem_limit_bytes=40 << 20),
        name="first",
    )(
        near, plan, levels, queue, fresh_noise, halos, later, next_frames, next_halos, far,
        far_halo, *own_part, *weights,
    )
    came = near_core(lax.ppermute(near_message, "noise", from_next))
    far = near_core(lax.ppermute(far_message, "noise", from_second))
    own_part = own_call(second_own_kernel, CELLS, near, plan, levels, own, *weights[:3])
    moved = pl.pallas_call(
        second_kernel,
        out_shape=jax.ShapeDtypeStruct((FR_DEV * FIELDS * 2, 128), F32),
        in_specs=[*([SMEM] * 3 + [VMEM] * 3), *both, *([VMEM] * 5)],
        out_specs=VMEM,
        scratch_shapes=[*window_scratch(CELLS, 2 * FR_DEV), *attention_scratch(CELLS)],
        compiler_params=pltpu.CompilerParams(vmem_limit_bytes=40 << 20),
        name="second",
    )(near, plan, levels, own, came, far, *own_part, *weights)
    return moved.reshape(queue_state.shape)


def solution(mesh):
    split = Mesh(
        mesh.devices.reshape(mesh.shape["noise"], 2, 4, 2), ("noise", "tile_0", "tile_1", "tile_2")
    )
    placed = (
        P("noise", None, TILE_AXES, None),
        P(None, None, TILE_AXES, None),
        P(),
        P("noise"),
        P(),
        P(),
        P(),
        P(),
        P(),
        P(),
        P(),
        P(),
        P(),
    )
    return jax.shard_map(
        shards,
        mesh=split,
        in_specs=placed,
        out_specs=P("noise", None, TILE_AXES, None),
        check_vma=False,
    )
```

```python
import jax
import jax.numpy as jnp
from jax import lax
from jax.experimental import pallas as pl
from jax.experimental.pallas import tpu as pltpu
from jax.sharding import Mesh
from jax.sharding import PartitionSpec as P

FIELDS = 69
ROWS = 72
WIDTH = 256
HEADS = 8
HEAD = WIDTH // HEADS
TILE = 16
CELLS = TILE * TILE
TAPS = 9
SLOT = 80
FR_DEV = 4
NTILES = 16
TILE_AXES = ("tile_0", "tile_1", "tile_2")
BF = jnp.bfloat16
F32 = jnp.float32

VMEM = pl.BlockSpec(memory_space=pltpu.VMEM)
SMEM = pl.BlockSpec(memory_space=pltpu.SMEM)


def near_core(array):
    return pltpu.with_memory_space_constraint(array, pltpu.VMEM)


def far_from_core(array):
    return pltpu.with_memory_space_constraint(array, pltpu.HBM)


def iota(shape, dim):
    return lax.broadcasted_iota(jnp.int32, shape, dim)


def mm(a, b):
    return jnp.dot(a, b, preferred_element_type=F32)


def mm_nt(a, b):
    return lax.dot_general(a, b, (((1,), (1,)), ((), ())), preferred_element_type=F32)


def split_hi_lo(v):
    hi = v.astype(BF).astype(F32)
    return hi, v - hi


def weights_kernel(
    in_ref, embed_ref, conv_ref, gain_ref, query_ref, memory_ref, out_ref, decode_ref, after_ref,
    taps_out, lift_out, qkv_out, attend_out, decode_out, folded,
):
    rows = iota((ROWS, WIDTH), 0)
    unit = (iota((ROWS, FIELDS), 0) == iota((ROWS, FIELDS), 1)).astype(BF)
    lift_t = mm(unit, in_ref[...])
    embed = jnp.broadcast_to(embed_ref[...], (ROWS, WIDTH))
    embed_hi, embed_lo = split_hi_lo(embed)
    stacked = jnp.where(
        rows == FIELDS, embed_hi, jnp.where(rows == FIELDS + 1, embed_lo, lift_t)
    ).astype(BF)
    lift_rows = jnp.where(
        rows >= FIELDS, jnp.where(rows == FIELDS + 2, embed_lo, embed_hi), lift_t
    )
    lift_out[...] = jnp.transpose(lift_rows).astype(BF)
    for tap in range(TAPS):
        both = mm_nt(stacked, conv_ref[tap])
        whole = jnp.broadcast_to(
            both[FIELDS : FIELDS + 1] + both[FIELDS + 1 : FIELDS + 2], (ROWS, WIDTH)
        )
        hi, lo = split_hi_lo(whole)
        folded[pl.ds(tap * ROWS, ROWS), :] = jnp.where(
            rows >= FIELDS, jnp.where(rows == FIELDS + 2, lo, hi), both
        )
    taps_out[...] = jnp.transpose(folded[...]).astype(BF)
    place = iota((WIDTH, WIDTH), 0)
    order = ((place % HEADS) * HEAD + place // HEADS == iota((WIDTH, WIDTH), 1)).astype(BF)
    gain = gain_ref[...]
    qkv_out[0:WIDTH, :] = (mm(order, query_ref[...]) * gain).astype(BF)
    for part in range(2):
        qkv_out[pl.ds((part + 1) * WIDTH, WIDTH), :] = (
            mm(order, memory_ref[pl.ds(part * WIDTH, WIDTH), :]) * gain
        ).astype(BF)
    attend_out[...] = mm_nt(out_ref[...], order).astype(BF)
    decode_out[...] = mm(unit, decode_ref[...]).astype(BF)


def prepare_weights(in_weight, embed, conv, gain, query, memory, attend, decode, after):
    return pl.pallas_call(
        weights_kernel,
        out_shape=(
            pltpu.VMEM((WIDTH, TAPS * ROWS), BF),
            pltpu.VMEM((WIDTH, ROWS), BF),
            pltpu.VMEM((3 * WIDTH, WIDTH), BF),
            pltpu.VMEM((WIDTH, WIDTH), BF),
            pltpu.VMEM((ROWS, WIDTH), BF),
        ),
        in_specs=[VMEM] * 8 + [SMEM],
        out_specs=(VMEM,) * 5,
        scratch_shapes=[pltpu.VMEM((TAPS * ROWS, WIDTH), F32)],
        compiler_params=pltpu.CompilerParams(vmem_limit_bytes=40 << 20),
        name="weights",
    )(
        *map(
            far_from_core,
            (
                in_weight.T, embed.reshape(1, WIDTH), conv, gain.reshape(1, WIDTH), query, memory,
                attend, decode,
            ),
        ),
        after,
    )


def frame_rows(queue_ref, frame):
    halves = [
        queue_ref[pl.ds(frame * 2 * FIELDS + half, FIELDS, stride=2), :] for half in range(2)
    ]
    return jnp.concatenate(halves, axis=1)


def sigma_rows(sigma, lanes):
    rows = iota((8, lanes), 0)
    first, rest = split_hi_lo(jnp.broadcast_to(sigma, (8, lanes)))
    second, third = split_hi_lo(rest)
    return jnp.where(rows == 5, first, jnp.where(rows == 6, second, third))


def border_kernel(
    near_ref, plan_ref, level_ref, queue_ref, fresh_ref,
    frames_out, front_out, slots_out, after_out, full, folded, later, lines,
):
    me = lax.axis_index(TILE_AXES)
    after_out[0] = 0
    for f in range(FR_DEV):
        sigma = jnp.full((8, CELLS), plan_ref[level_ref[f]], F32)
        full[pl.ds(f * ROWS + 64, 8), :] = sigma_rows(sigma, CELLS)
        full[pl.ds(f * ROWS, FIELDS), :] = frame_rows(queue_ref, f)
    full[pl.ds(FR_DEV * ROWS + 64, 8), :] = jnp.zeros((8, CELLS), F32)
    full[pl.ds(FR_DEV * ROWS, FIELDS), :] = fresh_ref[1, :, 0, :]

    @pl.when(lax.axis_index("noise") == 0)
    def _():
        full[0:FIELDS, :] = fresh_ref[0, :, 0, :]

    frames = full[...].astype(BF)
    for f in range(FR_DEV):
        frames_out[f] = full[pl.ds(f * ROWS, ROWS), :].astype(BF)
    front_out[...] = full[0:ROWS, :].astype(BF)
    cell = iota((CELLS, 128), 0)
    want = iota((CELLS, 128), 1)
    line = want // (2 * TILE)
    depth = want % (2 * TILE) // TILE
    along = want % TILE
    source = jnp.where(
        line == 0,
        along * TILE + TILE - 1 - depth,
        jnp.where(
            line == 1,
            along * TILE + depth,
            jnp.where(line == 2, (TILE - 1 - depth) * TILE + along, depth * TILE + along),
        ),
    )
    found = mm(frames, (cell == source).astype(BF))
    later[...] = found[FR_DEV * ROWS :]
    lane = iota((ROWS, 128), 1)
    lane9 = iota((9, 128), 1)
    folded[ROWS:SLOT, :] = jnp.zeros((SLOT - ROWS, 128), F32)
    for r in range(4):
        packed = jnp.zeros((ROWS, 128), F32)
        for f in range(FR_DEV):
            one = found[f * ROWS : (f + 1) * ROWS]
            turn = (2 * TILE * (f - r)) % 128
            if turn:
                one = pltpu.roll(one, turn, 1)
            packed = jnp.where(lane // (2 * TILE) == f, one, packed)
        folded[0:ROWS, :] = packed
        packed = jnp.zeros((9, 128), F32)
        for k in range(8):
            one = later[pl.ds(9 * k, 9), :]
            turn = (TILE * k - 2 * TILE * r) % 128
            if turn:
                one = pltpu.roll(one, turn, 1)
            packed = jnp.where(lane9 // TILE == k, one, packed)
        folded[FIELDS : FIELDS + 9, :] = packed
        lines[r] = folded[...].astype(BF)
    for j in range(NTILES):
        north = near_ref[2, j]
        beside = jnp.maximum(north, near_ref[3, j])
        from_west = jnp.logical_or(near_ref[0, j] == me, near_ref[0, beside] == me)
        from_east = jnp.logical_or(near_ref[1, j] == me, near_ref[1, beside] == me)
        vertical = jnp.where(north >= 0, 2, 3)
        code = jnp.where(from_west, 0, jnp.where(from_east, 1, vertical))
        slots_out[j] = lines[code]


def border_lines(near, plan, levels, queue, fresh):
    return pl.pallas_call(
        border_kernel,
        out_shape=(
            jax.ShapeDtypeStruct((FR_DEV, ROWS, CELLS), BF),
            jax.ShapeDtypeStruct((ROWS, CELLS), BF),
            jax.ShapeDtypeStruct((NTILES, SLOT, 128), BF),
            jax.ShapeDtypeStruct((1,), jnp.int32),
        ),
        in_specs=[SMEM, SMEM, SMEM, VMEM, VMEM],
        out_specs=(VMEM, VMEM, VMEM, SMEM),
        scratch_shapes=[
            pltpu.VMEM(((FR_DEV + 1) * ROWS, CELLS), F32),
            pltpu.VMEM((SLOT, 128), F32),
            pltpu.VMEM((ROWS, 128), F32),
            pltpu.VMEM((4, SLOT, 128), BF),
        ],
        compiler_params=pltpu.CompilerParams(vmem_limit_bytes=40 << 20),
        name="border",
    )(near, plan, levels, queue, fresh)


def halo_lane(row, column, near_row, far_row):
    west = jnp.where(column == -1, row, 64 + row)
    east = jnp.where(column == TILE, TILE + row, 80 + row)
    sides = jnp.where(column < 0, west, east)
    near_line = jnp.where(
        column == -1,
        48,
        jnp.where(column == TILE, 49, jnp.where(column < 0, 112, jnp.where(column > TILE, 115, 32 + column))),
    )
    far_line = jnp.where(
        column == -1,
        113,
        jnp.where(column == TILE, 116, jnp.where(column < 0, 114, jnp.where(column > TILE, 117, 96 + column))),
    )
    inside = jnp.logical_and(row >= 0, row < TILE)
    return jnp.where(
        inside,
        sides,
        jnp.where(row == near_row, near_line, jnp.where(row == far_row, far_line, -1)),
    )


def ring_kernel(near_ref, slots_ref, wait_ref, halo_out, front_out, later_out, picked, spare):
    me = lax.axis_index(TILE_AXES)
    north = near_ref[2, me]
    beside = jnp.maximum(north, near_ref[3, me])
    picked[:, 0:128] = slots_ref[near_ref[0, me]].astype(F32)
    picked[:, 128:256] = slots_ref[near_ref[1, me]].astype(F32)
    picked[:, 256:384] = slots_ref[beside].astype(F32)
    picked[:, 384:512] = slots_ref[near_ref[0, beside]].astype(F32)
    picked[:, 512:640] = slots_ref[near_ref[1, beside]].astype(F32)
    low = picked[...].astype(BF)
    is_north = (north >= 0).astype(jnp.int32)
    near_place = is_north * (TILE - 1)
    far_place = is_north * (TILE - 2) + (1 - is_north)

    def source(lane):
        block = lane // TILE
        along = lane % TILE
        side = jnp.where(block < 3, block, block - 4)
        deep = (lane >= 64).astype(jnp.int32)
        corner = jnp.logical_or(block == 3, block == 7)
        east_corner = jnp.where(block == 3, along, (along >= 3).astype(jnp.int32))
        which = jnp.where(block == 3, 0, 1 + along % 3)
        corner_deep = jnp.logical_or(which == 1, which == 3).astype(jnp.int32)
        corner_place = jnp.where(which >= 2, far_place, near_place)
        known = along < jnp.where(block == 3, 2, 6)
        plain = side * 128 + deep * TILE + along
        ends = (3 + east_corner) * 128 + corner_deep * TILE + corner_place
        lost = jnp.logical_and(corner, jnp.logical_not(known))
        later = jnp.where(corner, (3 + east_corner) * 128 + corner_place, side * 128 + along)
        return (
            jnp.where(lost, -10000, jnp.where(corner, ends, plain)),
            jnp.where(lost, -10000, later),
        )

    column = iota((8, FR_DEV * 128), 1)
    spot = source(column % 128)[0] + 2 * TILE * (column // 128)
    pick = (iota((5 * 128, FR_DEV * 128), 0) == spot[0:1]).astype(BF)
    halos = mm(low[0:ROWS], pick)
    for f in range(FR_DEV):
        halo_out[f] = halos[:, f * 128 : (f + 1) * 128].astype(BF)
    front_out[...] = halos[:, 0:128].astype(BF)
    column = iota((8, 8 * 64), 1)
    spot = source(column % 64)[1] + TILE * (column // 64)
    pick = (iota((5 * 128, 8 * 64), 0) == spot[0:1]).astype(BF)
    spare[...] = jnp.zeros_like(spare)
    blocks = mm(picked[64:SLOT].astype(BF), pick)
    for k in range(8):
        one = blocks[5:14, (k // 2) * 128 : (k // 2 + 1) * 128]
        spare[pl.ds(9 * k, 9), :] = pltpu.roll(one, 64, 1) if k % 2 else one
    later_out[...] = spare[...].astype(BF)


def halo_cells(near, slots, wait):
    return pl.pallas_call(
        ring_kernel,
        out_shape=(
            jax.ShapeDtypeStruct((FR_DEV, ROWS, 128), BF),
            jax.ShapeDtypeStruct((ROWS, 128), BF),
            jax.ShapeDtypeStruct((ROWS, 128), BF),
        ),
        in_specs=[SMEM, VMEM, pl.BlockSpec(memory_space=pl.ANY)],
        out_specs=(VMEM,) * 3,
        scratch_shapes=[pltpu.VMEM((SLOT, 5 * 128), F32), pltpu.VMEM((ROWS, 128), F32)],
        compiler_params=pltpu.CompilerParams(vmem_limit_bytes=40 << 20),
        name="ring",
    )(near, slots, wait)


def with_log_rows(scaled, log_hi, log_lo, lanes):
    rows = iota((ROWS, lanes), 0)
    return jnp.where(
        rows >= FIELDS, jnp.where(rows == FIELDS + 1, log_lo, log_hi), scaled
    )


def wide(row, lanes):
    return jnp.concatenate([row] * (lanes // 128), axis=1)


def features_of(
    frames, lanes, near_ref, taps_ref, lift_ref, states, sigmas, scaled, images, ring_windows
):
    me = lax.axis_index(TILE_AXES)
    at_north = near_ref[2, me] >= 0
    north_here = at_north.astype(F32)
    south_here = 1.0 - north_here
    extended = lanes > CELLS
    count = len(frames)
    begin = frames[0]
    total = CELLS + 128

    for p in frames:
        sigma = sigmas[p]
        log_hi, log_lo = split_hi_lo(jnp.log(sigma))
        scale = 1.0 / jnp.sqrt(sigma * sigma + 1.0)
        scaled[p] = with_log_rows(
            states[p] * wide(scale, total), wide(log_hi, total), wide(log_lo, total), total
        )
    ring_row = iota((128, 4 * CELLS), 0)
    column = iota((8, 4 * CELLS), 1)
    shift = column // CELLS - 2
    cell_x = column % TILE
    cell_y = (column % CELLS) // TILE
    line_x = cell_x + shift
    from_line = jnp.where(
        line_x < 0, 3 * TILE, jnp.where(line_x >= TILE, 3 * TILE + 1, 2 * TILE + line_x)
    )
    from_side = jnp.where(cell_x == 0, cell_y, TILE + cell_y)
    spot = jnp.where(column < CELLS, from_side, from_line)
    spread = (ring_row == spot[0:1]).astype(BF)
    low = scaled[begin : begin + count].reshape(count * ROWS, total).astype(BF)
    images[begin : begin + count] = mm(low[:, CELLS:], spread).reshape(count, ROWS, 4 * CELLS)
    if extended:
        near_row = jnp.where(at_north, -1, TILE)
        far_row = jnp.where(at_north, -2, TILE + 1)
        column = iota((8, 5 * 128), 1)
        tap = column // 64
        cell = column % 64
        block = cell // TILE
        along = cell % TILE
        row = jnp.where(block < 2, along, near_row) + tap // 3 - 1
        col = jnp.where(
            block == 0,
            -1,
            jnp.where(block == 1, TILE, jnp.where(block == 2, along, jnp.where(along == 0, -1, TILE))),
        )
        col = col + tap % 3 - 1
        in_tile = jnp.logical_and(
            jnp.logical_and(row >= 0, row < TILE), jnp.logical_and(col >= 0, col < TILE)
        )
        halo = halo_lane(row, col, near_row, far_row)
        spot = jnp.where(
            in_tile, row * TILE + col, jnp.where(halo >= 0, CELLS + halo, -1)
        )
        spot = jnp.where(cell < 50, spot, -1)
        pick = (iota((CELLS + 128, 5 * 128), 0) == spot[0:1]).astype(BF)
        ring_windows[begin : begin + count] = mm(low, pick).reshape(count, ROWS, 5 * 128)

    across = iota((ROWS, CELLS), 1) % TILE
    down = iota((ROWS, CELLS), 1) // TILE

    def features(p):
        inner = scaled[p, :, 0:CELLS].astype(BF).astype(F32)
        sides = images[p, :, 0:CELLS]
        shifted = (
            jnp.where(across == 0, sides, pltpu.roll(inner, 1, 1)),
            inner,
            jnp.where(across == TILE - 1, sides, pltpu.roll(inner, CELLS - 1, 1)),
        )
        up = []
        low = []
        for b in range(3):
            line = images[p, :, (b + 1) * CELLS : (b + 2) * CELLS]
            up.append(jnp.where(down == 0, line * north_here, pltpu.roll(shifted[b], TILE, 1)))
            low.append(
                jnp.where(
                    down == TILE - 1, line * south_here, pltpu.roll(shifted[b], CELLS - TILE, 1)
                )
            )
        windows = jnp.concatenate([*up, *shifted, *low], axis=0)
        if extended:
            beyond = []
            for tap in range(TAPS):
                one = ring_windows[p, :, (tap // 2) * 128 : (tap // 2 + 1) * 128]
                beyond.append(pltpu.roll(one, 64, 1) if tap % 2 else one)
            windows = jnp.concatenate([windows, jnp.concatenate(beyond, axis=0)], axis=1)
        convolved = mm(taps_ref[...], windows.astype(BF))
        lifted = mm(lift_ref[...], scaled[p, :, 0:lanes].astype(BF))
        hidden = lifted + convolved / (1.0 + jnp.exp(-convolved))
        power = jnp.mean(hidden * hidden, axis=0, keepdims=True)
        return hidden, (hidden * lax.rsqrt(power + 1e-06)).astype(BF)

    return features


OWN = range(FR_DEV - 1)
REST = range(FR_DEV - 1, 2 * FR_DEV)


def own_frames(lanes, near_ref, weights, states, sigmas, scratch, hidden_out, qkv_out):
    taps_ref, lift_ref, qkv_ref = weights
    features = features_of(OWN, lanes, near_ref, taps_ref, lift_ref, states, sigmas, *scratch)
    for p in OWN:
        hidden, normed = features(p)
        hidden_out[p] = hidden
        qkv_out[p] = mm(qkv_ref[...], normed).reshape(3 * HEAD, HEADS, lanes)


def denoise(
    lanes, near_ref, plan_ref, level_ref, weights, states, sigmas, scratch,
    hidden_own, qkv_own, hidden_all, qkv_all, context_all, arrived, finished,
):
    taps_ref, lift_ref, qkv_ref, attend_ref, decode_ref = weights
    is_last = lax.axis_index("noise") == lax.axis_size("noise") - 1
    held = len(OWN)
    copies = (
        pltpu.make_async_copy(qkv_own, qkv_all.at[pl.ds(0, held)], arrived.at[0]),
        pltpu.make_async_copy(hidden_own, hidden_all.at[pl.ds(0, held)], arrived.at[1]),
    )
    for copy in copies:
        copy.start()
    features = features_of(REST, lanes, near_ref, taps_ref, lift_ref, states, sigmas, *scratch)
    for p in REST:
        hidden, normed = features(p)
        if p < FR_DEV:
            hidden_all[p] = hidden
            qkv_all[p] = mm(qkv_ref[...], normed).reshape(3 * HEAD, HEADS, lanes)
        else:
            qkv_all[p, HEAD : 3 * HEAD] = mm(qkv_ref[WIDTH : 3 * WIDTH, :], normed).reshape(
                2 * HEAD, HEADS, lanes
            )
    for copy in copies:
        copy.wait()

    hide = jnp.where(is_last, -jnp.inf, 0.0)
    for part in range(lanes // 128):
        at = slice(part * 128, part * 128 + 128)

        zero = jnp.zeros((2 * FR_DEV, HEADS, 128), F32)
        sums = []
        for pair in range(0, FR_DEV, 2):

            def score(d, so_far, pair=pair):
                keys = qkv_all[:, HEAD + d, :, at]
                return tuple(
                    so_far[i] + qkv_all[pair + i, d, :, at][None] * keys for i in range(2)
                )

            sums.extend(lax.fori_loop(0, HEAD, score, (zero,) * 2, unroll=HEAD))
        second_half = iota((2 * FR_DEV, HEADS, 128), 0) >= FR_DEV
        weights = []
        for i in range(FR_DEV):
            scores = sums[i] * HEAD ** (-0.5) + jnp.where(second_half, hide, 0.0)
            top = jnp.max(scores, axis=0, keepdims=True)
            raised = jnp.exp(scores - top)
            weights.append(raised / jnp.sum(raised, axis=0, keepdims=True))

        def combine(d, carry):
            values = qkv_all[:, 2 * HEAD + d, :, at]
            for i in range(FR_DEV):
                context_all[i, d, :, at] = jnp.sum(weights[i] * values, axis=0)
            return carry

        lax.fori_loop(0, HEAD, combine, 0, unroll=HEAD)

    for p in range(FR_DEV):
        context = context_all[p].reshape(WIDTH, lanes).astype(BF)
        refined = (hidden_all[p] + mm(attend_ref[...], context)).astype(BF)
        projected = mm(decode_ref[...], refined)
        sigma = wide(sigmas[p], lanes)
        sigma_next = jnp.full((1, lanes), plan_ref[level_ref[p] + 1], F32)
        spread_of = sigma * sigma + 1.0
        slope = (sigma_next - sigma) / sigma
        state = states[p, :, 0:lanes]
        denoised = state / spread_of + sigma / jnp.sqrt(spread_of) * projected
        finished(p, state + slope * (state - denoised))


def own_sigmas(plan_ref, level_ref, sigmas):
    for f in range(FR_DEV):
        sigmas[f] = jnp.full((1, 128), plan_ref[level_ref[f]], F32)


def next_sigmas(next_frames_ref, sigmas):
    for f in range(FR_DEV):
        came = next_frames_ref[f, 64:ROWS, 0:128].astype(F32)
        sigmas[FR_DEV + f] = came[5:6] + came[6:7] + came[7:8]


def scale_entering(states, sigmas):
    group = lax.axis_index("noise")
    groups = lax.axis_size("noise")
    for p, holder in ((FR_DEV - 1, groups - 1), (2 * FR_DEV - 1, groups - 2)):

        @pl.when(group == holder)
        def _(p=p):
            states[p] = states[p] * wide(sigmas[p], CELLS + 128)


def first_own_states(queue_ref, halo_ref, states):
    for p in OWN:
        states[p, 64:ROWS, 0:CELLS] = jnp.zeros((ROWS - 64, CELLS), F32)
        states[p, 0:FIELDS, 0:CELLS] = frame_rows(queue_ref, p + 1)
        states[p, :, CELLS:] = halo_ref[p + 1].astype(F32)


def first_own_kernel(
    near_ref, plan_ref, level_ref, queue_ref, halo_ref, taps_ref, lift_ref, qkv_ref,
    hidden_out, qkv_out, states, sigmas, *scratch,
):
    own_sigmas(plan_ref, level_ref, sigmas)
    first_own_states(queue_ref, halo_ref, states)
    own_frames(
        CELLS + 128, near_ref, (taps_ref, lift_ref, qkv_ref), states, sigmas, scratch,
        hidden_out, qkv_out,
    )


def first_kernel(
    near_ref, plan_ref, level_ref, queue_ref, fresh_ref, halo_ref, later_ref, next_frames_ref,
    next_halo_ref, far_ref, far_halo_ref, hidden_own, qkv_own,
    taps_ref, lift_ref, qkv_ref, attend_ref, decode_ref,
    own_out, near_out, far_out,
    states, sigmas, scaled, images, ring_windows, hidden_all, qkv_all, context_all, arrived, message,
):
    own_sigmas(plan_ref, level_ref, sigmas)
    next_sigmas(next_frames_ref, sigmas)
    first_own_states(queue_ref, halo_ref, states)
    for f in range(FR_DEV):
        states[FR_DEV - 1 + f, :, 0:CELLS] = next_frames_ref[f].astype(F32)
        states[FR_DEV - 1 + f, :, CELLS:] = next_halo_ref[f].astype(F32)
    states[2 * FR_DEV - 1, :, 0:CELLS] = far_ref[...].astype(F32)
    states[2 * FR_DEV - 1, :, CELLS:] = far_halo_ref[...].astype(F32)
    scale_entering(states, sigmas)

    def finished(p, moved):
        own_out[p] = moved
        message[p, 0:64] = moved[0:64]
        rows = iota((8, CELLS + 128), 0)
        message[p, 64:ROWS] = jnp.where(
            rows >= FIELDS - 64, sigma_rows(wide(sigmas[p], CELLS + 128), CELLS + 128), moved[64:ROWS]
        )

    denoise(
        CELLS + 128, near_ref, plan_ref, level_ref,
        (taps_ref, lift_ref, qkv_ref, attend_ref, decode_ref),
        states, sigmas, (scaled, images, ring_windows), hidden_own, qkv_own,
        hidden_all, qkv_all, context_all, arrived, finished,
    )

    @pl.when(lax.axis_index("noise") == 0)
    def _():
        message[0, 0:FIELDS, 0:CELLS] = fresh_ref[1, :, 0, :]
        message[0, 0:FIELDS, CELLS:] = later_ref[...].astype(F32)[0:FIELDS]

    lane = iota((ROWS, 128), 1)
    for f in range(FR_DEV):
        near_out[f] = message[f, :, 0:CELLS].astype(BF)
    for pair in range(2):
        near_out[FR_DEV, :, pair * 128 : pair * 128 + 128] = jnp.where(
            lane < 64,
            message[2 * pair, :, CELLS:],
            pltpu.roll(message[2 * pair + 1, :, CELLS:], 64, 1),
        ).astype(BF)
    far_out[...] = message[0].astype(BF)


def second_own_states(own_ref, states):
    for p in OWN:
        states[p] = own_ref[p + 1]


def second_own_kernel(
    near_ref, plan_ref, level_ref, own_ref, taps_ref, lift_ref, qkv_ref,
    hidden_out, qkv_out, states, sigmas, *scratch,
):
    own_sigmas(plan_ref, level_ref, sigmas)
    second_own_states(own_ref, states)
    own_frames(
        CELLS, near_ref, (taps_ref, lift_ref, qkv_ref), states, sigmas, (*scratch, None),
        hidden_out, qkv_out,
    )


def second_kernel(
    near_ref, plan_ref, level_ref, own_ref, came_ref, far_ref, hidden_own, qkv_own,
    taps_ref, lift_ref, qkv_ref, attend_ref, decode_ref,
    out_ref, states, sigmas, scaled, images, hidden_all, qkv_all, context_all, arrived,
):
    own_sigmas(plan_ref, level_ref, sigmas)
    next_sigmas(came_ref, sigmas)
    second_own_states(own_ref, states)
    for f in range(FR_DEV):
        states[FR_DEV - 1 + f, :, 0:CELLS] = came_ref[f].astype(F32)
        pair = came_ref[FR_DEV, :, (f // 2) * 128 : (f // 2 + 1) * 128].astype(F32)
        states[FR_DEV - 1 + f, :, CELLS:] = pltpu.roll(pair, 64, 1) if f % 2 else pair
    states[2 * FR_DEV - 1] = far_ref[...].astype(F32)
    scale_entering(states, sigmas)

    def finished(p, moved):
        for half in range(2):
            out_ref[pl.ds(p * 2 * FIELDS + half, FIELDS, stride=2), :] = moved[
                0:FIELDS, half * 128 : half * 128 + 128
            ]

    denoise(
        CELLS, near_ref, plan_ref, level_ref,
        (taps_ref, lift_ref, qkv_ref, attend_ref, decode_ref),
        states, sigmas, (scaled, images, None), hidden_own, qkv_own,
        hidden_all, qkv_all, context_all, arrived, finished,
    )


def window_scratch(lanes, frames):
    found = [
        pltpu.VMEM((frames, ROWS, CELLS + 128), F32),
        pltpu.VMEM((frames, 1, 128), F32),
        pltpu.VMEM((frames, ROWS, CELLS + 128), F32),
        pltpu.VMEM((frames, ROWS, 4 * CELLS), F32),
    ]
    if lanes > CELLS:
        found.append(pltpu.VMEM((frames, ROWS, 5 * 128), F32))
    return found


def attention_scratch(lanes):
    return [
        pltpu.VMEM((FR_DEV, WIDTH, lanes), F32),
        pltpu.VMEM((2 * FR_DEV, 3 * HEAD, HEADS, lanes), F32),
        pltpu.VMEM((FR_DEV, HEAD, HEADS, lanes), F32),
        pltpu.SemaphoreType.DMA((2,)),
    ]


def own_call(kernel, lanes, *operands):
    return pl.pallas_call(
        kernel,
        out_shape=(
            pltpu.VMEM((len(OWN), WIDTH, lanes), F32),
            pltpu.VMEM((len(OWN), 3 * HEAD, HEADS, lanes), F32),
        ),
        in_specs=[SMEM] * 3 + [VMEM] * (len(operands) - 3),
        out_specs=(VMEM, VMEM),
        scratch_shapes=window_scratch(lanes, FR_DEV),
        compiler_params=pltpu.CompilerParams(vmem_limit_bytes=40 << 20),
    )(*operands)


def shards(
    queue_state, fresh_noise, plan, levels, neighbours, in_weight, level_embed, conv_weight,
    norm_gain, query_weight, memory_weight, attend_out, decode_weight,
):
    groups = lax.axis_size("noise")
    from_next = [((i + 1) % groups, i) for i in range(groups)]
    from_second = [((i + 2) % groups, i) for i in range(groups)]
    near = far_from_core(neighbours.T)
    plan = far_from_core(plan)
    levels = far_from_core(levels)
    fresh_noise = far_from_core(fresh_noise)
    queue = far_from_core(queue_state.reshape(FR_DEV * FIELDS * 2, 128))
    frames, front, slots, after = border_lines(near, plan, levels, queue, fresh_noise)
    next_frames = near_core(lax.ppermute(frames, "noise", from_next))
    slots = near_core(lax.all_to_all(slots, TILE_AXES, split_axis=0, concat_axis=0, tiled=True))
    far = lax.ppermute(front, "noise", from_second)
    weights = prepare_weights(
        in_weight, level_embed, conv_weight, norm_gain, query_weight, memory_weight,
        attend_out, decode_weight, after,
    )
    far = near_core(far)
    halos, front_halo, later = halo_cells(near, slots, weights[1])
    next_halos = near_core(lax.ppermute(halos, "noise", from_next))
    far_halo = near_core(lax.ppermute(front_halo, "noise", from_second))
    both = (pl.BlockSpec(memory_space=pl.ANY),) * 2
    lanes = CELLS + 128
    own_part = own_call(first_own_kernel, lanes, near, plan, levels, queue, halos, *weights[:3])
    own, near_message, far_message = pl.pallas_call(
        first_kernel,
        out_shape=(
            jax.ShapeDtypeStruct((FR_DEV, ROWS, lanes), F32),
            jax.ShapeDtypeStruct((FR_DEV + 1, ROWS, CELLS), BF),
            jax.ShapeDtypeStruct((ROWS, lanes), BF),
        ),
        in_specs=[*([SMEM] * 3 + [VMEM] * 8), *both, *([VMEM] * 5)],
        out_specs=(VMEM,) * 3,
        scratch_shapes=[
            *window_scratch(lanes, 2 * FR_DEV),
            *attention_scratch(lanes),
            pltpu.VMEM((FR_DEV, ROWS, lanes), F32),
        ],
        compiler_params=pltpu.CompilerParams(vmem_limit_bytes=40 << 20),
        name="first",
    )(
        near, plan, levels, queue, fresh_noise, halos, later, next_frames, next_halos, far,
        far_halo, *own_part, *weights,
    )
    came = near_core(lax.ppermute(near_message, "noise", from_next))
    far = near_core(lax.ppermute(far_message, "noise", from_second))
    own_part = own_call(second_own_kernel, CELLS, near, plan, levels, own, *weights[:3])
    moved = pl.pallas_call(
        second_kernel,
        out_shape=jax.ShapeDtypeStruct((FR_DEV * FIELDS * 2, 128), F32),
        in_specs=[*([SMEM] * 3 + [VMEM] * 3), *both, *([VMEM] * 5)],
        out_specs=VMEM,
        scratch_shapes=[*window_scratch(CELLS, 2 * FR_DEV), *attention_scratch(CELLS)],
        compiler_params=pltpu.CompilerParams(vmem_limit_bytes=40 << 20),
        name="second",
    )(near, plan, levels, own, came, far, *own_part, *weights)
    return moved.reshape(queue_state.shape)


def solution(mesh):
    split = Mesh(
        mesh.devices.reshape(mesh.shape["noise"], 2, 4, 2), ("noise", "tile_0", "tile_1", "tile_2")
    )
    placed = (
        P("noise", None, TILE_AXES, None),
        P(None, None, TILE_AXES, None),
        P(),
        P("noise"),
        P(),
        P(),
        P(),
        P(),
        P(),
        P(),
        P(),
        P(),
        P(),
    )
    return jax.shard_map(
        shards,
        mesh=split,
        in_specs=placed,
        out_specs=P("noise", None, TILE_AXES, None),
        check_vma=False,
    )
```

```python
import jax
import jax.numpy as jnp
from jax import lax
from jax.experimental import pallas as pl
from jax.experimental.pallas import tpu as pltpu
from jax.sharding import Mesh
from jax.sharding import PartitionSpec as P

FIELDS = 69
ROWS = 72
WIDTH = 256
HEADS = 8
HEAD = WIDTH // HEADS
TILE = 16
CELLS = TILE * TILE
TAPS = 9
SLOT = 80
FR_DEV = 4
NTILES = 16
TILE_AXES = ("tile_0", "tile_1", "tile_2")
BF = jnp.bfloat16
F32 = jnp.float32

VMEM = pl.BlockSpec(memory_space=pltpu.VMEM)
SMEM = pl.BlockSpec(memory_space=pltpu.SMEM)


def near_core(array):
    return pltpu.with_memory_space_constraint(array, pltpu.VMEM)


def far_from_core(array):
    return pltpu.with_memory_space_constraint(array, pltpu.HBM)


def iota(shape, dim):
    return lax.broadcasted_iota(jnp.int32, shape, dim)


def mm(a, b):
    return jnp.dot(a, b, preferred_element_type=F32)


def mm_nt(a, b):
    return lax.dot_general(a, b, (((1,), (1,)), ((), ())), preferred_element_type=F32)


def split_hi_lo(v):
    hi = v.astype(BF).astype(F32)
    return hi, v - hi


def weights_kernel(
    in_ref, embed_ref, conv_ref, gain_ref, query_ref, memory_ref, out_ref, decode_ref, after_ref,
    taps_out, lift_out, qkv_out, attend_out, decode_out, folded,
):
    rows = iota((ROWS, WIDTH), 0)
    unit = (iota((ROWS, FIELDS), 0) == iota((ROWS, FIELDS), 1)).astype(BF)
    lift_t = mm(unit, in_ref[...])
    embed = jnp.broadcast_to(embed_ref[...], (ROWS, WIDTH))
    embed_hi, embed_lo = split_hi_lo(embed)
    stacked = jnp.where(
        rows == FIELDS, embed_hi, jnp.where(rows == FIELDS + 1, embed_lo, lift_t)
    ).astype(BF)
    lift_rows = jnp.where(
        rows >= FIELDS, jnp.where(rows == FIELDS + 2, embed_lo, embed_hi), lift_t
    )
    lift_out[...] = jnp.transpose(lift_rows).astype(BF)
    for tap in range(TAPS):
        both = mm_nt(stacked, conv_ref[tap])
        whole = jnp.broadcast_to(
            both[FIELDS : FIELDS + 1] + both[FIELDS + 1 : FIELDS + 2], (ROWS, WIDTH)
        )
        hi, lo = split_hi_lo(whole)
        folded[pl.ds(tap * ROWS, ROWS), :] = jnp.where(
            rows >= FIELDS, jnp.where(rows == FIELDS + 2, lo, hi), both
        )
    taps_out[...] = jnp.transpose(folded[...]).astype(BF)
    place = iota((WIDTH, WIDTH), 0)
    order = ((place % HEADS) * HEAD + place // HEADS == iota((WIDTH, WIDTH), 1)).astype(BF)
    gain = gain_ref[...]
    qkv_out[0:WIDTH, :] = (mm(order, query_ref[...]) * gain).astype(BF)
    for part in range(2):
        qkv_out[pl.ds((part + 1) * WIDTH, WIDTH), :] = (
            mm(order, memory_ref[pl.ds(part * WIDTH, WIDTH), :]) * gain
        ).astype(BF)
    attend_out[...] = mm_nt(out_ref[...], order).astype(BF)
    decode_out[...] = mm(unit, decode_ref[...]).astype(BF)


def prepare_weights(in_weight, embed, conv, gain, query, memory, attend, decode, after):
    return pl.pallas_call(
        weights_kernel,
        out_shape=(
            pltpu.VMEM((WIDTH, TAPS * ROWS), BF),
            pltpu.VMEM((WIDTH, ROWS), BF),
            pltpu.VMEM((3 * WIDTH, WIDTH), BF),
            pltpu.VMEM((WIDTH, WIDTH), BF),
            pltpu.VMEM((ROWS, WIDTH), BF),
        ),
        in_specs=[VMEM] * 8 + [SMEM],
        out_specs=(VMEM,) * 5,
        scratch_shapes=[pltpu.VMEM((TAPS * ROWS, WIDTH), F32)],
        compiler_params=pltpu.CompilerParams(vmem_limit_bytes=40 << 20),
        name="weights",
    )(
        *map(
            far_from_core,
            (
                in_weight.T, embed.reshape(1, WIDTH), conv, gain.reshape(1, WIDTH), query, memory,
                attend, decode,
            ),
        ),
        after,
    )


def frame_rows(queue_ref, frame):
    halves = [
        queue_ref[pl.ds(frame * 2 * FIELDS + half, FIELDS, stride=2), :] for half in range(2)
    ]
    return jnp.concatenate(halves, axis=1)


def sigma_rows(sigma, lanes):
    rows = iota((8, lanes), 0)
    first, rest = split_hi_lo(jnp.broadcast_to(sigma, (8, lanes)))
    second, third = split_hi_lo(rest)
    return jnp.where(rows == 5, first, jnp.where(rows == 6, second, third))


def border_kernel(
    near_ref, plan_ref, level_ref, queue_ref, fresh_ref,
    frames_out, front_out, slots_out, after_out, full, folded, later, lines,
):
    me = lax.axis_index(TILE_AXES)
    after_out[0] = 0
    for f in range(FR_DEV):
        sigma = jnp.full((8, CELLS), plan_ref[level_ref[f]], F32)
        full[pl.ds(f * ROWS + 64, 8), :] = sigma_rows(sigma, CELLS)
        full[pl.ds(f * ROWS, FIELDS), :] = frame_rows(queue_ref, f)
    full[pl.ds(FR_DEV * ROWS + 64, 8), :] = jnp.zeros((8, CELLS), F32)
    full[pl.ds(FR_DEV * ROWS, FIELDS), :] = fresh_ref[1, :, 0, :]

    @pl.when(lax.axis_index("noise") == 0)
    def _():
        full[0:FIELDS, :] = fresh_ref[0, :, 0, :]

    frames = full[...].astype(BF)
    for f in range(FR_DEV):
        frames_out[f] = full[pl.ds(f * ROWS, ROWS), :].astype(BF)
    front_out[...] = full[0:ROWS, :].astype(BF)
    cell = iota((CELLS, 128), 0)
    want = iota((CELLS, 128), 1)
    line = want // (2 * TILE)
    depth = want % (2 * TILE) // TILE
    along = want % TILE
    source = jnp.where(
        line == 0,
        along * TILE + TILE - 1 - depth,
        jnp.where(
            line == 1,
            along * TILE + depth,
            jnp.where(line == 2, (TILE - 1 - depth) * TILE + along, depth * TILE + along),
        ),
    )
    found = mm(frames, (cell == source).astype(BF))
    later[...] = found[FR_DEV * ROWS :]
    lane = iota((ROWS, 128), 1)
    lane9 = iota((9, 128), 1)
    folded[ROWS:SLOT, :] = jnp.zeros((SLOT - ROWS, 128), F32)
    for r in range(4):
        packed = jnp.zeros((ROWS, 128), F32)
        for f in range(FR_DEV):
            one = found[f * ROWS : (f + 1) * ROWS]
            turn = (2 * TILE * (f - r)) % 128
            if turn:
                one = pltpu.roll(one, turn, 1)
            packed = jnp.where(lane // (2 * TILE) == f, one, packed)
        folded[0:ROWS, :] = packed
        packed = jnp.zeros((9, 128), F32)
        for k in range(8):
            one = later[pl.ds(9 * k, 9), :]
            turn = (TILE * k - 2 * TILE * r) % 128
            if turn:
                one = pltpu.roll(one, turn, 1)
            packed = jnp.where(lane9 // TILE == k, one, packed)
        folded[FIELDS : FIELDS + 9, :] = packed
        lines[r] = folded[...].astype(BF)
    for j in range(NTILES):
        north = near_ref[2, j]
        beside = jnp.maximum(north, near_ref[3, j])
        from_west = jnp.logical_or(near_ref[0, j] == me, near_ref[0, beside] == me)
        from_east = jnp.logical_or(near_ref[1, j] == me, near_ref[1, beside] == me)
        vertical = jnp.where(north >= 0, 2, 3)
        code = jnp.where(from_west, 0, jnp.where(from_east, 1, vertical))
        slots_out[j] = lines[code]


def border_lines(near, plan, levels, queue, fresh):
    return pl.pallas_call(
        border_kernel,
        out_shape=(
            jax.ShapeDtypeStruct((FR_DEV, ROWS, CELLS), BF),
            jax.ShapeDtypeStruct((ROWS, CELLS), BF),
            jax.ShapeDtypeStruct((NTILES, SLOT, 128), BF),
            jax.ShapeDtypeStruct((1,), jnp.int32),
        ),
        in_specs=[SMEM, SMEM, SMEM, VMEM, VMEM],
        out_specs=(VMEM, VMEM, VMEM, SMEM),
        scratch_shapes=[
            pltpu.VMEM(((FR_DEV + 1) * ROWS, CELLS), F32),
            pltpu.VMEM((SLOT, 128), F32),
            pltpu.VMEM((ROWS, 128), F32),
            pltpu.VMEM((4, SLOT, 128), BF),
        ],
        compiler_params=pltpu.CompilerParams(vmem_limit_bytes=40 << 20),
        name="border",
    )(near, plan, levels, queue, fresh)


def halo_lane(row, column, near_row, far_row):
    west = jnp.where(column == -1, row, 64 + row)
    east = jnp.where(column == TILE, TILE + row, 80 + row)
    sides = jnp.where(column < 0, west, east)
    near_line = jnp.where(
        column == -1,
        48,
        jnp.where(column == TILE, 49, jnp.where(column < 0, 112, jnp.where(column > TILE, 115, 32 + column))),
    )
    far_line = jnp.where(
        column == -1,
        113,
        jnp.where(column == TILE, 116, jnp.where(column < 0, 114, jnp.where(column > TILE, 117, 96 + column))),
    )
    inside = jnp.logical_and(row >= 0, row < TILE)
    return jnp.where(
        inside,
        sides,
        jnp.where(row == near_row, near_line, jnp.where(row == far_row, far_line, -1)),
    )


def ring_kernel(near_ref, slots_ref, wait_ref, halo_out, front_out, later_out, picked, spare):
    me = lax.axis_index(TILE_AXES)
    north = near_ref[2, me]
    beside = jnp.maximum(north, near_ref[3, me])
    picked[:, 0:128] = slots_ref[near_ref[0, me]].astype(F32)
    picked[:, 128:256] = slots_ref[near_ref[1, me]].astype(F32)
    picked[:, 256:384] = slots_ref[beside].astype(F32)
    picked[:, 384:512] = slots_ref[near_ref[0, beside]].astype(F32)
    picked[:, 512:640] = slots_ref[near_ref[1, beside]].astype(F32)
    low = picked[...].astype(BF)
    is_north = (north >= 0).astype(jnp.int32)
    near_place = is_north * (TILE - 1)
    far_place = is_north * (TILE - 2) + (1 - is_north)

    def source(lane):
        block = lane // TILE
        along = lane % TILE
        side = jnp.where(block < 3, block, block - 4)
        deep = (lane >= 64).astype(jnp.int32)
        corner = jnp.logical_or(block == 3, block == 7)
        east_corner = jnp.where(block == 3, along, (along >= 3).astype(jnp.int32))
        which = jnp.where(block == 3, 0, 1 + along % 3)
        corner_deep = jnp.logical_or(which == 1, which == 3).astype(jnp.int32)
        corner_place = jnp.where(which >= 2, far_place, near_place)
        known = along < jnp.where(block == 3, 2, 6)
        plain = side * 128 + deep * TILE + along
        ends = (3 + east_corner) * 128 + corner_deep * TILE + corner_place
        lost = jnp.logical_and(corner, jnp.logical_not(known))
        later = jnp.where(corner, (3 + east_corner) * 128 + corner_place, side * 128 + along)
        return (
            jnp.where(lost, -10000, jnp.where(corner, ends, plain)),
            jnp.where(lost, -10000, later),
        )

    column = iota((8, FR_DEV * 128), 1)
    spot = source(column % 128)[0] + 2 * TILE * (column // 128)
    pick = (iota((5 * 128, FR_DEV * 128), 0) == spot[0:1]).astype(BF)
    halos = mm(low[0:ROWS], pick)
    for f in range(FR_DEV):
        halo_out[f] = halos[:, f * 128 : (f + 1) * 128].astype(BF)
    front_out[...] = halos[:, 0:128].astype(BF)
    column = iota((8, 8 * 64), 1)
    spot = source(column % 64)[1] + TILE * (column // 64)
    pick = (iota((5 * 128, 8 * 64), 0) == spot[0:1]).astype(BF)
    spare[...] = jnp.zeros_like(spare)
    blocks = mm(picked[64:SLOT].astype(BF), pick)
    for k in range(8):
        one = blocks[5:14, (k // 2) * 128 : (k // 2 + 1) * 128]
        spare[pl.ds(9 * k, 9), :] = pltpu.roll(one, 64, 1) if k % 2 else one
    later_out[...] = spare[...].astype(BF)


def halo_cells(near, slots, wait):
    return pl.pallas_call(
        ring_kernel,
        out_shape=(
            jax.ShapeDtypeStruct((FR_DEV, ROWS, 128), BF),
            jax.ShapeDtypeStruct((ROWS, 128), BF),
            jax.ShapeDtypeStruct((ROWS, 128), BF),
        ),
        in_specs=[SMEM, VMEM, pl.BlockSpec(memory_space=pl.ANY)],
        out_specs=(VMEM,) * 3,
        scratch_shapes=[pltpu.VMEM((SLOT, 5 * 128), F32), pltpu.VMEM((ROWS, 128), F32)],
        compiler_params=pltpu.CompilerParams(vmem_limit_bytes=40 << 20),
        name="ring",
    )(near, slots, wait)


def with_log_rows(scaled, log_hi, log_lo, lanes):
    rows = iota((ROWS, lanes), 0)
    return jnp.where(
        rows >= FIELDS, jnp.where(rows == FIELDS + 1, log_lo, log_hi), scaled
    )


def wide(row, lanes):
    return jnp.concatenate([row] * (lanes // 128), axis=1)


def features_of(
    frames, lanes, near_ref, taps_ref, lift_ref, states, sigmas, scaled, images, ring_windows
):
    me = lax.axis_index(TILE_AXES)
    at_north = near_ref[2, me] >= 0
    north_here = at_north.astype(F32)
    south_here = 1.0 - north_here
    extended = lanes > CELLS
    count = len(frames)
    begin = frames[0]
    total = CELLS + 128

    for p in frames:
        sigma = sigmas[p]
        log_hi, log_lo = split_hi_lo(jnp.log(sigma))
        scale = 1.0 / jnp.sqrt(sigma * sigma + 1.0)
        scaled[p] = with_log_rows(
            states[p] * wide(scale, total), wide(log_hi, total), wide(log_lo, total), total
        )
    ring_row = iota((128, 4 * CELLS), 0)
    column = iota((8, 4 * CELLS), 1)
    shift = column // CELLS - 2
    cell_x = column % TILE
    cell_y = (column % CELLS) // TILE
    line_x = cell_x + shift
    from_line = jnp.where(
        line_x < 0, 3 * TILE, jnp.where(line_x >= TILE, 3 * TILE + 1, 2 * TILE + line_x)
    )
    from_side = jnp.where(cell_x == 0, cell_y, TILE + cell_y)
    spot = jnp.where(column < CELLS, from_side, from_line)
    spread = (ring_row == spot[0:1]).astype(BF)
    low = scaled[begin : begin + count].reshape(count * ROWS, total).astype(BF)
    images[begin : begin + count] = mm(low[:, CELLS:], spread).reshape(count, ROWS, 4 * CELLS)
    if extended:
        near_row = jnp.where(at_north, -1, TILE)
        far_row = jnp.where(at_north, -2, TILE + 1)
        column = iota((8, 5 * 128), 1)
        tap = column // 64
        cell = column % 64
        block = cell // TILE
        along = cell % TILE
        row = jnp.where(block < 2, along, near_row) + tap // 3 - 1
        col = jnp.where(
            block == 0,
            -1,
            jnp.where(block == 1, TILE, jnp.where(block == 2, along, jnp.where(along == 0, -1, TILE))),
        )
        col = col + tap % 3 - 1
        in_tile = jnp.logical_and(
            jnp.logical_and(row >= 0, row < TILE), jnp.logical_and(col >= 0, col < TILE)
        )
        halo = halo_lane(row, col, near_row, far_row)
        spot = jnp.where(
            in_tile, row * TILE + col, jnp.where(halo >= 0, CELLS + halo, -1)
        )
        spot = jnp.where(cell < 50, spot, -1)
        pick = (iota((CELLS + 128, 5 * 128), 0) == spot[0:1]).astype(BF)
        ring_windows[begin : begin + count] = mm(low, pick).reshape(count, ROWS, 5 * 128)

    across = iota((ROWS, CELLS), 1) % TILE
    down = iota((ROWS, CELLS), 1) // TILE

    def features(p):
        inner = scaled[p, :, 0:CELLS].astype(BF).astype(F32)
        sides = images[p, :, 0:CELLS]
        shifted = (
            jnp.where(across == 0, sides, pltpu.roll(inner, 1, 1)),
            inner,
            jnp.where(across == TILE - 1, sides, pltpu.roll(inner, CELLS - 1, 1)),
        )
        up = []
        low = []
        for b in range(3):
            line = images[p, :, (b + 1) * CELLS : (b + 2) * CELLS]
            up.append(jnp.where(down == 0, line * north_here, pltpu.roll(shifted[b], TILE, 1)))
            low.append(
                jnp.where(
                    down == TILE - 1, line * south_here, pltpu.roll(shifted[b], CELLS - TILE, 1)
                )
            )
        windows = jnp.concatenate([*up, *shifted, *low], axis=0)
        if extended:
            beyond = []
            for tap in range(TAPS):
                one = ring_windows[p, :, (tap // 2) * 128 : (tap // 2 + 1) * 128]
                beyond.append(pltpu.roll(one, 64, 1) if tap % 2 else one)
            windows = jnp.concatenate([windows, jnp.concatenate(beyond, axis=0)], axis=1)
        convolved = mm(taps_ref[...], windows.astype(BF))
        lifted = mm(lift_ref[...], scaled[p, :, 0:lanes].astype(BF))
        hidden = lifted + convolved / (1.0 + jnp.exp(-convolved))
        power = jnp.mean(hidden * hidden, axis=0, keepdims=True)
        return hidden, (hidden * lax.rsqrt(power + 1e-06)).astype(BF)

    return features


OWN = range(FR_DEV - 1)
REST = range(FR_DEV - 1, 2 * FR_DEV)


def own_frames(lanes, near_ref, weights, states, sigmas, scratch, hidden_out, qkv_out):
    taps_ref, lift_ref, qkv_ref = weights
    features = features_of(OWN, lanes, near_ref, taps_ref, lift_ref, states, sigmas, *scratch)
    for p in OWN:
        hidden, normed = features(p)
        hidden_out[p] = hidden
        qkv_out[p] = mm(qkv_ref[...], normed).reshape(3 * HEAD, HEADS, lanes)


def denoise(
    lanes, near_ref, plan_ref, level_ref, weights, states, sigmas, scratch,
    hidden_own, qkv_own, hidden_all, qkv_all, context_all, finished,
):
    taps_ref, lift_ref, qkv_ref, attend_ref, decode_ref = weights
    is_last = lax.axis_index("noise") == lax.axis_size("noise") - 1
    held = len(OWN)
    features = features_of(REST, lanes, near_ref, taps_ref, lift_ref, states, sigmas, *scratch)
    for p in REST:
        hidden, normed = features(p)
        if p < FR_DEV:
            hidden_all[...] = hidden
            qkv_all[p - held] = mm(qkv_ref[...], normed).reshape(3 * HEAD, HEADS, lanes)
        else:
            qkv_all[p - held, HEAD : 3 * HEAD] = mm(qkv_ref[WIDTH : 3 * WIDTH, :], normed).reshape(
                2 * HEAD, HEADS, lanes
            )

    def every(row, at):
        return jnp.concatenate([qkv_own[:, row, :, at], qkv_all[:, row, :, at]], axis=0)

    def query(i, d, at):
        return qkv_own[i, d, :, at] if i < held else qkv_all[i - held, d, :, at]

    hide = jnp.where(is_last, -jnp.inf, 0.0)
    for part in range(lanes // 128):
        at = slice(part * 128, part * 128 + 128)

        zero = jnp.zeros((2 * FR_DEV, HEADS, 128), F32)
        sums = []
        for pair in range(0, FR_DEV, 2):

            def score(d, so_far, pair=pair):
                keys = every(HEAD + d, at)
                return tuple(
                    so_far[i] + query(pair + i, d, at)[None] * keys for i in range(2)
                )

            sums.extend(lax.fori_loop(0, HEAD, score, (zero,) * 2, unroll=HEAD))
        second_half = iota((2 * FR_DEV, HEADS, 128), 0) >= FR_DEV
        weights = []
        for i in range(FR_DEV):
            scores = sums[i] * HEAD ** (-0.5) + jnp.where(second_half, hide, 0.0)
            top = jnp.max(scores, axis=0, keepdims=True)
            raised = jnp.exp(scores - top)
            weights.append(raised * (1.0 / jnp.sum(raised, axis=0, keepdims=True)))

        def combine(d, carry):
            values = every(2 * HEAD + d, at)
            for i in range(FR_DEV):
                context_all[i, d, :, at] = jnp.sum(weights[i] * values, axis=0)
            return carry

        lax.fori_loop(0, HEAD, combine, 0, unroll=HEAD)

    for p in range(FR_DEV):
        context = context_all[p].reshape(WIDTH, lanes).astype(BF)
        hidden = hidden_own[p] if p < held else hidden_all[...]
        refined = (hidden + mm(attend_ref[...], context)).astype(BF)
        projected = mm(decode_ref[...], refined)
        sigma = wide(sigmas[p], lanes)
        sigma_next = jnp.full((1, lanes), plan_ref[level_ref[p] + 1], F32)
        spread_of = sigma * sigma + 1.0
        slope = (sigma_next - sigma) / sigma
        state = states[p, :, 0:lanes]
        denoised = state / spread_of + sigma / jnp.sqrt(spread_of) * projected
        finished(p, state + slope * (state - denoised))


def own_sigmas(plan_ref, level_ref, sigmas):
    for f in range(FR_DEV):
        sigmas[f] = jnp.full((1, 128), plan_ref[level_ref[f]], F32)


def next_sigmas(next_frames_ref, sigmas):
    for f in range(FR_DEV):
        came = next_frames_ref[f, 64:ROWS, 0:128].astype(F32)
        sigmas[FR_DEV + f] = came[5:6] + came[6:7] + came[7:8]


def scale_entering(states, sigmas):
    group = lax.axis_index("noise")
    groups = lax.axis_size("noise")
    for p, holder in ((FR_DEV - 1, groups - 1), (2 * FR_DEV - 1, groups - 2)):

        @pl.when(group == holder)
        def _(p=p):
            states[p] = states[p] * wide(sigmas[p], CELLS + 128)


def first_own_states(queue_ref, halo_ref, states):
    for p in OWN:
        states[p, 64:ROWS, 0:CELLS] = jnp.zeros((ROWS - 64, CELLS), F32)
        states[p, 0:FIELDS, 0:CELLS] = frame_rows(queue_ref, p + 1)
        states[p, :, CELLS:] = halo_ref[p + 1].astype(F32)


def first_own_kernel(
    near_ref, plan_ref, level_ref, queue_ref, halo_ref, taps_ref, lift_ref, qkv_ref,
    hidden_out, qkv_out, states, sigmas, *scratch,
):
    own_sigmas(plan_ref, level_ref, sigmas)
    first_own_states(queue_ref, halo_ref, states)
    own_frames(
        CELLS + 128, near_ref, (taps_ref, lift_ref, qkv_ref), states, sigmas, scratch,
        hidden_out, qkv_out,
    )


def first_kernel(
    near_ref, plan_ref, level_ref, queue_ref, fresh_ref, halo_ref, later_ref, next_frames_ref,
    next_halo_ref, far_ref, far_halo_ref, hidden_own, qkv_own,
    taps_ref, lift_ref, qkv_ref, attend_ref, decode_ref,
    own_out, near_out, far_out,
    states, sigmas, scaled, images, ring_windows, hidden_all, qkv_all, context_all, message,
):
    own_sigmas(plan_ref, level_ref, sigmas)
    next_sigmas(next_frames_ref, sigmas)
    first_own_states(queue_ref, halo_ref, states)
    for f in range(FR_DEV):
        states[FR_DEV - 1 + f, :, 0:CELLS] = next_frames_ref[f].astype(F32)
        states[FR_DEV - 1 + f, :, CELLS:] = next_halo_ref[f].astype(F32)
    states[2 * FR_DEV - 1, :, 0:CELLS] = far_ref[...].astype(F32)
    states[2 * FR_DEV - 1, :, CELLS:] = far_halo_ref[...].astype(F32)
    scale_entering(states, sigmas)

    def finished(p, moved):
        own_out[p] = moved
        message[p, 0:64] = moved[0:64]
        rows = iota((8, CELLS + 128), 0)
        message[p, 64:ROWS] = jnp.where(
            rows >= FIELDS - 64, sigma_rows(wide(sigmas[p], CELLS + 128), CELLS + 128), moved[64:ROWS]
        )

    denoise(
        CELLS + 128, near_ref, plan_ref, level_ref,
        (taps_ref, lift_ref, qkv_ref, attend_ref, decode_ref),
        states, sigmas, (scaled, images, ring_windows), hidden_own, qkv_own,
        hidden_all, qkv_all, context_all, finished,
    )

    @pl.when(lax.axis_index("noise") == 0)
    def _():
        message[0, 0:FIELDS, 0:CELLS] = fresh_ref[1, :, 0, :]
        message[0, 0:FIELDS, CELLS:] = later_ref[...].astype(F32)[0:FIELDS]

    lane = iota((ROWS, 128), 1)
    for f in range(FR_DEV):
        near_out[f] = message[f, :, 0:CELLS].astype(BF)
    for pair in range(2):
        near_out[FR_DEV, :, pair * 128 : pair * 128 + 128] = jnp.where(
            lane < 64,
            message[2 * pair, :, CELLS:],
            pltpu.roll(message[2 * pair + 1, :, CELLS:], 64, 1),
        ).astype(BF)
    far_out[...] = message[0].astype(BF)


def second_own_states(own_ref, states):
    for p in OWN:
        states[p] = own_ref[p + 1]


def second_own_kernel(
    near_ref, plan_ref, level_ref, own_ref, taps_ref, lift_ref, qkv_ref,
    hidden_out, qkv_out, states, sigmas, *scratch,
):
    own_sigmas(plan_ref, level_ref, sigmas)
    second_own_states(own_ref, states)
    own_frames(
        CELLS, near_ref, (taps_ref, lift_ref, qkv_ref), states, sigmas, (*scratch, None),
        hidden_out, qkv_out,
    )


def second_kernel(
    near_ref, plan_ref, level_ref, own_ref, came_ref, far_ref, hidden_own, qkv_own,
    taps_ref, lift_ref, qkv_ref, attend_ref, decode_ref,
    out_ref, states, sigmas, scaled, images, hidden_all, qkv_all, context_all,
):
    own_sigmas(plan_ref, level_ref, sigmas)
    next_sigmas(came_ref, sigmas)
    second_own_states(own_ref, states)
    for f in range(FR_DEV):
        states[FR_DEV - 1 + f, :, 0:CELLS] = came_ref[f].astype(F32)
        pair = came_ref[FR_DEV, :, (f // 2) * 128 : (f // 2 + 1) * 128].astype(F32)
        states[FR_DEV - 1 + f, :, CELLS:] = pltpu.roll(pair, 64, 1) if f % 2 else pair
    states[2 * FR_DEV - 1] = far_ref[...].astype(F32)
    scale_entering(states, sigmas)

    def finished(p, moved):
        for half in range(2):
            out_ref[pl.ds(p * 2 * FIELDS + half, FIELDS, stride=2), :] = moved[
                0:FIELDS, half * 128 : half * 128 + 128
            ]

    denoise(
        CELLS, near_ref, plan_ref, level_ref,
        (taps_ref, lift_ref, qkv_ref, attend_ref, decode_ref),
        states, sigmas, (scaled, images, None), hidden_own, qkv_own,
        hidden_all, qkv_all, context_all, finished,
    )


def window_scratch(lanes, frames):
    found = [
        pltpu.VMEM((frames, ROWS, CELLS + 128), F32),
        pltpu.VMEM((frames, 1, 128), F32),
        pltpu.VMEM((frames, ROWS, CELLS + 128), F32),
        pltpu.VMEM((frames, ROWS, 4 * CELLS), F32),
    ]
    if lanes > CELLS:
        found.append(pltpu.VMEM((frames, ROWS, 5 * 128), F32))
    return found


def attention_scratch(lanes):
    return [
        pltpu.VMEM((WIDTH, lanes), F32),
        pltpu.VMEM((len(REST), 3 * HEAD, HEADS, lanes), F32),
        pltpu.VMEM((FR_DEV, HEAD, HEADS, lanes), F32),
    ]


def own_call(kernel, lanes, *operands):
    return pl.pallas_call(
        kernel,
        out_shape=(
            pltpu.VMEM((len(OWN), WIDTH, lanes), F32),
            pltpu.VMEM((len(OWN), 3 * HEAD, HEADS, lanes), F32),
        ),
        in_specs=[SMEM] * 3 + [VMEM] * (len(operands) - 3),
        out_specs=(VMEM, VMEM),
        scratch_shapes=window_scratch(lanes, FR_DEV),
        compiler_params=pltpu.CompilerParams(vmem_limit_bytes=40 << 20),
    )(*operands)


def shards(
    queue_state, fresh_noise, plan, levels, neighbours, in_weight, level_embed, conv_weight,
    norm_gain, query_weight, memory_weight, attend_out, decode_weight,
):
    groups = lax.axis_size("noise")
    from_next = [((i + 1) % groups, i) for i in range(groups)]
    from_second = [((i + 2) % groups, i) for i in range(groups)]
    near = far_from_core(neighbours.T)
    plan = far_from_core(plan)
    levels = far_from_core(levels)
    fresh_noise = far_from_core(fresh_noise)
    queue = far_from_core(queue_state.reshape(FR_DEV * FIELDS * 2, 128))
    frames, front, slots, after = border_lines(near, plan, levels, queue, fresh_noise)
    next_frames = near_core(lax.ppermute(frames, "noise", from_next))
    slots = near_core(lax.all_to_all(slots, TILE_AXES, split_axis=0, concat_axis=0, tiled=True))
    far = lax.ppermute(front, "noise", from_second)
    weights = prepare_weights(
        in_weight, level_embed, conv_weight, norm_gain, query_weight, memory_weight,
        attend_out, decode_weight, after,
    )
    far = near_core(far)
    halos, front_halo, later = halo_cells(near, slots, weights[1])
    next_halos = near_core(lax.ppermute(halos, "noise", from_next))
    far_halo = near_core(lax.ppermute(front_halo, "noise", from_second))
    both = (VMEM,) * 2
    lanes = CELLS + 128
    own_part = own_call(first_own_kernel, lanes, near, plan, levels, queue, halos, *weights[:3])
    own, near_message, far_message = pl.pallas_call(
        first_kernel,
        out_shape=(
            jax.ShapeDtypeStruct((FR_DEV, ROWS, lanes), F32),
            jax.ShapeDtypeStruct((FR_DEV + 1, ROWS, CELLS), BF),
            jax.ShapeDtypeStruct((ROWS, lanes), BF),
        ),
        in_specs=[*([SMEM] * 3 + [VMEM] * 8), *both, *([VMEM] * 5)],
        out_specs=(VMEM,) * 3,
        scratch_shapes=[
            *window_scratch(lanes, 2 * FR_DEV),
            *attention_scratch(lanes),
            pltpu.VMEM((FR_DEV, ROWS, lanes), F32),
        ],
        compiler_params=pltpu.CompilerParams(vmem_limit_bytes=40 << 20),
        name="first",
    )(
        near, plan, levels, queue, fresh_noise, halos, later, next_frames, next_halos, far,
        far_halo, *own_part, *weights,
    )
    came = near_core(lax.ppermute(near_message, "noise", from_next))
    far = near_core(lax.ppermute(far_message, "noise", from_second))
    own_part = own_call(second_own_kernel, CELLS, near, plan, levels, own, *weights[:3])
    moved = pl.pallas_call(
        second_kernel,
        out_shape=jax.ShapeDtypeStruct((FR_DEV * FIELDS * 2, 128), F32),
        in_specs=[*([SMEM] * 3 + [VMEM] * 3), *both, *([VMEM] * 5)],
        out_specs=VMEM,
        scratch_shapes=[*window_scratch(CELLS, 2 * FR_DEV), *attention_scratch(CELLS)],
        compiler_params=pltpu.CompilerParams(vmem_limit_bytes=40 << 20),
        name="second",
    )(near, plan, levels, own, came, far, *own_part, *weights)
    return moved.reshape(queue_state.shape)


def solution(mesh):
    split = Mesh(
        mesh.devices.reshape(mesh.shape["noise"], 2, 4, 2), ("noise", "tile_0", "tile_1", "tile_2")
    )
    placed = (
        P("noise", None, TILE_AXES, None),
        P(None, None, TILE_AXES, None),
        P(),
        P("noise"),
        P(),
        P(),
        P(),
        P(),
        P(),
        P(),
        P(),
        P(),
        P(),
    )
    return jax.shard_map(
        shards,
        mesh=split,
        in_specs=placed,
        out_specs=P("noise", None, TILE_AXES, None),
        check_vma=False,
    )
```

```python
import jax
import jax.numpy as jnp
from jax import lax
from jax.experimental import pallas as pl
from jax.experimental.pallas import tpu as pltpu
from jax.sharding import Mesh
from jax.sharding import PartitionSpec as P

FIELDS = 69
ROWS = 72
WIDTH = 256
HEADS = 8
HEAD = WIDTH // HEADS
TILE = 16
CELLS = TILE * TILE
TAPS = 9
SLOT = 80
FR_DEV = 4
NTILES = 16
TILE_AXES = ("tile_0", "tile_1", "tile_2")
BF = jnp.bfloat16
F32 = jnp.float32

VMEM = pl.BlockSpec(memory_space=pltpu.VMEM)
SMEM = pl.BlockSpec(memory_space=pltpu.SMEM)


def near_core(array):
    return pltpu.with_memory_space_constraint(array, pltpu.VMEM)


def far_from_core(array):
    return pltpu.with_memory_space_constraint(array, pltpu.HBM)


def iota(shape, dim):
    return lax.broadcasted_iota(jnp.int32, shape, dim)


def mm(a, b):
    return jnp.dot(a, b, preferred_element_type=F32)


def mm_nt(a, b):
    return lax.dot_general(a, b, (((1,), (1,)), ((), ())), preferred_element_type=F32)


def split_hi_lo(v):
    hi = v.astype(BF).astype(F32)
    return hi, v - hi


def weights_kernel(
    in_ref, embed_ref, conv_ref, gain_ref, query_ref, memory_ref, out_ref, decode_ref, near_ref,
    after_ref, taps_out, lift_out, spread_out, pick_out, qkv_out, attend_out, decode_out, folded,
):
    selections(near_ref[2, lax.axis_index(TILE_AXES)] >= 0, spread_out, pick_out)
    rows = iota((ROWS, WIDTH), 0)
    unit = (iota((ROWS, FIELDS), 0) == iota((ROWS, FIELDS), 1)).astype(BF)
    lift_t = mm(unit, in_ref[...])
    embed = jnp.broadcast_to(embed_ref[...], (ROWS, WIDTH))
    embed_hi, embed_lo = split_hi_lo(embed)
    stacked = jnp.where(
        rows == FIELDS, embed_hi, jnp.where(rows == FIELDS + 1, embed_lo, lift_t)
    ).astype(BF)
    lift_rows = jnp.where(
        rows >= FIELDS, jnp.where(rows == FIELDS + 2, embed_lo, embed_hi), lift_t
    )
    lift_out[...] = jnp.transpose(lift_rows).astype(BF)
    for tap in range(TAPS):
        both = mm_nt(stacked, conv_ref[tap])
        whole = jnp.broadcast_to(
            both[FIELDS : FIELDS + 1] + both[FIELDS + 1 : FIELDS + 2], (ROWS, WIDTH)
        )
        hi, lo = split_hi_lo(whole)
        folded[pl.ds(tap * ROWS, ROWS), :] = jnp.where(
            rows >= FIELDS, jnp.where(rows == FIELDS + 2, lo, hi), both
        )
    taps_out[...] = jnp.transpose(folded[...]).astype(BF)
    place = iota((WIDTH, WIDTH), 0)
    order = ((place % HEADS) * HEAD + place // HEADS == iota((WIDTH, WIDTH), 1)).astype(BF)
    gain = gain_ref[...]
    qkv_out[0:WIDTH, :] = (mm(order, query_ref[...]) * gain).astype(BF)
    for part in range(2):
        qkv_out[pl.ds((part + 1) * WIDTH, WIDTH), :] = (
            mm(order, memory_ref[pl.ds(part * WIDTH, WIDTH), :]) * gain
        ).astype(BF)
    attend_out[...] = mm_nt(out_ref[...], order).astype(BF)
    decode_out[...] = mm(unit, decode_ref[...]).astype(BF)


def prepare_weights(in_weight, embed, conv, gain, query, memory, attend, decode, near, after):
    return pl.pallas_call(
        weights_kernel,
        out_shape=(
            pltpu.VMEM((WIDTH, TAPS * ROWS), BF),
            pltpu.VMEM((WIDTH, ROWS), BF),
            pltpu.VMEM((128, 4 * CELLS), BF),
            pltpu.VMEM((CELLS + 128, 5 * 128), BF),
            pltpu.VMEM((3 * WIDTH, WIDTH), BF),
            pltpu.VMEM((WIDTH, WIDTH), BF),
            pltpu.VMEM((ROWS, WIDTH), BF),
        ),
        in_specs=[VMEM] * 8 + [SMEM] * 2,
        out_specs=(VMEM,) * 7,
        scratch_shapes=[pltpu.VMEM((TAPS * ROWS, WIDTH), F32)],
        compiler_params=pltpu.CompilerParams(vmem_limit_bytes=40 << 20),
        name="weights",
    )(
        *map(
            far_from_core,
            (
                in_weight.T, embed.reshape(1, WIDTH), conv, gain.reshape(1, WIDTH), query, memory,
                attend, decode,
            ),
        ),
        near,
        after,
    )


def frame_rows(queue_ref, frame):
    halves = [
        queue_ref[pl.ds(frame * 2 * FIELDS + half, FIELDS, stride=2), :] for half in range(2)
    ]
    return jnp.concatenate(halves, axis=1)


def sigma_rows(sigma, lanes):
    rows = iota((8, lanes), 0)
    first, rest = split_hi_lo(jnp.broadcast_to(sigma, (8, lanes)))
    second, third = split_hi_lo(rest)
    return jnp.where(rows == 5, first, jnp.where(rows == 6, second, third))


def border_kernel(
    near_ref, plan_ref, level_ref, queue_ref, fresh_ref,
    frames_out, front_out, slots_out, after_out, full, folded, later, lines,
):
    me = lax.axis_index(TILE_AXES)
    after_out[0] = 0
    for f in range(FR_DEV):
        sigma = jnp.full((8, CELLS), plan_ref[level_ref[f]], F32)
        full[pl.ds(f * ROWS + 64, 8), :] = sigma_rows(sigma, CELLS)
        full[pl.ds(f * ROWS, FIELDS), :] = frame_rows(queue_ref, f)
    full[pl.ds(FR_DEV * ROWS + 64, 8), :] = jnp.zeros((8, CELLS), F32)
    full[pl.ds(FR_DEV * ROWS, FIELDS), :] = fresh_ref[1, :, 0, :]

    @pl.when(lax.axis_index("noise") == 0)
    def _():
        full[0:FIELDS, :] = fresh_ref[0, :, 0, :]

    frames = full[...].astype(BF)
    for f in range(FR_DEV):
        frames_out[f] = full[pl.ds(f * ROWS, ROWS), :].astype(BF)
    front_out[...] = full[0:ROWS, :].astype(BF)
    cell = iota((CELLS, 128), 0)
    want = iota((CELLS, 128), 1)
    line = want // (2 * TILE)
    depth = want % (2 * TILE) // TILE
    along = want % TILE
    source = jnp.where(
        line == 0,
        along * TILE + TILE - 1 - depth,
        jnp.where(
            line == 1,
            along * TILE + depth,
            jnp.where(line == 2, (TILE - 1 - depth) * TILE + along, depth * TILE + along),
        ),
    )
    found = mm(frames, (cell == source).astype(BF))
    later[...] = found[FR_DEV * ROWS :]
    lane = iota((ROWS, 128), 1)
    lane9 = iota((9, 128), 1)
    folded[ROWS:SLOT, :] = jnp.zeros((SLOT - ROWS, 128), F32)
    for r in range(4):
        packed = jnp.zeros((ROWS, 128), F32)
        for f in range(FR_DEV):
            one = found[f * ROWS : (f + 1) * ROWS]
            turn = (2 * TILE * (f - r)) % 128
            if turn:
                one = pltpu.roll(one, turn, 1)
            packed = jnp.where(lane // (2 * TILE) == f, one, packed)
        folded[0:ROWS, :] = packed
        packed = jnp.zeros((9, 128), F32)
        for k in range(8):
            one = later[pl.ds(9 * k, 9), :]
            turn = (TILE * k - 2 * TILE * r) % 128
            if turn:
                one = pltpu.roll(one, turn, 1)
            packed = jnp.where(lane9 // TILE == k, one, packed)
        folded[FIELDS : FIELDS + 9, :] = packed
        lines[r] = folded[...].astype(BF)
    for j in range(NTILES):
        north = near_ref[2, j]
        beside = jnp.maximum(north, near_ref[3, j])
        from_west = jnp.logical_or(near_ref[0, j] == me, near_ref[0, beside] == me)
        from_east = jnp.logical_or(near_ref[1, j] == me, near_ref[1, beside] == me)
        vertical = jnp.where(north >= 0, 2, 3)
        code = jnp.where(from_west, 0, jnp.where(from_east, 1, vertical))
        slots_out[j] = lines[code]


def border_lines(near, plan, levels, queue, fresh):
    return pl.pallas_call(
        border_kernel,
        out_shape=(
            jax.ShapeDtypeStruct((FR_DEV, ROWS, CELLS), BF),
            jax.ShapeDtypeStruct((ROWS, CELLS), BF),
            jax.ShapeDtypeStruct((NTILES, SLOT, 128), BF),
            jax.ShapeDtypeStruct((1,), jnp.int32),
        ),
        in_specs=[SMEM, SMEM, SMEM, VMEM, VMEM],
        out_specs=(VMEM, VMEM, VMEM, SMEM),
        scratch_shapes=[
            pltpu.VMEM(((FR_DEV + 1) * ROWS, CELLS), F32),
            pltpu.VMEM((SLOT, 128), F32),
            pltpu.VMEM((ROWS, 128), F32),
            pltpu.VMEM((4, SLOT, 128), BF),
        ],
        compiler_params=pltpu.CompilerParams(vmem_limit_bytes=40 << 20),
        name="border",
    )(near, plan, levels, queue, fresh)


def halo_lane(row, column, near_row, far_row):
    west = jnp.where(column == -1, row, 64 + row)
    east = jnp.where(column == TILE, TILE + row, 80 + row)
    sides = jnp.where(column < 0, west, east)
    near_line = jnp.where(
        column == -1,
        48,
        jnp.where(column == TILE, 49, jnp.where(column < 0, 112, jnp.where(column > TILE, 115, 32 + column))),
    )
    far_line = jnp.where(
        column == -1,
        113,
        jnp.where(column == TILE, 116, jnp.where(column < 0, 114, jnp.where(column > TILE, 117, 96 + column))),
    )
    inside = jnp.logical_and(row >= 0, row < TILE)
    return jnp.where(
        inside,
        sides,
        jnp.where(row == near_row, near_line, jnp.where(row == far_row, far_line, -1)),
    )


def ring_kernel(near_ref, slots_ref, wait_ref, halo_out, front_out, later_out, picked, spare):
    me = lax.axis_index(TILE_AXES)
    north = near_ref[2, me]
    beside = jnp.maximum(north, near_ref[3, me])
    picked[:, 0:128] = slots_ref[near_ref[0, me]].astype(F32)
    picked[:, 128:256] = slots_ref[near_ref[1, me]].astype(F32)
    picked[:, 256:384] = slots_ref[beside].astype(F32)
    picked[:, 384:512] = slots_ref[near_ref[0, beside]].astype(F32)
    picked[:, 512:640] = slots_ref[near_ref[1, beside]].astype(F32)
    low = picked[...].astype(BF)
    is_north = (north >= 0).astype(jnp.int32)
    near_place = is_north * (TILE - 1)
    far_place = is_north * (TILE - 2) + (1 - is_north)

    def source(lane):
        block = lane // TILE
        along = lane % TILE
        side = jnp.where(block < 3, block, block - 4)
        deep = (lane >= 64).astype(jnp.int32)
        corner = jnp.logical_or(block == 3, block == 7)
        east_corner = jnp.where(block == 3, along, (along >= 3).astype(jnp.int32))
        which = jnp.where(block == 3, 0, 1 + along % 3)
        corner_deep = jnp.logical_or(which == 1, which == 3).astype(jnp.int32)
        corner_place = jnp.where(which >= 2, far_place, near_place)
        known = along < jnp.where(block == 3, 2, 6)
        plain = side * 128 + deep * TILE + along
        ends = (3 + east_corner) * 128 + corner_deep * TILE + corner_place
        lost = jnp.logical_and(corner, jnp.logical_not(known))
        later = jnp.where(corner, (3 + east_corner) * 128 + corner_place, side * 128 + along)
        return (
            jnp.where(lost, -10000, jnp.where(corner, ends, plain)),
            jnp.where(lost, -10000, later),
        )

    column = iota((8, FR_DEV * 128), 1)
    spot = source(column % 128)[0] + 2 * TILE * (column // 128)
    pick = (iota((5 * 128, FR_DEV * 128), 0) == spot[0:1]).astype(BF)
    halos = mm(low[0:ROWS], pick)
    for f in range(FR_DEV):
        halo_out[f] = halos[:, f * 128 : (f + 1) * 128].astype(BF)
    front_out[...] = halos[:, 0:128].astype(BF)
    column = iota((8, 8 * 64), 1)
    spot = source(column % 64)[1] + TILE * (column // 64)
    pick = (iota((5 * 128, 8 * 64), 0) == spot[0:1]).astype(BF)
    spare[...] = jnp.zeros_like(spare)
    blocks = mm(picked[64:SLOT].astype(BF), pick)
    for k in range(8):
        one = blocks[5:14, (k // 2) * 128 : (k // 2 + 1) * 128]
        spare[pl.ds(9 * k, 9), :] = pltpu.roll(one, 64, 1) if k % 2 else one
    later_out[...] = spare[...].astype(BF)


def halo_cells(near, slots, wait):
    return pl.pallas_call(
        ring_kernel,
        out_shape=(
            jax.ShapeDtypeStruct((FR_DEV, ROWS, 128), BF),
            jax.ShapeDtypeStruct((ROWS, 128), BF),
            jax.ShapeDtypeStruct((ROWS, 128), BF),
        ),
        in_specs=[SMEM, VMEM, pl.BlockSpec(memory_space=pl.ANY)],
        out_specs=(VMEM,) * 3,
        scratch_shapes=[pltpu.VMEM((SLOT, 5 * 128), F32), pltpu.VMEM((ROWS, 128), F32)],
        compiler_params=pltpu.CompilerParams(vmem_limit_bytes=40 << 20),
        name="ring",
    )(near, slots, wait)


def with_log_rows(scaled, log_hi, log_lo, lanes):
    rows = iota((ROWS, lanes), 0)
    return jnp.where(
        rows >= FIELDS, jnp.where(rows == FIELDS + 1, log_lo, log_hi), scaled
    )


def wide(row, lanes):
    return jnp.concatenate([row] * (lanes // 128), axis=1)


def selections(at_north, spread_out, pick_out):
    ring_row = iota((128, 4 * CELLS), 0)
    column = iota((8, 4 * CELLS), 1)
    shift = column // CELLS - 2
    cell_x = column % TILE
    cell_y = (column % CELLS) // TILE
    line_x = cell_x + shift
    from_line = jnp.where(
        line_x < 0, 3 * TILE, jnp.where(line_x >= TILE, 3 * TILE + 1, 2 * TILE + line_x)
    )
    from_side = jnp.where(cell_x == 0, cell_y, TILE + cell_y)
    spot = jnp.where(column < CELLS, from_side, from_line)
    spread_out[...] = (ring_row == spot[0:1]).astype(BF)
    near_row = jnp.where(at_north, -1, TILE)
    far_row = jnp.where(at_north, -2, TILE + 1)
    column = iota((8, 5 * 128), 1)
    tap = column // 64
    cell = column % 64
    block = cell // TILE
    along = cell % TILE
    row = jnp.where(block < 2, along, near_row) + tap // 3 - 1
    col = jnp.where(
        block == 0,
        -1,
        jnp.where(block == 1, TILE, jnp.where(block == 2, along, jnp.where(along == 0, -1, TILE))),
    )
    col = col + tap % 3 - 1
    in_tile = jnp.logical_and(
        jnp.logical_and(row >= 0, row < TILE), jnp.logical_and(col >= 0, col < TILE)
    )
    halo = halo_lane(row, col, near_row, far_row)
    spot = jnp.where(
        in_tile, row * TILE + col, jnp.where(halo >= 0, CELLS + halo, -1)
    )
    spot = jnp.where(cell < 50, spot, -1)
    pick_out[...] = (iota((CELLS + 128, 5 * 128), 0) == spot[0:1]).astype(BF)


def features_of(
    frames, lanes, near_ref, taps_ref, lift_ref, spread_ref, pick_ref, states, sigmas, scaled,
    images, ring_windows,
):
    me = lax.axis_index(TILE_AXES)
    at_north = near_ref[2, me] >= 0
    north_here = at_north.astype(F32)
    south_here = 1.0 - north_here
    extended = lanes > CELLS
    count = len(frames)
    begin = frames[0]
    total = CELLS + 128

    for p in frames:
        sigma = sigmas[p]
        log_hi, log_lo = split_hi_lo(jnp.log(sigma))
        scale = 1.0 / jnp.sqrt(sigma * sigma + 1.0)
        scaled[p] = with_log_rows(
            states[p] * wide(scale, total), wide(log_hi, total), wide(log_lo, total), total
        )
    low = scaled[begin : begin + count].reshape(count * ROWS, total).astype(BF)
    images[begin : begin + count] = mm(low[:, CELLS:], spread_ref[...]).reshape(count, ROWS, 4 * CELLS)
    if extended:
        ring_windows[begin : begin + count] = mm(low, pick_ref[...]).reshape(count, ROWS, 5 * 128)

    across = iota((ROWS, CELLS), 1) % TILE
    down = iota((ROWS, CELLS), 1) // TILE

    def features(p):
        inner = scaled[p, :, 0:CELLS].astype(BF).astype(F32)
        sides = images[p, :, 0:CELLS]
        shifted = (
            jnp.where(across == 0, sides, pltpu.roll(inner, 1, 1)),
            inner,
            jnp.where(across == TILE - 1, sides, pltpu.roll(inner, CELLS - 1, 1)),
        )
        up = []
        low = []
        for b in range(3):
            line = images[p, :, (b + 1) * CELLS : (b + 2) * CELLS]
            up.append(jnp.where(down == 0, line * north_here, pltpu.roll(shifted[b], TILE, 1)))
            low.append(
                jnp.where(
                    down == TILE - 1, line * south_here, pltpu.roll(shifted[b], CELLS - TILE, 1)
                )
            )
        windows = jnp.concatenate([*up, *shifted, *low], axis=0)
        if extended:
            beyond = []
            for tap in range(TAPS):
                one = ring_windows[p, :, (tap // 2) * 128 : (tap // 2 + 1) * 128]
                beyond.append(pltpu.roll(one, 64, 1) if tap % 2 else one)
            windows = jnp.concatenate([windows, jnp.concatenate(beyond, axis=0)], axis=1)
        convolved = mm(taps_ref[...], windows.astype(BF))
        lifted = mm(lift_ref[...], scaled[p, :, 0:lanes].astype(BF))
        hidden = lifted + convolved / (1.0 + jnp.exp(-convolved))
        power = jnp.mean(hidden * hidden, axis=0, keepdims=True)
        return hidden, (hidden * lax.rsqrt(power + 1e-06)).astype(BF)

    return features


OWN = range(FR_DEV - 1)
REST = range(FR_DEV - 1, 2 * FR_DEV)


def own_frames(lanes, near_ref, weights, states, sigmas, scratch, hidden_out, qkv_out):
    taps_ref, lift_ref, spread_ref, pick_ref, qkv_ref = weights
    features = features_of(
        OWN, lanes, near_ref, taps_ref, lift_ref, spread_ref, pick_ref, states, sigmas, *scratch
    )
    for p in OWN:
        hidden, normed = features(p)
        hidden_out[p] = hidden
        qkv_out[p] = mm(qkv_ref[...], normed).reshape(3 * HEAD, HEADS, lanes)


def denoise(
    lanes, near_ref, plan_ref, level_ref, weights, states, sigmas, scratch,
    hidden_own, qkv_own, hidden_all, qkv_all, context_all, finished,
):
    taps_ref, lift_ref, spread_ref, pick_ref, qkv_ref, attend_ref, decode_ref = weights
    is_last = lax.axis_index("noise") == lax.axis_size("noise") - 1
    held = len(OWN)
    features = features_of(
        REST, lanes, near_ref, taps_ref, lift_ref, spread_ref, pick_ref, states, sigmas, *scratch
    )
    for p in REST:
        hidden, normed = features(p)
        if p < FR_DEV:
            hidden_all[...] = hidden
            qkv_all[p - held] = mm(qkv_ref[...], normed).reshape(3 * HEAD, HEADS, lanes)
        else:
            qkv_all[p - held, HEAD : 3 * HEAD] = mm(qkv_ref[WIDTH : 3 * WIDTH, :], normed).reshape(
                2 * HEAD, HEADS, lanes
            )

    def every(row, at):
        return jnp.concatenate([qkv_own[:, row, :, at], qkv_all[:, row, :, at]], axis=0)

    def query(i, d, at):
        return qkv_own[i, d, :, at] if i < held else qkv_all[i - held, d, :, at]

    hide = jnp.where(is_last, -jnp.inf, 0.0)
    for part in range(lanes // 128):
        at = slice(part * 128, part * 128 + 128)

        zero = jnp.zeros((2 * FR_DEV, HEADS, 128), F32)
        sums = []
        for pair in range(0, FR_DEV, 2):

            def score(d, so_far, pair=pair):
                keys = every(HEAD + d, at)
                return tuple(
                    so_far[i] + query(pair + i, d, at)[None] * keys for i in range(2)
                )

            sums.extend(lax.fori_loop(0, HEAD, score, (zero,) * 2, unroll=HEAD))
        second_half = iota((2 * FR_DEV, HEADS, 128), 0) >= FR_DEV
        weights = []
        for i in range(FR_DEV):
            scores = sums[i] * HEAD ** (-0.5) + jnp.where(second_half, hide, 0.0)
            top = jnp.max(scores, axis=0, keepdims=True)
            raised = jnp.exp(scores - top)
            weights.append(raised * (1.0 / jnp.sum(raised, axis=0, keepdims=True)))

        def combine(d, carry):
            values = every(2 * HEAD + d, at)
            for i in range(FR_DEV):
                context_all[i, d, :, at] = jnp.sum(weights[i] * values, axis=0)
            return carry

        lax.fori_loop(0, HEAD, combine, 0, unroll=HEAD)

    for p in range(FR_DEV):
        context = context_all[p].reshape(WIDTH, lanes).astype(BF)
        hidden = hidden_own[p] if p < held else hidden_all[...]
        refined = (hidden + mm(attend_ref[...], context)).astype(BF)
        projected = mm(decode_ref[...], refined)
        sigma = wide(sigmas[p], lanes)
        sigma_next = jnp.full((1, lanes), plan_ref[level_ref[p] + 1], F32)
        spread_of = sigma * sigma + 1.0
        slope = (sigma_next - sigma) / sigma
        state = states[p, :, 0:lanes]
        denoised = state / spread_of + sigma / jnp.sqrt(spread_of) * projected
        finished(p, state + slope * (state - denoised))


def own_sigmas(plan_ref, level_ref, sigmas):
    for f in range(FR_DEV):
        sigmas[f] = jnp.full((1, 128), plan_ref[level_ref[f]], F32)


def next_sigmas(next_frames_ref, sigmas):
    for f in range(FR_DEV):
        came = next_frames_ref[f, 64:ROWS, 0:128].astype(F32)
        sigmas[FR_DEV + f] = came[5:6] + came[6:7] + came[7:8]


def scale_entering(states, sigmas):
    group = lax.axis_index("noise")
    groups = lax.axis_size("noise")
    for p, holder in ((FR_DEV - 1, groups - 1), (2 * FR_DEV - 1, groups - 2)):

        @pl.when(group == holder)
        def _(p=p):
            states[p] = states[p] * wide(sigmas[p], CELLS + 128)


def first_own_states(queue_ref, halo_ref, states):
    for p in OWN:
        states[p, 64:ROWS, 0:CELLS] = jnp.zeros((ROWS - 64, CELLS), F32)
        states[p, 0:FIELDS, 0:CELLS] = frame_rows(queue_ref, p + 1)
        states[p, :, CELLS:] = halo_ref[p + 1].astype(F32)


def first_own_kernel(
    near_ref, plan_ref, level_ref, queue_ref, halo_ref, taps_ref, lift_ref, spread_ref, pick_ref, qkv_ref,
    hidden_out, qkv_out, states, sigmas, *scratch,
):
    own_sigmas(plan_ref, level_ref, sigmas)
    first_own_states(queue_ref, halo_ref, states)
    own_frames(
        CELLS + 128, near_ref, (taps_ref, lift_ref, spread_ref, pick_ref, qkv_ref), states, sigmas, scratch,
        hidden_out, qkv_out,
    )


def first_kernel(
    near_ref, plan_ref, level_ref, queue_ref, fresh_ref, halo_ref, later_ref, next_frames_ref,
    next_halo_ref, far_ref, far_halo_ref, hidden_own, qkv_own,
    taps_ref, lift_ref, spread_ref, pick_ref, qkv_ref, attend_ref, decode_ref,
    own_out, near_out, far_out,
    states, sigmas, scaled, images, ring_windows, hidden_all, qkv_all, context_all, message,
):
    own_sigmas(plan_ref, level_ref, sigmas)
    next_sigmas(next_frames_ref, sigmas)
    first_own_states(queue_ref, halo_ref, states)
    for f in range(FR_DEV):
        states[FR_DEV - 1 + f, :, 0:CELLS] = next_frames_ref[f].astype(F32)
        states[FR_DEV - 1 + f, :, CELLS:] = next_halo_ref[f].astype(F32)
    states[2 * FR_DEV - 1, :, 0:CELLS] = far_ref[...].astype(F32)
    states[2 * FR_DEV - 1, :, CELLS:] = far_halo_ref[...].astype(F32)
    scale_entering(states, sigmas)

    def finished(p, moved):
        own_out[p] = moved
        message[p, 0:64] = moved[0:64]
        rows = iota((8, CELLS + 128), 0)
        message[p, 64:ROWS] = jnp.where(
            rows >= FIELDS - 64, sigma_rows(wide(sigmas[p], CELLS + 128), CELLS + 128), moved[64:ROWS]
        )

    denoise(
        CELLS + 128, near_ref, plan_ref, level_ref,
        (taps_ref, lift_ref, spread_ref, pick_ref, qkv_ref, attend_ref, decode_ref),
        states, sigmas, (scaled, images, ring_windows), hidden_own, qkv_own,
        hidden_all, qkv_all, context_all, finished,
    )

    @pl.when(lax.axis_index("noise") == 0)
    def _():
        message[0, 0:FIELDS, 0:CELLS] = fresh_ref[1, :, 0, :]
        message[0, 0:FIELDS, CELLS:] = later_ref[...].astype(F32)[0:FIELDS]

    lane = iota((ROWS, 128), 1)
    for f in range(FR_DEV):
        near_out[f] = message[f, :, 0:CELLS].astype(BF)
    for pair in range(2):
        near_out[FR_DEV, :, pair * 128 : pair * 128 + 128] = jnp.where(
            lane < 64,
            message[2 * pair, :, CELLS:],
            pltpu.roll(message[2 * pair + 1, :, CELLS:], 64, 1),
        ).astype(BF)
    far_out[...] = message[0].astype(BF)


def second_own_states(own_ref, states):
    for p in OWN:
        states[p] = own_ref[p + 1]


def second_own_kernel(
    near_ref, plan_ref, level_ref, own_ref, taps_ref, lift_ref, spread_ref, pick_ref, qkv_ref,
    hidden_out, qkv_out, states, sigmas, *scratch,
):
    own_sigmas(plan_ref, level_ref, sigmas)
    second_own_states(own_ref, states)
    own_frames(
        CELLS, near_ref, (taps_ref, lift_ref, spread_ref, pick_ref, qkv_ref), states, sigmas, (*scratch, None),
        hidden_out, qkv_out,
    )


def second_kernel(
    near_ref, plan_ref, level_ref, own_ref, came_ref, far_ref, hidden_own, qkv_own,
    taps_ref, lift_ref, spread_ref, pick_ref, qkv_ref, attend_ref, decode_ref,
    out_ref, states, sigmas, scaled, images, hidden_all, qkv_all, context_all,
):
    own_sigmas(plan_ref, level_ref, sigmas)
    next_sigmas(came_ref, sigmas)
    second_own_states(own_ref, states)
    for f in range(FR_DEV):
        states[FR_DEV - 1 + f, :, 0:CELLS] = came_ref[f].astype(F32)
        pair = came_ref[FR_DEV, :, (f // 2) * 128 : (f // 2 + 1) * 128].astype(F32)
        states[FR_DEV - 1 + f, :, CELLS:] = pltpu.roll(pair, 64, 1) if f % 2 else pair
    states[2 * FR_DEV - 1] = far_ref[...].astype(F32)
    scale_entering(states, sigmas)

    def finished(p, moved):
        for half in range(2):
            out_ref[pl.ds(p * 2 * FIELDS + half, FIELDS, stride=2), :] = moved[
                0:FIELDS, half * 128 : half * 128 + 128
            ]

    denoise(
        CELLS, near_ref, plan_ref, level_ref,
        (taps_ref, lift_ref, spread_ref, pick_ref, qkv_ref, attend_ref, decode_ref),
        states, sigmas, (scaled, images, None), hidden_own, qkv_own,
        hidden_all, qkv_all, context_all, finished,
    )


def window_scratch(lanes, frames):
    found = [
        pltpu.VMEM((frames, ROWS, CELLS + 128), F32),
        pltpu.VMEM((frames, 1, 128), F32),
        pltpu.VMEM((frames, ROWS, CELLS + 128), F32),
        pltpu.VMEM((frames, ROWS, 4 * CELLS), F32),
    ]
    if lanes > CELLS:
        found.append(pltpu.VMEM((frames, ROWS, 5 * 128), F32))
    return found


def attention_scratch(lanes):
    return [
        pltpu.VMEM((WIDTH, lanes), F32),
        pltpu.VMEM((len(REST), 3 * HEAD, HEADS, lanes), F32),
        pltpu.VMEM((FR_DEV, HEAD, HEADS, lanes), F32),
    ]


def own_call(kernel, lanes, *operands):
    return pl.pallas_call(
        kernel,
        out_shape=(
            pltpu.VMEM((len(OWN), WIDTH, lanes), F32),
            pltpu.VMEM((len(OWN), 3 * HEAD, HEADS, lanes), F32),
        ),
        in_specs=[SMEM] * 3 + [VMEM] * (len(operands) - 3),
        out_specs=(VMEM, VMEM),
        scratch_shapes=window_scratch(lanes, FR_DEV),
        compiler_params=pltpu.CompilerParams(vmem_limit_bytes=40 << 20),
    )(*operands)


def shards(
    queue_state, fresh_noise, plan, levels, neighbours, in_weight, level_embed, conv_weight,
    norm_gain, query_weight, memory_weight, attend_out, decode_weight,
):
    groups = lax.axis_size("noise")
    from_next = [((i + 1) % groups, i) for i in range(groups)]
    from_second = [((i + 2) % groups, i) for i in range(groups)]
    near = far_from_core(neighbours.T)
    plan = far_from_core(plan)
    levels = far_from_core(levels)
    fresh_noise = far_from_core(fresh_noise)
    queue = far_from_core(queue_state.reshape(FR_DEV * FIELDS * 2, 128))
    frames, front, slots, after = border_lines(near, plan, levels, queue, fresh_noise)
    next_frames = near_core(lax.ppermute(frames, "noise", from_next))
    slots = near_core(lax.all_to_all(slots, TILE_AXES, split_axis=0, concat_axis=0, tiled=True))
    far = lax.ppermute(front, "noise", from_second)
    weights = prepare_weights(
        in_weight, level_embed, conv_weight, norm_gain, query_weight, memory_weight,
        attend_out, decode_weight, near, after,
    )
    far = near_core(far)
    halos, front_halo, later = halo_cells(near, slots, weights[1])
    next_halos = near_core(lax.ppermute(halos, "noise", from_next))
    far_halo = near_core(lax.ppermute(front_halo, "noise", from_second))
    both = (VMEM,) * 2
    lanes = CELLS + 128
    own_part = own_call(first_own_kernel, lanes, near, plan, levels, queue, halos, *weights[:5])
    own, near_message, far_message = pl.pallas_call(
        first_kernel,
        out_shape=(
            jax.ShapeDtypeStruct((FR_DEV, ROWS, lanes), F32),
            jax.ShapeDtypeStruct((FR_DEV + 1, ROWS, CELLS), BF),
            jax.ShapeDtypeStruct((ROWS, lanes), BF),
        ),
        in_specs=[*([SMEM] * 3 + [VMEM] * 8), *both, *([VMEM] * 7)],
        out_specs=(VMEM,) * 3,
        scratch_shapes=[
            *window_scratch(lanes, 2 * FR_DEV),
            *attention_scratch(lanes),
            pltpu.VMEM((FR_DEV, ROWS, lanes), F32),
        ],
        compiler_params=pltpu.CompilerParams(vmem_limit_bytes=40 << 20),
        name="first",
    )(
        near, plan, levels, queue, fresh_noise, halos, later, next_frames, next_halos, far,
        far_halo, *own_part, *weights,
    )
    came = near_core(lax.ppermute(near_message, "noise", from_next))
    far = near_core(lax.ppermute(far_message, "noise", from_second))
    own_part = own_call(second_own_kernel, CELLS, near, plan, levels, own, *weights[:5])
    moved = pl.pallas_call(
        second_kernel,
        out_shape=jax.ShapeDtypeStruct((FR_DEV * FIELDS * 2, 128), F32),
        in_specs=[*([SMEM] * 3 + [VMEM] * 3), *both, *([VMEM] * 7)],
        out_specs=VMEM,
        scratch_shapes=[*window_scratch(CELLS, 2 * FR_DEV), *attention_scratch(CELLS)],
        compiler_params=pltpu.CompilerParams(vmem_limit_bytes=40 << 20),
        name="second",
    )(near, plan, levels, own, came, far, *own_part, *weights)
    return moved.reshape(queue_state.shape)


def solution(mesh):
    split = Mesh(
        mesh.devices.reshape(mesh.shape["noise"], 2, 4, 2), ("noise", "tile_0", "tile_1", "tile_2")
    )
    placed = (
        P("noise", None, TILE_AXES, None),
        P(None, None, TILE_AXES, None),
        P(),
        P("noise"),
        P(),
        P(),
        P(),
        P(),
        P(),
        P(),
        P(),
        P(),
        P(),
    )
    return jax.shard_map(
        shards,
        mesh=split,
        in_specs=placed,
        out_specs=P("noise", None, TILE_AXES, None),
        check_vma=False,
    )
```
